128 devices in a mesh: gx: 16 (over y, z_lo, core), gy: 8 (over x, z_hi).
Axes of the slice: x: 4, y: 4, z: 4 (z_hi: 2, z_lo: 2; z = z_hi * 2 + z_lo), core: 2. Of those that a mesh axis runs over, the one named last changes fastest.
Arguments:
- density: float32 [512, 512, 128], P('gx', 'gy'), may hold values from 0 to 1
- transfer_table: int32 [4, 128], replicated, may hold values from 0 to 255
- shear_x: int32 [2, 512], P(None, 'gx'), may hold values from -16 to 15, as said below
- shear_y: int32 [2, 512], P(None, 'gy'), may hold values from -16 to 15, as said below
- direction: int32 [2, 2], replicated, may hold values from 0 to 1
Outputs:
- image_x: float32 [2, 4, 512, 128], P(None, None, ('gy', 'gx'))
- image_y: float32 [2, 4, 512, 128], P(None, None, ('gx', 'gy'))
The draws below stay inside these ranges and needn't reach their ends.
Inputs may be any that keep to these rules, and one draw needn't show every extreme that they name: `shear_x`: the shift along z of a slice in a view. `shear_y`: the shift along z of a slice in a view.
All inputs are finite; a program needn't handle non-finite values.
Results may differ from the reference program's by a relative error of at most 0.0003.
Values sent between devices are 32-bit elements; how exact they have to be, the bound alone decides.
No kernel may reach another device: no remote copies, remote signals or barrier semaphores. Data moves between devices by JAX's collectives and lax.ppermute only.
A program may use at most 192 MiB of HBM per device.

```python
import jax
import jax.numpy as jnp
from jax import lax

NZ = 128
KNOTS = 128
SHEAR = 16
VIEWS = 2
NX = 512
NY = 512


def shear_table(key, length):
    slopes = jax.random.randint(jax.random.fold_in(key, 1), (VIEWS,), -SHEAR, SHEAR + 1)
    starts = jax.random.randint(jax.random.fold_in(key, 2), (VIEWS,), -SHEAR, SHEAR)
    jitter = jax.random.randint(jax.random.fold_in(key, 3), (VIEWS, length), -1, 2)
    positions = jnp.arange(length, dtype=jnp.int32)
    table = starts[:, None] + positions[None, :] * slopes[:, None] // length + jitter
    table = jnp.clip(table, -SHEAR, SHEAR - 1).astype(jnp.int32)
    chosen = jax.random.permutation(jax.random.fold_in(key, 5), VIEWS)
    spots = jax.random.randint(jax.random.fold_in(key, 7), (2,), 0, length)
    table = table.at[chosen[0], spots[0]].set(SHEAR - 1)
    table = table.at[chosen[1], spots[1]].set(-SHEAR)
    return table.astype(jnp.int32)


def draw_shear_x(key, part):
    return shear_table(jax.random.fold_in(key, 17), NX)


def draw_shear_y(key, part):
    return shear_table(jax.random.fold_in(key, 29), NY)


def plant(array, key, smallest, high):
    longest = array.shape.index(max(array.shape))
    spots = []
    for shift in (0, 1):
        where = [jax.random.randint(jax.random.fold_in(key, axis), (), 0, length) for axis, length in enumerate(array.shape)]
        where[longest] = (where[longest] + shift) % array.shape[longest]
        spots.append(tuple(where))
    return array.at[spots[0]].set(smallest).at[spots[1]].set(high)


def block_scale(key, dims, pieces, least, top_value):
    def one(axis_at, shards_of):
        heights = jax.random.uniform(jax.random.fold_in(jax.random.fold_in(key, 6), axis_at), (shards_of,), jnp.float32, least / len(pieces), top_value / len(pieces))
        return jnp.repeat(jnp.exp(heights), dims[axis_at] // shards_of).reshape((-1,) + (1,) * (len(dims) - axis_at - 1))

    gain = one(*pieces[0])
    for cut in pieces[1:]:
        gain = gain * one(*cut)
    return gain


def setup_inputs(seed: int = 0) -> dict:
    arg_keys = jax.random.split(jax.random.key(seed), 6)
    density = jnp.clip(1.0 * jax.random.uniform(arg_keys[0], (NX, NY, NZ), jnp.float32) ** block_scale(arg_keys[0], (NX, NY, NZ), ((0, 16), (1, 8)), -0.2, 0.2), 0.0, 1.0)
    transfer_table = plant(jax.random.randint(arg_keys[1], (4, KNOTS), 0, 256), jax.random.fold_in(arg_keys[1], 1), 0, 255).astype(jnp.int32)
    shear_x = draw_shear_x(jax.random.fold_in(arg_keys[5], 71), 0)
    shear_y = draw_shear_y(jax.random.fold_in(arg_keys[5], 71), 0)
    direction = plant(jax.random.randint(arg_keys[4], (2, VIEWS), 0, 2), jax.random.fold_in(arg_keys[4], 1), 0, 1).astype(jnp.int32)
    return dict(density=density, transfer_table=transfer_table, shear_x=shear_x, shear_y=shear_y, direction=direction)


light_x = 1.0 / 3.0
light_y = 2.0 / 3.0
light_z = 2.0 / 3.0
highest = lax.Precision.HIGHEST

def shading(padded):
    framed = jnp.pad(padded, ((0, 0), (0, 0), (1, 1)))
    grad_x = (framed[2:, 1:-1, 1:-1] - framed[:-2, 1:-1, 1:-1]) * 0.5
    grad_y = (framed[1:-1, 2:, 1:-1] - framed[1:-1, :-2, 1:-1]) * 0.5
    grad_z = (framed[1:-1, 1:-1, 2:] - framed[1:-1, 1:-1, :-2]) * 0.5
    facing = jnp.abs(light_x * grad_x + light_y * grad_y + light_z * grad_z)
    return 0.3 + 0.7 * facing / jnp.sqrt(grad_x * grad_x + grad_y * grad_y + grad_z * grad_z + 0.01)

def lookup(values, transfer_table):
    knot_count = transfer_table.shape[1]
    levels = transfer_table.astype(jnp.float32) / 255.0
    places = jnp.arange(knot_count, dtype=jnp.float32)
    scaled = values * (knot_count - 1.0)
    weights = jnp.maximum(0.0, 1.0 - jnp.abs(places[:, None] - scaled[None, :]))
    return jnp.dot(levels, weights, precision=highest, preferred_element_type=jnp.float32)

def classify(density, transfer_table):

    def one_slice(plane_cells):
        return lookup(plane_cells.reshape(-1), transfer_table).reshape((4,) + plane_cells.shape)
    return lax.map(one_slice, density)

def emission(classed, shaded, step_len):
    optical = step_len * 2.0 * classed[:, 3]
    opacity = 1.0 - jnp.exp(-optical)
    colour = classed[:, :3] * (shaded * opacity)[:, None]
    return jnp.concatenate([colour, optical[:, None]], axis=1)

def shift_slice(slab, offset):
    framed = jnp.pad(slab, ((0, 0), (0, 0), (SHEAR, SHEAR)))
    return lax.dynamic_slice_in_dim(framed, (SHEAR - offset).astype(jnp.int32), slab.shape[2], 2)

def render(fields, offsets, turn_flags):

    def one_view(inputs):
        offset_row, turn_flag = inputs
        sheared = jax.vmap(shift_slice)(fields, offset_row)
        depths = sheared[:, 3]
        running = jnp.cumsum(depths, axis=0)
        summed = running[-1]
        before = jnp.where(turn_flag == 0, running - depths, summed[None] - running)
        colour = lax.optimization_barrier(jnp.sum(jnp.exp(-before)[:, None] * sheared[:, :3], axis=0))
        return jnp.concatenate([colour, (1.0 - jnp.exp(-summed))[None]], axis=0)
    return lax.map(one_view, (offsets, turn_flags))

def reference(density, transfer_table, shear_x, shear_y, direction):
    padded = jnp.pad(density, ((1, 1), (1, 1), (0, 0)))
    shaded = shading(padded)
    classed = classify(density, transfer_table)
    along_x = emission(classed, shaded, 1.0 / NX)
    image_x = render(along_x, shear_x, direction[0])
    along_y = emission(classed, shaded, 1.0 / NY).transpose(2, 1, 0, 3)
    image_y = render(along_y, shear_y, direction[1])
    return (image_x, image_y)
```

```python
import functools

import jax
import jax.numpy as jnp
from jax import lax
from jax.experimental import pallas as pl
from jax.experimental.pallas import tpu as pltpu
from jax.sharding import PartitionSpec as P

LANES = 128
ROWS = 8
LOG2E = 1.4426950408889634
light_x = 1.0 / 3.0
light_y = 2.0 / 3.0
light_z = 2.0 / 3.0


def lane_take(table, index):
    return jnp.take_along_axis(table, index, axis=1, mode="promise_in_bounds")


def brick_kernel(step_len, turn_ref, shear_x_ref, shear_y_ref, table_ref, density_ref, low_x_ref,
                 high_x_ref, low_y_ref, high_y_ref, out_x_ref, out_y_ref, cells_ref, field_ref,
                 lut_ref):
    count_x, count_y, cells_z = density_ref.shape
    pad = ROWS

    levels = table_ref[...].astype(jnp.float32) / 255.0
    lane = lax.broadcasted_iota(jnp.int32, (ROWS, cells_z), 1)
    for c in range(4):
        row = jnp.broadcast_to(levels[c:c + 1], (ROWS, cells_z))
        after = pltpu.roll(row, cells_z - 1, 1)
        lut_ref[2 * c] = row
        lut_ref[2 * c + 1] = jnp.where(lane == cells_z - 1, 0.0, after - row)

    cells_ref[0, pl.ds(pad, count_y), :] = low_x_ref[...]
    cells_ref[count_x + 1, pl.ds(pad, count_y), :] = high_x_ref[...]

    def place(i, carry):
        cells_ref[i + 1, pl.ds(pad, count_y), :] = density_ref[i]
        cells_ref[i + 1, pl.ds(pad - 1, 1), :] = low_y_ref[pl.ds(i, 1), :]
        cells_ref[i + 1, pl.ds(pad + count_y, 1), :] = high_y_ref[pl.ds(i, 1), :]
        return carry

    lax.fori_loop(0, count_x, place, 0, unroll=4)

    def shade_classify(i, base):
        here = cells_ref[i + 1, pl.ds(base + pad, ROWS), :]
        diff_x = (cells_ref[i + 2, pl.ds(base + pad, ROWS), :]
                  - cells_ref[i, pl.ds(base + pad, ROWS), :]) * 0.5
        diff_y = (cells_ref[i + 1, pl.ds(base + pad + 1, ROWS), :]
                  - cells_ref[i + 1, pl.ds(base + pad - 1, ROWS), :]) * 0.5
        above = jnp.where(lane == cells_z - 1, 0.0, pltpu.roll(here, cells_z - 1, 1))
        below = jnp.where(lane == 0, 0.0, pltpu.roll(here, 1, 1))
        diff_z = (above - below) * 0.5
        facing = jnp.abs(light_x * diff_x + light_y * diff_y + light_z * diff_z)
        norm = diff_x * diff_x + diff_y * diff_y + diff_z * diff_z + 0.01
        shaded = 0.3 + 0.7 * facing * lax.rsqrt(norm)
        scaled = here * (cells_z - 1.0)
        knot = scaled.astype(jnp.int32)
        frac = scaled - knot.astype(jnp.float32)
        classed = [lane_take(lut_ref[2 * c], knot) + frac * lane_take(lut_ref[2 * c + 1], knot)
                   for c in range(4)]
        optical = (2.0 * step_len) * classed[3]
        weight = shaded * (1.0 - jnp.exp(-optical))
        return [classed[0] * weight, classed[1] * weight, classed[2] * weight, optical]

    def march(fields, shift, flag, scale, state):
        total, red, green, blue = state
        kept = ((lane - shift) & -cells_z) == 0
        amount = shift & (cells_z - 1)
        moved = [pltpu.roll(f, amount, 1) for f in fields]
        depth = jnp.where(kept, moved[3], 0.0)
        seen = jnp.where(kept, jnp.exp2((total + flag * depth) * scale), 0.0)
        return (total + depth, red + seen * moved[0], green + seen * moved[1],
                blue + seen * moved[2])

    flags, scales = [], []
    for family in range(2):
        turned = [turn_ref[family, v] != 0 for v in range(2)]
        flags.append([jnp.where(t, 1.0, 0.0).astype(jnp.float32) for t in turned])
        scales.append([jnp.where(t, LOG2E, -LOG2E).astype(jnp.float32) for t in turned])

    zeros = jnp.zeros((ROWS, cells_z), jnp.float32)

    def settle(family, v, state):
        fade = jnp.exp2(state[0] * (flags[family][v] * -LOG2E))
        return [state[1] * fade, state[2] * fade, state[3] * fade, state[0]]

    def emit_out(out_ref, block, family, v, state):
        for c, value in enumerate(settle(family, v, state)):
            for half in range(2):
                out_ref[2 * block + half, c, pl.ds(4 * v, 4), :] = value[4 * half:4 * half + 4]

    def x_block(block, carry):
        base = pl.multiple_of(block * ROWS, ROWS)

        def body(i, states):
            fields = shade_classify(i, base)
            for c in range(4):
                field_ref[c, pl.ds(i * count_y + base, ROWS), :] = fields[c]
            return tuple(march(fields, shear_x_ref[v, i], flags[0][v], scales[0][v], states[v])
                         for v in range(2))

        states = lax.fori_loop(0, count_x, body, ((zeros,) * 4,) * 2, unroll=4)
        for v in range(2):
            emit_out(out_x_ref, block, 0, v, states[v])
        return carry

    lax.fori_loop(0, count_y // ROWS, x_block, 0)

    def y_block(block, carry):
        def body(j, states):
            fields = [field_ref[c, pl.ds(block * ROWS * count_y + j, ROWS, stride=count_y), :]
                      for c in range(4)]
            return tuple(march(fields, shear_y_ref[v, j], flags[1][v], scales[1][v], states[v])
                         for v in range(2))

        states = lax.fori_loop(0, count_y, body, ((zeros,) * 4,) * 2, unroll=4)
        for v in range(2):
            emit_out(out_y_ref, block, 1, v, states[v])
        return carry

    lax.fori_loop(0, count_x // ROWS, y_block, 0)


def bricks(density, low_x, high_x, low_y, high_y, transfer_table, shear_x, shear_y, direction,
           step_len):
    count_x, count_y, cells_z = density.shape
    smem = pl.BlockSpec(memory_space=pltpu.SMEM)
    vmem = pl.BlockSpec(memory_space=pltpu.VMEM)
    return pl.pallas_call(
        functools.partial(brick_kernel, step_len),
        out_shape=(jax.ShapeDtypeStruct((count_y // 4, 4, 8, cells_z), jnp.float32),
                   jax.ShapeDtypeStruct((count_x // 4, 4, 8, cells_z), jnp.float32)),
        in_specs=[smem] * 3 + [vmem] * 6,
        out_specs=(vmem, vmem),
        scratch_shapes=[
            pltpu.VMEM((count_x + 2, count_y + 2 * ROWS, cells_z), jnp.float32),
            pltpu.VMEM((4, count_x * count_y, cells_z), jnp.float32),
            pltpu.VMEM((8, ROWS, cells_z), jnp.float32),
        ],
        name="brick",
    )(direction, shear_x, shear_y, transfer_table, density, low_x, high_x, low_y, high_y)


def join_kernel(turn_ref, part_x_ref, part_y_ref, out_x_ref, out_y_ref):
    row = lax.broadcasted_iota(jnp.int32, (8, LANES), 0)
    for family, (part_ref, out_ref) in enumerate(((part_x_ref, out_x_ref), (part_y_ref, out_y_ref))):
        count = part_ref.shape[0]
        turned = jnp.where(row < 4, turn_ref[family, 0], turn_ref[family, 1]) != 0
        total = part_ref[0, 3]
        for i in range(1, count):
            total = total + part_ref[i, 3]
        passed = jnp.zeros_like(total)
        colour = [jnp.zeros_like(total) for _ in range(3)]
        for i in range(count):
            depth = part_ref[i, 3]
            before = jnp.where(turned, total - (passed + depth), passed)
            passed = passed + depth
            seen = jnp.exp(-before)
            colour = [colour[c] + seen * part_ref[i, c] for c in range(3)]
        for c, value in enumerate(colour + [1.0 - jnp.exp(-total)]):
            for v in range(2):
                out_ref[v, c] = value[4 * v:4 * v + 4]


def join(part_x, part_y, direction):
    cells_z = part_x.shape[-1]
    vmem = pl.BlockSpec(memory_space=pltpu.VMEM)
    shape = jax.ShapeDtypeStruct((2, 4, 4, cells_z), jnp.float32)
    return pl.pallas_call(
        join_kernel,
        out_shape=(shape, shape),
        in_specs=[pl.BlockSpec(memory_space=pltpu.SMEM), vmem, vmem],
        out_specs=(vmem, vmem),
        name="join",
    )(direction, part_x, part_y)


def faces(block, axis, dim):
    count = lax.axis_size(axis)
    forward = [(i, i + 1) for i in range(count - 1)]
    backward = [(target, source) for source, target in forward]
    last = lax.index_in_dim(block, block.shape[dim] - 1, dim, keepdims=False)
    first = lax.index_in_dim(block, 0, dim, keepdims=False)
    return lax.ppermute(last, axis, forward), lax.ppermute(first, axis, backward)


def local(density, transfer_table, shear_x, shear_y, direction):
    low_x, high_x = faces(density, "gx", 0)
    low_y, high_y = faces(density, "gy", 1)
    step_len = 1.0 / (density.shape[0] * lax.axis_size("gx"))
    part_x, part_y = bricks(density, low_x, high_x, low_y, high_y, transfer_table, shear_x,
                            shear_y, direction, step_len)
    part_x = lax.all_to_all(part_x, "gx", split_axis=0, concat_axis=0, tiled=True)
    part_y = lax.all_to_all(part_y, "gy", split_axis=0, concat_axis=0, tiled=True)
    return join(part_x, part_y, direction)


def solution(mesh):
    placed = (P("gx", "gy", None), P(), P(None, "gx"), P(None, "gy"), P())
    return jax.shard_map(
        local,
        mesh=mesh,
        in_specs=placed,
        out_specs=(P(None, None, ("gy", "gx"), None), P(None, None, ("gx", "gy"), None)),
        check_vma=False,
    )
```

```python
import functools

import jax
import jax.numpy as jnp
from jax import lax
from jax.experimental import pallas as pl
from jax.experimental.pallas import tpu as pltpu
from jax.sharding import PartitionSpec as P

LANES = 128
SHEAR = 16
ROWS = 8
LOG2E = 1.4426950408889634


def lane_take(values, index):
    numbers = lax.GatherDimensionNumbers(
        offset_dims=(), collapsed_slice_dims=(1,), start_index_map=(1,),
        operand_batching_dims=(0,), start_indices_batching_dims=(0,))
    return lax.gather(values, index[..., None], numbers, slice_sizes=(1, 1),
                      mode=lax.GatherScatterMode.PROMISE_IN_BOUNDS)


def classify_kernel(step_len, table_ref, density_ref, field_ref, lut_ref):
    count_x, count_y, cells_z = density_ref.shape
    pitch = field_ref.shape[1] // count_x

    levels = table_ref[...].astype(jnp.float32) / 255.0
    lane = lax.broadcasted_iota(jnp.int32, (ROWS, cells_z), 1)
    for c in range(4):
        scale = 2.0 * step_len * LOG2E if c == 3 else 1.0
        row = jnp.broadcast_to(levels[c:c + 1] * scale, (ROWS, cells_z))
        after = pltpu.roll(row, cells_z - 1, 1)
        lut_ref[2 * c] = row
        lut_ref[2 * c + 1] = jnp.where(lane == cells_z - 1, 0.0, after - row)

    def body(i, carry):
        for base in range(0, count_y, ROWS):
            scaled = density_ref[i, pl.ds(base, ROWS), :] * (cells_z - 1.0)
            knot = scaled.astype(jnp.int32)
            frac = scaled - knot.astype(jnp.float32)
            classed = [lane_take(lut_ref[2 * c], knot) + frac * lane_take(lut_ref[2 * c + 1], knot)
                       for c in range(4)]
            opacity = 1.0 - jnp.exp2(-classed[3])
            values = [classed[c] * opacity for c in range(3)] + [classed[3]]
            for c in range(4):
                field_ref[c, pl.ds(i * pitch + base, ROWS), :] = values[c]
        return carry

    lax.fori_loop(0, count_x, body, 0, unroll=UNROLL_C)


def shift_tables(index_ref, mask_ref):
    cells_z = index_ref.shape[-1]
    lane = lax.broadcasted_iota(jnp.int32, (ROWS, cells_z), 1)

    def body(s, carry):
        source = lane - (s - SHEAR)
        kept = (source & -cells_z) == 0
        index_ref[s] = source & (cells_z - 1)
        mask_ref[s] = jnp.where(kept, -1.0, 0.0)
        mask_ref[s + 2 * SHEAR] = jnp.where(kept, 1.0, 0.0)
        return carry

    lax.fori_loop(0, 2 * SHEAR, body, 0, unroll=4)


def march(fields, shift, turned, index_ref, mask_ref, states):
    place = shift + SHEAR
    index = index_ref[place]
    mask = mask_ref[place + jnp.where(turned, 2 * SHEAR, 0)]
    out = []
    for (red, green, blue, optical), state in zip(fields, states):
        depth = lane_take(optical, index) * mask
        after = state[0] + depth
        seen = jnp.exp2(jnp.where(turned, after, state[0])) * mask
        out.append((after, state[1] + seen * lane_take(red, index),
                    state[2] + seen * lane_take(green, index),
                    state[3] + seen * lane_take(blue, index)))
    return tuple(out)


def emit_out(out_ref, block, v, turned, state):
    sign = jnp.where(turned, 1.0, -1.0)
    total = state[0] * sign
    fade = jnp.exp2(jnp.where(turned, -total, 0.0)) * sign
    for c, value in enumerate([state[1] * fade, state[2] * fade, state[3] * fade, total]):
        for half in range(2):
            out_ref[2 * block + half, c, pl.ds(4 * v, 4), :] = value[4 * half:4 * half + 4]


def x_kernel(group, turn_ref, shear_x_ref, density_ref, low_x_ref, high_x_ref, low_y_ref,
             high_y_ref, field_ref, out_ref, emit_ref, cells_ref, index_ref, mask_ref):
    count_x, count_y, cells_z = density_ref.shape
    pitch = field_ref.shape[1] // count_x
    pad = ROWS
    lane = lax.broadcasted_iota(jnp.int32, (ROWS, cells_z), 1)
    shift_tables(index_ref, mask_ref)

    cells_ref[0, pl.ds(pad, count_y), :] = low_x_ref[...]
    cells_ref[count_x + 1, pl.ds(pad, count_y), :] = high_x_ref[...]

    def place(i, carry):
        cells_ref[i + 1, pl.ds(pad, count_y), :] = density_ref[i]
        cells_ref[i + 1, pl.ds(pad - 1, 1), :] = low_y_ref[pl.ds(i, 1), :]
        cells_ref[i + 1, pl.ds(pad + count_y, 1), :] = high_y_ref[pl.ds(i, 1), :]
        return carry

    lax.fori_loop(0, count_x, place, 0, unroll=4)
    turned = [turn_ref[0, v] != 0 for v in range(2)]
    zeros = jnp.zeros((ROWS, cells_z), jnp.float32)

    def shade(i, base):
        here = cells_ref[i + 1, pl.ds(base + pad, ROWS), :]
        diff_x = (cells_ref[i + 2, pl.ds(base + pad, ROWS), :]
                  - cells_ref[i, pl.ds(base + pad, ROWS), :])
        diff_y = (cells_ref[i + 1, pl.ds(base + pad + 1, ROWS), :]
                  - cells_ref[i + 1, pl.ds(base + pad - 1, ROWS), :])
        above = jnp.where(lane == cells_z - 1, 0.0, pltpu.roll(here, cells_z - 1, 1))
        below = jnp.where(lane == 0, 0.0, pltpu.roll(here, 1, 1))
        diff_z = above - below
        side = diff_y + diff_z
        facing = jnp.abs(diff_x + (side + side))
        norm = diff_x * diff_x + diff_y * diff_y + diff_z * diff_z + 0.04
        return 0.3 + (0.7 / 3.0) * facing * lax.rsqrt(norm)

    def block_of(block, carry):
        base = pl.multiple_of(block * (ROWS * group), ROWS)

        def body(i, states):
            fields = []
            for g in range(group):
                shaded = shade(i, base + g * ROWS)
                row = i * pitch + base + g * ROWS
                colours = [field_ref[c, pl.ds(row, ROWS), :] * shaded for c in range(3)]
                for c in range(3):
                    emit_ref[c, pl.ds(row, ROWS), :] = colours[c]
                fields.append((*colours, field_ref[3, pl.ds(row, ROWS), :]))
            return tuple(march(fields, shear_x_ref[v, i], turned[v], index_ref, mask_ref,
                               states[v]) for v in range(2))

        states = lax.fori_loop(0, count_x, body, (((zeros,) * 4,) * group,) * 2,
                               unroll=UNROLL_X)
        for v in range(2):
            for g in range(group):
                emit_out(out_ref, block * group + g, v, turned[v], states[v][g])
        return carry

    lax.fori_loop(0, count_y // (ROWS * group), block_of, 0)


def y_kernel(group, count_x, turn_ref, shear_y_ref, emit_ref, field_ref, out_ref, index_ref,
             mask_ref):
    cells_z = emit_ref.shape[-1]
    pitch = field_ref.shape[1] // count_x
    count_y = shear_y_ref.shape[1]
    shift_tables(index_ref, mask_ref)
    turned = [turn_ref[1, v] != 0 for v in range(2)]
    zeros = jnp.zeros((ROWS, cells_z), jnp.float32)

    def block_of(block, carry):
        def body(j, states):
            fields = []
            for g in range(group):
                rows = pl.ds((block * group + g) * ROWS * pitch + j, ROWS, stride=pitch)
                fields.append((emit_ref[0, rows, :], emit_ref[1, rows, :], emit_ref[2, rows, :],
                               field_ref[3, rows, :]))
            return tuple(march(fields, shear_y_ref[v, j], turned[v], index_ref, mask_ref,
                               states[v]) for v in range(2))

        states = lax.fori_loop(0, count_y, body, (((zeros,) * 4,) * group,) * 2,
                               unroll=UNROLL_Y)
        for v in range(2):
            for g in range(group):
                emit_out(out_ref, block * group + g, v, turned[v], states[v][g])
        return carry

    lax.fori_loop(0, count_x // (ROWS * group), block_of, 0)


SMEM = pl.BlockSpec(memory_space=pltpu.SMEM)
VMEM = pl.BlockSpec(memory_space=pltpu.VMEM)
LIMIT = pltpu.CompilerParams(vmem_limit_bytes=16 << 20)
GROUP_X, GROUP_Y = 4, 4
UNROLL_C, UNROLL_X, UNROLL_Y = 4, 2, 4


def table_scratch(cells_z):
    return [pltpu.VMEM((2 * SHEAR, ROWS, cells_z), jnp.int32),
            pltpu.VMEM((4 * SHEAR, ROWS, cells_z), jnp.float32)]


def classify(density, transfer_table, step_len):
    count_x, count_y, cells_z = density.shape
    return pl.pallas_call(
        functools.partial(classify_kernel, step_len),
        out_shape=jax.ShapeDtypeStruct((4, count_x * (count_y + 1), cells_z), jnp.float32),
        in_specs=[VMEM, VMEM],
        out_specs=VMEM,
        scratch_shapes=[pltpu.VMEM((8, ROWS, cells_z), jnp.float32)],
        compiler_params=LIMIT,
        name="classify",
    )(transfer_table, density)


def x_march(density, halo, field, shear_x, direction):
    count_x, count_y, cells_z = density.shape
    return pl.pallas_call(
        functools.partial(x_kernel, GROUP_X),
        out_shape=(jax.ShapeDtypeStruct((count_y // 4, 4, 8, cells_z), jnp.float32),
                   jax.ShapeDtypeStruct((3, *field.shape[1:]), jnp.float32)),
        in_specs=[SMEM] * 2 + [VMEM] * 6,
        out_specs=(VMEM, VMEM),
        scratch_shapes=[pltpu.VMEM((count_x + 2, count_y + 2 * ROWS, cells_z), jnp.float32)]
        + table_scratch(cells_z),
        compiler_params=LIMIT,
        name="x_march",
    )(direction, shear_x, density, *halo, field)


def y_march(emitted, field, shear_y, direction, count_x):
    cells_z = field.shape[-1]
    return pl.pallas_call(
        functools.partial(y_kernel, GROUP_Y, count_x),
        out_shape=jax.ShapeDtypeStruct((count_x // 4, 4, 8, cells_z), jnp.float32),
        in_specs=[SMEM] * 2 + [VMEM] * 2,
        out_specs=VMEM,
        scratch_shapes=table_scratch(cells_z),
        compiler_params=LIMIT,
        name="y_march",
    )(direction, shear_y, emitted, field)


def bricks(density, low_x, high_x, low_y, high_y, transfer_table, shear_x, shear_y, direction,
           step_len):
    field = classify(density, transfer_table, step_len)
    part_x, emitted = x_march(density, (low_x, high_x, low_y, high_y), field, shear_x, direction)
    part_y = y_march(emitted, field, shear_y, direction, density.shape[0])
    return part_x, part_y


def join_kernel(turn_ref, part_x_ref, part_y_ref, out_x_ref, out_y_ref):
    row = lax.broadcasted_iota(jnp.int32, (8, LANES), 0)
    for family, (part_ref, out_ref) in enumerate(((part_x_ref, out_x_ref), (part_y_ref, out_y_ref))):
        count = part_ref.shape[0]
        turned = jnp.where(row < 4, turn_ref[family, 0], turn_ref[family, 1]) != 0
        total = part_ref[0, 3]
        for i in range(1, count):
            total = total + part_ref[i, 3]
        passed = jnp.zeros_like(total)
        colour = [jnp.zeros_like(total) for _ in range(3)]
        for i in range(count):
            depth = part_ref[i, 3]
            before = jnp.where(turned, total - (passed + depth), passed)
            passed = passed + depth
            seen = jnp.exp2(-before)
            colour = [colour[c] + seen * part_ref[i, c] for c in range(3)]
        for c, value in enumerate(colour + [1.0 - jnp.exp2(-total)]):
            for v in range(2):
                out_ref[v, c] = value[4 * v:4 * v + 4]


def join(part_x, part_y, direction):
    cells_z = part_x.shape[-1]
    vmem = pl.BlockSpec(memory_space=pltpu.VMEM)
    shape = jax.ShapeDtypeStruct((2, 4, 4, cells_z), jnp.float32)
    return pl.pallas_call(
        join_kernel,
        out_shape=(shape, shape),
        in_specs=[pl.BlockSpec(memory_space=pltpu.SMEM), vmem, vmem],
        out_specs=(vmem, vmem),
        name="join",
    )(direction, part_x, part_y)


def faces(block, axis, dim):
    count = lax.axis_size(axis)
    forward = [(i, i + 1) for i in range(count - 1)]
    backward = [(target, source) for source, target in forward]
    last = lax.index_in_dim(block, block.shape[dim] - 1, dim, keepdims=False)
    first = lax.index_in_dim(block, 0, dim, keepdims=False)
    return lax.ppermute(last, axis, forward), lax.ppermute(first, axis, backward)


def local(density, transfer_table, shear_x, shear_y, direction):
    low_x, high_x = faces(density, "gx", 0)
    low_y, high_y = faces(density, "gy", 1)
    step_len = 1.0 / (density.shape[0] * lax.axis_size("gx"))
    part_x, part_y = bricks(density, low_x, high_x, low_y, high_y, transfer_table, shear_x,
                            shear_y, direction, step_len)
    part_x = lax.all_to_all(part_x, "gx", split_axis=0, concat_axis=0, tiled=True)
    part_y = lax.all_to_all(part_y, "gy", split_axis=0, concat_axis=0, tiled=True)
    return join(part_x, part_y, direction)


def solution(mesh):
    placed = (P("gx", "gy", None), P(), P(None, "gx"), P(None, "gy"), P())
    return jax.shard_map(
        local,
        mesh=mesh,
        in_specs=placed,
        out_specs=(P(None, None, ("gy", "gx"), None), P(None, None, ("gx", "gy"), None)),
        check_vma=False,
    )
```

```python
import functools

import jax
import jax.numpy as jnp
from jax import lax
from jax.experimental import pallas as pl
from jax.experimental.pallas import tpu as pltpu
from jax.sharding import PartitionSpec as P

SHEAR = 16
ROWS = 8
PIECE = 4
LOG2E = 1.4426950408889634
PACK = 1024.0
ROUNDER = 12582912.0
GROUP_X, GROUP_Y = 4, 2
UNROLL_C, UNROLL_X, UNROLL_Y = 4, 2, 8

SMEM = pl.BlockSpec(memory_space=pltpu.SMEM)
VMEM = pl.BlockSpec(memory_space=pltpu.VMEM)


def lane_take(values, index):
    numbers = lax.GatherDimensionNumbers(
        offset_dims=(), collapsed_slice_dims=(1,), start_index_map=(1,),
        operand_batching_dims=(0,), start_indices_batching_dims=(0,))
    return lax.gather(values, index[..., None], numbers, slice_sizes=(1, 1),
                      mode=lax.GatherScatterMode.PROMISE_IN_BOUNDS)


def load_kernel(odd_ref, table_ref, density_ref, cells_ref, face_xa_ref, face_xb_ref, face_ya_ref,
                face_yb_ref, lut_ref, index_ref, mask_ref, sem):
    count_x, count_y, cells_z = density_ref.shape
    inner = cells_ref.at[pl.ds(1, count_x), pl.ds(ROWS, count_y), :]
    copy = pltpu.make_async_copy(density_ref, inner, sem)
    copy.start()

    lane = lax.broadcasted_iota(jnp.int32, (ROWS, cells_z), 1)
    levels = table_ref[...].astype(jnp.float32)
    for c in range(4):
        row = jnp.broadcast_to(levels[c:c + 1], (ROWS, cells_z))
        rise = jnp.where(lane == cells_z - 1, 0.0, pltpu.roll(row, cells_z - 1, 1) - row)
        lut_ref[c] = row + rise * (1.0 / PACK)

    def shifted(s, carry):
        source = lane - (s - SHEAR)
        kept = (source & -cells_z) == 0
        index_ref[s] = source & (cells_z - 1)
        mask_ref[s] = jnp.where(kept, -1.0, 0.0)
        mask_ref[s + 2 * SHEAR] = jnp.where(kept, 1.0, 0.0)
        return carry

    lax.fori_loop(0, 2 * SHEAR, shifted, 0, unroll=4)
    copy.wait()

    odd_x, odd_y = odd_ref[0] != 0, odd_ref[1] != 0
    first, last = cells_ref[1, pl.ds(ROWS, count_y), :], cells_ref[count_x, pl.ds(ROWS, count_y), :]
    face_xa_ref[...] = jnp.where(odd_x, last, first)
    face_xb_ref[...] = jnp.where(odd_x, first, last)
    first, last = (cells_ref[pl.ds(1, count_x), ROWS, :],
                   cells_ref[pl.ds(1, count_x), ROWS + count_y - 1, :])
    face_ya_ref[...] = jnp.where(odd_y, last, first)
    face_yb_ref[...] = jnp.where(odd_y, first, last)


def classify_kernel(step_len, cells_ref, lut_ref, field_ref):
    count_x, cells_z = cells_ref.shape[0] - 2, cells_ref.shape[2]
    count_y = cells_ref.shape[1] - 2 * ROWS
    pitch = field_ref.shape[1] // count_x

    def body(i, carry):
        for base in range(0, count_y, ROWS):
            scaled = cells_ref[i + 1, pl.ds(ROWS + base, ROWS), :] * (cells_z - 1.0)
            knot = scaled.astype(jnp.int32)
            part = (scaled - knot.astype(jnp.float32)) * PACK - 1.0
            classed = []
            for c in range(4):
                packed = lane_take(lut_ref[c], knot)
                level = (packed + ROUNDER) - ROUNDER
                classed.append(packed + (packed - level) * part)
            optical = classed[3] * (2.0 * step_len * LOG2E / 255.0)
            opacity = (1.0 - jnp.exp2(-optical)) * (1.0 / 255.0)
            values = [classed[c] * opacity for c in range(3)] + [optical]
            for c in range(4):
                field_ref[c, pl.ds(i * pitch + base, ROWS), :] = values[c]
        return carry

    lax.fori_loop(0, count_x, body, 0, unroll=UNROLL_C)


def march(fields, shift, turned, index_ref, mask_ref, states):
    place = shift + SHEAR
    index = index_ref[place]
    mask = mask_ref[place + jnp.where(turned, 2 * SHEAR, 0)]
    out = []
    for (red, green, blue, optical), state in zip(fields, states):
        depth = lane_take(optical, index) * mask
        after = state[0] + depth
        seen = jnp.exp2(jnp.where(turned, after, state[0])) * mask
        out.append((after, state[1] + seen * lane_take(red, index),
                    state[2] + seen * lane_take(green, index),
                    state[3] + seen * lane_take(blue, index)))
    return tuple(out)


def emit_out(out_ref, block, v, turned, state):
    sign = jnp.where(turned, 1.0, -1.0)
    total = state[0] * sign
    fade = jnp.exp2(jnp.where(turned, -total, 0.0)) * sign
    for c, value in enumerate([state[1] * fade, state[2] * fade, state[3] * fade, total]):
        for half in range(2):
            out_ref[2 * block + half, c, pl.ds(4 * v, 4), :] = value[4 * half:4 * half + 4]


def x_kernel(group, turn_ref, odd_ref, shear_ref, face_xa_ref, face_xb_ref, face_ya_ref,
             face_yb_ref, field_ref, index_ref, mask_ref, _, out_ref, emit_ref, cells_ref):
    count_x, cells_z = cells_ref.shape[0] - 2, cells_ref.shape[2]
    count_y = cells_ref.shape[1] - 2 * ROWS
    pitch = field_ref.shape[1] // count_x
    pad = ROWS
    lane = lax.broadcasted_iota(jnp.int32, (ROWS, cells_z), 1)

    odd_x, odd_y = odd_ref[0] != 0, odd_ref[1] != 0
    cells_ref[0, pl.ds(pad, count_y), :] = jnp.where(odd_x, face_xb_ref[...], face_xa_ref[...])
    cells_ref[count_x + 1, pl.ds(pad, count_y), :] = jnp.where(odd_x, face_xa_ref[...],
                                                               face_xb_ref[...])
    low_y = jnp.where(odd_y, face_yb_ref[...], face_ya_ref[...])
    high_y = jnp.where(odd_y, face_ya_ref[...], face_yb_ref[...])
    for i in range(count_x):
        cells_ref[i + 1, pl.ds(pad - 1, 1), :] = low_y[i:i + 1]
        cells_ref[i + 1, pl.ds(pad + count_y, 1), :] = high_y[i:i + 1]

    turned = [turn_ref[0, v] != 0 for v in range(2)]
    zeros = jnp.zeros((ROWS, cells_z), jnp.float32)
    up, down = (lane + 1) & (cells_z - 1), (lane - 1) & (cells_z - 1)

    def shade(i, base):
        here = cells_ref[i + 1, pl.ds(base + pad, ROWS), :]
        diff_x = (cells_ref[i + 2, pl.ds(base + pad, ROWS), :]
                  - cells_ref[i, pl.ds(base + pad, ROWS), :])
        diff_y = (cells_ref[i + 1, pl.ds(base + pad + 1, ROWS), :]
                  - cells_ref[i + 1, pl.ds(base + pad - 1, ROWS), :])
        above = jnp.where(lane == cells_z - 1, 0.0, lane_take(here, up))
        below = jnp.where(lane == 0, 0.0, lane_take(here, down))
        diff_z = above - below
        side = diff_y + diff_z
        facing = jnp.abs(diff_x + (side + side))
        norm = diff_x * diff_x + diff_y * diff_y + diff_z * diff_z + 0.04
        return 0.3 + (0.7 / 3.0) * facing * lax.rsqrt(norm)

    def block_of(block, carry):
        base = pl.multiple_of(block * (ROWS * group), ROWS)

        def body(i, states):
            fields = []
            for g in range(group):
                shaded = shade(i, base + g * ROWS)
                row = i * pitch + base + g * ROWS
                colours = [field_ref[c, pl.ds(row, ROWS), :] * shaded for c in range(3)]
                for c in range(3):
                    emit_ref[c, pl.ds(row, ROWS), :] = colours[c]
                fields.append((*colours, field_ref[3, pl.ds(row, ROWS), :]))
            return tuple(march(fields, shear_ref[v, i], turned[v], index_ref, mask_ref,
                               states[v]) for v in range(2))

        states = lax.fori_loop(0, count_x, body, (((zeros,) * 4,) * group,) * 2, unroll=UNROLL_X)
        for v in range(2):
            for g in range(group):
                emit_out(out_ref, block * group + g, v, turned[v], states[v][g])
        return carry

    lax.fori_loop(0, count_y // (ROWS * group), block_of, 0)


def y_kernel(group, first, pitch, turn_ref, shear_ref, emit_ref, field_ref, index_ref, mask_ref,
             out_ref):
    cells_z = emit_ref.shape[-1]
    count_y = shear_ref.shape[1]
    turned = [turn_ref[1, v] != 0 for v in range(2)]
    zeros = jnp.zeros((ROWS, cells_z), jnp.float32)

    def block_of(block, carry):
        def body(j, states):
            fields = []
            for g in range(group):
                start = (first + (block * group + g) * ROWS) * pitch
                rows = pl.ds(start + j, ROWS, stride=pitch)
                fields.append((emit_ref[0, rows, :], emit_ref[1, rows, :], emit_ref[2, rows, :],
                               field_ref[3, rows, :]))
            return tuple(march(fields, shear_ref[v, j], turned[v], index_ref, mask_ref,
                               states[v]) for v in range(2))

        states = lax.fori_loop(0, count_y, body, (((zeros,) * 4,) * group,) * 2, unroll=UNROLL_Y)
        for v in range(2):
            for g in range(group):
                emit_out(out_ref, block * group + g, v, turned[v], states[v][g])
        return carry

    lax.fori_loop(0, out_ref.shape[0] * PIECE // (ROWS * group), block_of, 0)


def options(micros):
    return dict(
        compiler_params=pltpu.CompilerParams(vmem_limit_bytes=16 << 20),
        cost_estimate=pl.CostEstimate(flops=0, transcendentals=0,
                                      bytes_accessed=int(micros * 3.5e6)))


def floats(*shape):
    return jax.ShapeDtypeStruct(shape, jnp.float32)


def load(density, transfer_table, odd):
    count_x, count_y, cells_z = density.shape
    return pl.pallas_call(
        load_kernel,
        out_shape=(floats(count_x + 2, count_y + 2 * ROWS, cells_z),
                   floats(count_y, cells_z), floats(count_y, cells_z),
                   floats(count_x, cells_z), floats(count_x, cells_z),
                   floats(4, ROWS, cells_z),
                   jax.ShapeDtypeStruct((2 * SHEAR, ROWS, cells_z), jnp.int32),
                   floats(4 * SHEAR, ROWS, cells_z)),
        in_specs=[SMEM, VMEM, pl.BlockSpec(memory_space=pl.ANY)],
        out_specs=(VMEM,) * 8,
        scratch_shapes=[pltpu.SemaphoreType.DMA],
        name="load",
        **options(2),
    )(odd, transfer_table, density)


def classify(cells, lut, step_len):
    count_x, count_y, cells_z = cells.shape[0] - 2, cells.shape[1] - 2 * ROWS, cells.shape[2]
    return pl.pallas_call(
        functools.partial(classify_kernel, step_len),
        out_shape=floats(4, count_x * (count_y + 1), cells_z),
        in_specs=[VMEM, VMEM],
        out_specs=VMEM,
        name="classify",
        **options(3),
    )(cells, lut)


def x_march(cells, halo, field, shifts, shear_x, direction, odd):
    count_y, cells_z = cells.shape[1] - 2 * ROWS, cells.shape[2]
    part, emitted, _ = pl.pallas_call(
        functools.partial(x_kernel, GROUP_X),
        out_shape=(floats(count_y // PIECE, 4, 2 * PIECE, cells_z),
                   floats(3, *field.shape[1:]), floats(*cells.shape)),
        in_specs=[SMEM] * 3 + [VMEM] * 8,
        out_specs=(VMEM,) * 3,
        input_output_aliases={10: 2},
        name="x_march",
        **options(8),
    )(direction, odd, shear_x, *halo, field, *shifts, cells)
    return part, emitted


def y_march(emitted, field, shifts, shear_y, direction, count_x, first, size):
    cells_z = field.shape[-1]
    return pl.pallas_call(
        functools.partial(y_kernel, GROUP_Y, first, field.shape[1] // count_x),
        out_shape=floats(size // PIECE, 4, 2 * PIECE, cells_z),
        in_specs=[SMEM] * 2 + [VMEM] * 4,
        out_specs=VMEM,
        name=f"y_march_{first}",
        **options(2.5),
    )(direction, shear_y, emitted, field, *shifts)


def bricks(density, low_x, high_x, low_y, high_y, transfer_table, shear_x, shear_y, direction,
           step_len):
    odd = jnp.zeros((2,), jnp.int32)
    cells, xa, xb, ya, yb, lut, *shifts = load(density, transfer_table, odd)
    field = classify(cells, lut, step_len)
    part_x, emitted = x_march(cells, (low_x, high_x, low_y, high_y), field, shifts, shear_x,
                              direction, odd)
    count_x = density.shape[0]
    part_y = jnp.concatenate([
        y_march(emitted, field, shifts, shear_y, direction, count_x, first, count_x // 2)
        for first in (0, count_x // 2)])
    return part_x, part_y


def neighbours(axis, offset):
    count = lax.axis_size(axis)
    pairs = [(i, i + 1) for i in range(offset, count - 1, 2)]
    return pairs + [(target, source) for source, target in pairs]


def swapped(axis, mask):
    return [(i, i ^ mask) for i in range(lax.axis_size(axis))]


def over(mine, theirs, lower, turned):
    mine_ahead = turned ^ lower
    front = jnp.where(mine_ahead, mine, theirs)
    back = jnp.where(mine_ahead, theirs, mine)
    channel = lax.broadcasted_iota(jnp.int32, (1, 4, 1, 1), 1)
    return front + back * jnp.where(channel == 3, 1.0, jnp.exp2(-front[:, 3:4]))


def halve(parts, high):
    pairs = parts.reshape(parts.shape[0] // 2, 2, *parts.shape[1:])
    return (jnp.where(high, pairs[:, 1], pairs[:, 0]), jnp.where(high, pairs[:, 0], pairs[:, 1]))


def ring_halve(parts, inner, upper):
    small, large = (jnp.where(inner, parts[1], parts[0]), jnp.where(inner, parts[2], parts[3]))
    return jnp.stack([jnp.where(upper, large, small), jnp.where(upper, small, large)])


class Exchange:
    def __init__(self, axis, direction):
        row = lax.broadcasted_iota(jnp.int32, (1, 1, 2 * PIECE, 1), 2)
        self.turned = jnp.where(row < PIECE, direction[0], direction[1]) != 0
        self.axis, self.me = axis, lax.axis_index(axis)

    def bit(self, mask):
        return (self.me & mask) != 0

    def send(self, keep, give, mask, lower_bit):
        self.keep, self.lower = keep, ~self.bit(lower_bit)
        self.got = lax.ppermute(give, self.axis, swapped(self.axis, mask))

    def receive(self):
        return over(self.keep, self.got, self.lower, self.turned)

    def pair(self, parts, mask):
        keep, give = halve(parts, self.bit(mask))
        self.send(keep, give, mask, mask)

    def ring_first(self, parts, mask):
        upper = self.bit(2 * mask)
        inner = self.bit(mask) ^ upper
        self.send(ring_halve(parts, inner, upper), ring_halve(parts, ~inner, upper), mask, mask)

    def ring_second(self, parts, mask):
        self.send(parts[:1], parts[1:], 3 * mask, 2 * mask)

    def image(self, parts):
        channel = lax.broadcasted_iota(jnp.int32, (1, 4, 1, 1), 1)
        done = jnp.where(channel == 3, 1.0 - jnp.exp2(-parts), parts)[0]
        return done.reshape(4, 2, PIECE, done.shape[-1]).transpose(1, 0, 2, 3)


def local(density, transfer_table, shear_x, shear_y, direction):
    count_x = density.shape[0]
    step_len = 1.0 / (count_x * lax.axis_size("gx"))
    odd = jnp.stack([lax.axis_index("gx") & 1, lax.axis_index("gy") & 1]).astype(jnp.int32)
    cells, *faces, lut, index, mask = load(density, transfer_table, odd)
    shifts = (index, mask)
    halo = [lax.ppermute(face, axis, neighbours(axis, offset)) for face, axis, offset in
            zip(faces, ("gx", "gx", "gy", "gy"), (1, 0, 1, 0))]
    field = classify(cells, lut, step_len)
    part_x, emitted = x_march(cells, halo, field, shifts, shear_x, direction, odd)

    x, y = Exchange("gx", direction[0]), Exchange("gy", direction[1])
    x.pair(part_x, 1)
    half = count_x // 2
    part_y = [y_march(emitted, field, shifts, shear_y, direction, count_x, first, half)
              for first in (0, half)]
    x.pair(x.receive(), 2)
    x.ring_first(x.receive(), 4)
    y.pair(jnp.concatenate(part_y), 1)
    x.ring_second(x.receive(), 4)
    y.ring_first(y.receive(), 2)
    image_x = x.image(x.receive())
    y.ring_second(y.receive(), 2)
    return image_x, y.image(y.receive())


def solution(mesh):
    placed = (P("gx", "gy", None), P(), P(None, "gx"), P(None, "gy"), P())
    return jax.shard_map(
        local,
        mesh=mesh,
        in_specs=placed,
        out_specs=(P(None, None, ("gy", "gx"), None), P(None, None, ("gx", "gy"), None)),
        check_vma=False,
    )
```

```python
import functools

import jax
import jax.numpy as jnp
from jax import lax
from jax.experimental import pallas as pl
from jax.experimental.pallas import tpu as pltpu
from jax.sharding import PartitionSpec as P


SHEAR = 16
ROWS = 8
PIECE = 4
LOG2E = 1.4426950408889634
PACK = 1024.0
ROUNDER = 12582912.0
GROUP_X, GROUP_Y = 4, 2
UNROLL_C, UNROLL_X, UNROLL_Y = 4, 2, 8

SMEM = pl.BlockSpec(memory_space=pltpu.SMEM)
VMEM = pl.BlockSpec(memory_space=pltpu.VMEM)
HBM = pl.BlockSpec(memory_space=pltpu.HBM)
STAGES = ((1, 2, 4, 8), (1, 2, 4))


def slot_of(i, count):
    piece = i // PIECE
    return (piece % 2) * (count // 2) + (piece // 2) * PIECE + i % PIECE


def lane_take(values, index):
    numbers = lax.GatherDimensionNumbers(
        offset_dims=(), collapsed_slice_dims=(1,), start_index_map=(1,),
        operand_batching_dims=(0,), start_indices_batching_dims=(0,))
    return lax.gather(values, index[..., None], numbers, slice_sizes=(1, 1),
                      mode=lax.GatherScatterMode.PROMISE_IN_BOUNDS)


def load_kernel(stages, turn_ref, spot_ref, table_ref, density_ref, cells_ref, face_xa_ref,
                face_xb_ref, face_ya_ref, face_yb_ref, lut_ref, index_ref, mask_ref, ahead_ref,
                levels_ref, sem, table_sem):
    count_x, count_y, cells_z = density_ref.shape
    inner = cells_ref.at[pl.ds(1, count_x), pl.ds(ROWS, count_y), :]
    copy = pltpu.make_async_copy(density_ref, inner, sem)
    copy.start()
    table_copy = pltpu.make_async_copy(table_ref, levels_ref, table_sem)
    table_copy.start()

    lane = lax.broadcasted_iota(jnp.int32, (ROWS, cells_z), 1)
    row = lax.broadcasted_iota(jnp.int32, (ROWS, cells_z), 0)
    stage = 0
    for family, masks in enumerate(stages):
        turned = jnp.where(row < PIECE, turn_ref[family, 0], turn_ref[family, 1])
        for mask in masks:
            upper = jnp.where((spot_ref[family] & mask) != 0, 1, 0)
            ahead_ref[stage] = jnp.where(turned == upper, 1.0, 0.0)
            stage += 1

    def shifted(s, carry):
        source = lane - (s - SHEAR)
        kept = (source & -cells_z) == 0
        index_ref[s] = source & (cells_z - 1)
        mask_ref[s] = jnp.where(kept, -1.0, 0.0)
        mask_ref[s + 2 * SHEAR] = jnp.where(kept, 1.0, 0.0)
        return carry

    lax.fori_loop(0, 2 * SHEAR, shifted, 0, unroll=4)
    table_copy.wait()
    levels = levels_ref[...].astype(jnp.float32)
    for c in range(4):
        level = jnp.broadcast_to(levels[c:c + 1], (ROWS, cells_z))
        rise = jnp.where(lane == cells_z - 1, 0.0, pltpu.roll(level, cells_z - 1, 1) - level)
        lut_ref[c] = level + rise * (1.0 / PACK)
    copy.wait()

    odd_x, odd_y = (spot_ref[0] & 1) != 0, (spot_ref[1] & 1) != 0
    first, last = cells_ref[1, pl.ds(ROWS, count_y), :], cells_ref[count_x, pl.ds(ROWS, count_y), :]
    face_xa_ref[...] = jnp.where(odd_x, last, first)
    face_xb_ref[...] = jnp.where(odd_x, first, last)
    first, last = (cells_ref[pl.ds(1, count_x), ROWS, :],
                   cells_ref[pl.ds(1, count_x), ROWS + count_y - 1, :])
    face_ya_ref[...] = jnp.where(odd_y, last, first)
    face_yb_ref[...] = jnp.where(odd_y, first, last)


def classify_kernel(step_len, cells_ref, lut_ref, field_ref):
    count_x, cells_z = cells_ref.shape[0] - 2, cells_ref.shape[2]
    count_y = cells_ref.shape[1] - 2 * ROWS
    pitch = field_ref.shape[1] // count_x

    def body(i, carry):
        slot = slot_of(i, count_x) * pitch
        for base in range(0, count_y, ROWS):
            scaled = cells_ref[i + 1, pl.ds(ROWS + base, ROWS), :] * (cells_z - 1.0)
            knot = scaled.astype(jnp.int32)
            part = (scaled - knot.astype(jnp.float32)) * PACK - 1.0
            classed = []
            for c in range(4):
                packed = lane_take(lut_ref[c], knot)
                level = (packed + ROUNDER) - ROUNDER
                classed.append(packed + (packed - level) * part)
            optical = classed[3] * (2.0 * step_len * LOG2E / 255.0)
            opacity = (1.0 - jnp.exp2(-optical)) * (1.0 / 255.0)
            values = [classed[c] * opacity for c in range(3)] + [optical]
            for c in range(4):
                field_ref[c, pl.ds(slot + base, ROWS), :] = values[c]
        return carry

    lax.fori_loop(0, count_x, body, 0, unroll=UNROLL_C)


def march(fields, shift, turned, index_ref, mask_ref, states):
    place = shift + SHEAR
    index = index_ref[place]
    mask = mask_ref[place + jnp.where(turned, 2 * SHEAR, 0)]
    out = []
    for (red, green, blue, optical), state in zip(fields, states):
        depth = lane_take(optical, index) * mask
        after = state[0] + depth
        seen = jnp.exp2(jnp.where(turned, after, state[0])) * mask
        out.append((after, state[1] + seen * lane_take(red, index),
                    state[2] + seen * lane_take(green, index),
                    state[3] + seen * lane_take(blue, index)))
    return tuple(out)


def settle(turned, state):
    sign = jnp.where(turned, 1.0, -1.0)
    total = state[0] * sign
    fade = jnp.exp2(jnp.where(turned, -total, 0.0)) * sign
    return [state[1] * fade, state[2] * fade, state[3] * fade, total]


def x_kernel(group, turn_ref, spot_ref, shear_ref, face_xa_ref, face_xb_ref, face_ya_ref,
             face_yb_ref, field_ref, index_ref, mask_ref, _, keep_ref, give_ref, emit_ref,
             cells_ref):
    count_x, cells_z = cells_ref.shape[0] - 2, cells_ref.shape[2]
    count_y = cells_ref.shape[1] - 2 * ROWS
    pitch = field_ref.shape[1] // count_x
    pad = ROWS
    lane = lax.broadcasted_iota(jnp.int32, (ROWS, cells_z), 1)

    odd_x, odd_y = (spot_ref[0] & 1) != 0, (spot_ref[1] & 1) != 0
    cells_ref[0, pl.ds(pad, count_y), :] = jnp.where(odd_x, face_xb_ref[...], face_xa_ref[...])
    cells_ref[count_x + 1, pl.ds(pad, count_y), :] = jnp.where(odd_x, face_xa_ref[...],
                                                               face_xb_ref[...])
    low_y = jnp.where(odd_y, face_yb_ref[...], face_ya_ref[...])
    high_y = jnp.where(odd_y, face_ya_ref[...], face_yb_ref[...])
    for i in range(count_x):
        cells_ref[i + 1, pl.ds(pad - 1, 1), :] = low_y[i:i + 1]
        cells_ref[i + 1, pl.ds(pad + count_y, 1), :] = high_y[i:i + 1]

    turned = [turn_ref[0, v] != 0 for v in range(2)]
    zeros = jnp.zeros((ROWS, cells_z), jnp.float32)
    up, down = (lane + 1) & (cells_z - 1), (lane - 1) & (cells_z - 1)

    def shade(i, base):
        here = cells_ref[i + 1, pl.ds(base + pad, ROWS), :]
        diff_x = (cells_ref[i + 2, pl.ds(base + pad, ROWS), :]
                  - cells_ref[i, pl.ds(base + pad, ROWS), :])
        diff_y = (cells_ref[i + 1, pl.ds(base + pad + 1, ROWS), :]
                  - cells_ref[i + 1, pl.ds(base + pad - 1, ROWS), :])
        above = jnp.where(lane == cells_z - 1, 0.0, lane_take(here, up))
        below = jnp.where(lane == 0, 0.0, lane_take(here, down))
        diff_z = above - below
        side = diff_y + diff_z
        facing = jnp.abs(diff_x + (side + side))
        norm = diff_x * diff_x + diff_y * diff_y + diff_z * diff_z + 0.04
        return 0.3 + (0.7 / 3.0) * facing * lax.rsqrt(norm)

    def block_of(block, carry):
        base = pl.multiple_of(block * (ROWS * group), ROWS)

        def body(i, states):
            fields = []
            slot = slot_of(i, count_x) * pitch
            for g in range(group):
                shaded = shade(i, base + g * ROWS)
                row = slot + base + g * ROWS
                colours = [field_ref[c, pl.ds(row, ROWS), :] * shaded for c in range(3)]
                for c in range(3):
                    emit_ref[c, pl.ds(row, ROWS), :] = colours[c]
                fields.append((*colours, field_ref[3, pl.ds(row, ROWS), :]))
            return tuple(march(fields, shear_ref[v, i], turned[v], index_ref, mask_ref,
                               states[v]) for v in range(2))

        states = lax.fori_loop(0, count_x, body, (((zeros,) * 4,) * group,) * 2, unroll=UNROLL_X)
        for v in range(2):
            for g in range(group):
                for c, value in enumerate(settle(turned[v], states[v][g])):
                    even, odd = value[:PIECE], value[PIECE:]
                    spot, rows = block * group + g, pl.ds(PIECE * v, PIECE)
                    keep_ref[spot, c, rows, :] = jnp.where(odd_x, odd, even)
                    give_ref[spot, c, rows, :] = jnp.where(odd_x, even, odd)
        return carry

    lax.fori_loop(0, count_y // (ROWS * group), block_of, 0)


def y_kernel(group, kept, pitch, turn_ref, spot_ref, shear_ref, emit_ref, field_ref, index_ref, mask_ref,
             out_ref):
    cells_z = emit_ref.shape[-1]
    count_y = shear_ref.shape[1]
    size = out_ref.shape[0] * PIECE
    first = ((spot_ref[1] & 1) ^ (1 - kept)) * size
    turned = [turn_ref[1, v] != 0 for v in range(2)]
    zeros = jnp.zeros((ROWS, cells_z), jnp.float32)

    def block_of(block, carry):
        def body(j, states):
            fields = []
            for g in range(group):
                start = (first + (block * group + g) * ROWS) * pitch
                rows = pl.ds(start + j, ROWS, stride=pitch)
                fields.append((emit_ref[0, rows, :], emit_ref[1, rows, :], emit_ref[2, rows, :],
                               field_ref[3, rows, :]))
            return tuple(march(fields, shear_ref[v, j], turned[v], index_ref, mask_ref,
                               states[v]) for v in range(2))

        states = lax.fori_loop(0, count_y, body, (((zeros,) * 4,) * group,) * 2, unroll=UNROLL_Y)
        for v in range(2):
            for g in range(group):
                for c, value in enumerate(settle(turned[v], states[v][g])):
                    for half in range(2):
                        out_ref[2 * (block * group + g) + half, c, pl.ds(PIECE * v, PIECE), :] = (
                            value[PIECE * half:PIECE * (half + 1)])
        return carry

    lax.fori_loop(0, size // (ROWS * group), block_of, 0)


def options(micros, limit=16 << 20):
    return dict(
        compiler_params=pltpu.CompilerParams(vmem_limit_bytes=limit),
        cost_estimate=pl.CostEstimate(flops=0, transcendentals=0,
                                      bytes_accessed=int(micros * 3.5e6)))


def floats(*shape):
    return jax.ShapeDtypeStruct(shape, jnp.float32)


def load(density, transfer_table, direction, spot):
    count_x, count_y, cells_z = density.shape
    return pl.pallas_call(
        functools.partial(load_kernel, STAGES),
        out_shape=(floats(count_x + 2, count_y + 2 * ROWS, cells_z),
                   floats(count_y, cells_z), floats(count_y, cells_z),
                   floats(count_x, cells_z), floats(count_x, cells_z),
                   floats(4, ROWS, cells_z),
                   jax.ShapeDtypeStruct((2 * SHEAR, ROWS, cells_z), jnp.int32),
                   floats(4 * SHEAR, ROWS, cells_z),
                   floats(sum(map(len, STAGES)), ROWS, cells_z)),
        in_specs=[SMEM, SMEM, HBM, HBM],
        out_specs=(VMEM,) * 9,
        scratch_shapes=[pltpu.VMEM(transfer_table.shape, jnp.int32), pltpu.SemaphoreType.DMA,
                        pltpu.SemaphoreType.DMA],
        name="load",
        **options(2),
    )(direction, spot, transfer_table, density)


def classify(cells, lut, step_len):
    count_x, count_y, cells_z = cells.shape[0] - 2, cells.shape[1] - 2 * ROWS, cells.shape[2]
    return pl.pallas_call(
        functools.partial(classify_kernel, step_len),
        out_shape=floats(4, count_x * (count_y + 1), cells_z),
        in_specs=[VMEM, VMEM],
        out_specs=VMEM,
        name="classify",
        **options(3),
    )(cells, lut)


def x_march(cells, halo, field, shifts, shear_x, direction, spot):
    count_y, cells_z = cells.shape[1] - 2 * ROWS, cells.shape[2]
    part = floats(count_y // (2 * PIECE), 4, 2 * PIECE, cells_z)
    keep, give, emitted, _ = pl.pallas_call(
        functools.partial(x_kernel, GROUP_X),
        out_shape=(part, part, floats(3, *field.shape[1:]), floats(*cells.shape)),
        in_specs=[SMEM] * 3 + [VMEM] * 8,
        out_specs=(VMEM,) * 4,
        input_output_aliases={10: 3},
        name="x_march",
        **options(8),
    )(direction, spot, shear_x, *halo, field, *shifts, cells)
    return keep, give, emitted


def y_march(emitted, field, shifts, shear_y, direction, spot, count_x, kept):
    cells_z = field.shape[-1]
    return pl.pallas_call(
        functools.partial(y_kernel, GROUP_Y, kept, field.shape[1] // count_x),
        out_shape=floats(count_x // (2 * PIECE), 4, 2 * PIECE, cells_z),
        in_specs=[SMEM] * 3 + [VMEM] * 4,
        out_specs=VMEM,
        **options(2.5),
    )(direction, spot, shear_y, emitted, field, *shifts)


def neighbours(axis, offset):
    count = lax.axis_size(axis)
    pairs = [(i, i + 1) for i in range(offset, count - 1, 2)]
    return pairs + [(target, source) for source, target in pairs]


def swapped(axis, mask):
    return [(i, i ^ mask) for i in range(lax.axis_size(axis))]


def stage_kernel(family, mask, order, split, spot_ref, keep_ref, got_ref, ahead_ref, *out_refs):
    me = spot_ref[family]
    mine_ahead = ahead_ref[order] > 0.5

    def joined(p):
        mine, theirs = [[ref[p, c] for c in range(4)] for ref in (keep_ref, got_ref)]
        seen = jnp.exp2(-jnp.where(mine_ahead, mine[3], theirs[3]))
        near, far = jnp.where(mine_ahead, 1.0, seen), jnp.where(mine_ahead, seen, 1.0)
        return [mine[c] * near + theirs[c] * far for c in range(3)] + [mine[3] + theirs[3]]

    parts = [joined(p) for p in range(keep_ref.shape[0])]
    if split == "image":
        red, green, blue, total = parts[0]
        for c, value in enumerate((red, green, blue, 1.0 - jnp.exp2(-total))):
            for v in range(2):
                out_refs[0][v, c] = value[PIECE * v:PIECE * (v + 1)]
        return
    pick = lambda flag, a, b: [jnp.where(flag, one, two) for one, two in zip(a, b)]
    if split == "pair":
        high = (me & mask) != 0
        pairs = list(zip(parts[::2], parts[1::2]))
        keep = [pick(high, b, a) for a, b in pairs]
        give = [pick(high, a, b) for a, b in pairs]
    elif split == "ring_first":
        upper = (me & (2 * mask)) != 0
        edge = ((me // mask + me // (2 * mask)) & 1) == 0
        ends, middle = (parts[0], parts[3]), (parts[1], parts[2])
        small, large = [pick(edge, ends[k], middle[k]) for k in range(2)]
        keep = [pick(upper, large, small), pick(upper, small, large)]
        small, large = [pick(edge, middle[k], ends[k]) for k in range(2)]
        give = [pick(upper, large, small), pick(upper, small, large)]
    else:
        keep, give = parts[:1], parts[1:]
    for ref, pieces in zip(out_refs, (keep, give)):
        for p, piece in enumerate(pieces):
            for c in range(4):
                ref[p, c] = piece[c]


class Exchange:
    def __init__(self, family, axis, ahead, spot):
        self.family, self.axis, self.ahead, self.spot = family, axis, ahead, spot
        self.stage = 0

    def send(self, keep, give, mask):
        self.keep, self.stage = keep, self.stage + 1
        self.got = lax.ppermute(give, self.axis, swapped(self.axis, mask))

    def meet(self, split, mask=0):
        count, *rest = self.keep.shape
        if split == "image":
            shape = floats(2, 4, PIECE, rest[-1])
        else:
            shape = (floats(count // 2, *rest),) * 2
        order = self.family * len(STAGES[0]) + self.stage - 1
        return pl.pallas_call(
            functools.partial(stage_kernel, self.family, mask, order, split),
            out_shape=shape,
            in_specs=[SMEM] + [VMEM] * 3,
            out_specs=VMEM if split == "image" else (VMEM, VMEM),
            **options(0.3),
        )(self.spot, self.keep, self.got, self.ahead)


def local(density, transfer_table, shear_x, shear_y, direction):
    count_x = density.shape[0]
    step_len = 1.0 / (count_x * lax.axis_size("gx"))
    spot = jnp.stack([lax.axis_index("gx"), lax.axis_index("gy")]).astype(jnp.int32)
    cells, *faces, lut, index, mask, ahead = load(density, transfer_table, direction, spot)
    shifts = (index, mask)
    halo = [lax.ppermute(face, axis, neighbours(axis, offset)) for face, axis, offset in
            zip(faces, ("gx", "gx", "gy", "gy"), (1, 0, 1, 0))]
    field = classify(cells, lut, step_len)
    keep_x, give_x, emitted = x_march(cells, halo, field, shifts, shear_x, direction, spot)

    x, y = Exchange(0, "gx", ahead, spot), Exchange(1, "gy", ahead, spot)
    x.send(keep_x, give_x, 1)
    given = y_march(emitted, field, shifts, shear_y, direction, spot, count_x, 0)
    kept = y_march(emitted, field, shifts, shear_y, direction, spot, count_x, 1)
    x.send(*x.meet("pair", 2), 2)
    y.send(kept, given, 1)
    x.send(*x.meet("ring_first", 4), 4)
    x.send(*x.meet("ring_second"), 12)
    y.send(*y.meet("ring_first", 2), 2)
    image_x = x.meet("image")
    y.send(*y.meet("ring_second"), 6)
    return image_x, y.meet("image")


def solution(mesh):
    placed = (P("gx", "gy", None), P(), P(None, "gx"), P(None, "gy"), P())
    return jax.shard_map(
        local,
        mesh=mesh,
        in_specs=placed,
        out_specs=(P(None, None, ("gy", "gx"), None), P(None, None, ("gx", "gy"), None)),
        check_vma=False,
    )
```

```python
import functools

import jax
import jax.numpy as jnp
from jax import lax
from jax.experimental import pallas as pl
from jax.experimental.pallas import tpu as pltpu
from jax.sharding import PartitionSpec as P


SHEAR = 16
ROWS = 8
PIECE = 4
LOG2E = 1.4426950408889634
LOAD_COST = 2
PACK = 1024.0
ROUNDER = 12582912.0
GROUP_X, GROUP_Y = 4, 2
UNROLL_C, UNROLL_E, UNROLL_X, UNROLL_Y = 32, 32, 32, 64

SMEM = pl.BlockSpec(memory_space=pltpu.SMEM)
VMEM = pl.BlockSpec(memory_space=pltpu.VMEM)
HBM = pl.BlockSpec(memory_space=pltpu.HBM)
STAGES = (("gx", (1, 2, 4, 8)), ("gy", (1, 2, 4)))


def is_set(axis, mask):
    return (lax.axis_index(axis) & mask) != 0


def slot_of(i, count):
    piece = i // PIECE
    return (piece % 2) * (count // 2) + (piece // 2) * PIECE + i % PIECE


def lane_take(values, index):
    numbers = lax.GatherDimensionNumbers(
        offset_dims=(), collapsed_slice_dims=(1,), start_index_map=(1,),
        operand_batching_dims=(0,), start_indices_batching_dims=(0,))
    return lax.gather(values, index[..., None], numbers, slice_sizes=(1, 1),
                      mode=lax.GatherScatterMode.PROMISE_IN_BOUNDS)


def load_kernel(density_ref, cells_ref, face_xa_ref, face_xb_ref, face_ya_ref, face_yb_ref,
                index_ref, mask_ref, sem):
    count_x, count_y, cells_z = density_ref.shape
    inner = cells_ref.at[pl.ds(1, count_x), pl.ds(ROWS, count_y), :]
    copy = pltpu.make_async_copy(density_ref, inner, sem)
    copy.start()

    lane = lax.broadcasted_iota(jnp.int32, (ROWS, cells_z), 1)

    def shifted(s, carry):
        source = lane - (s - SHEAR)
        kept = (source & -cells_z) == 0
        index_ref[s] = source & (cells_z - 1)
        mask_ref[s] = jnp.where(kept, -1.0, 0.0)
        mask_ref[s + 2 * SHEAR] = jnp.where(kept, 1.0, 0.0)
        return carry

    lax.fori_loop(0, 2 * SHEAR, shifted, 0, unroll=4)
    copy.wait()

    odd_x, odd_y = is_set("gx", 1), is_set("gy", 1)
    first, last = cells_ref[1, pl.ds(ROWS, count_y), :], cells_ref[count_x, pl.ds(ROWS, count_y), :]
    face_xa_ref[...] = jnp.where(odd_x, last, first)
    face_xb_ref[...] = jnp.where(odd_x, first, last)
    first, last = (cells_ref[pl.ds(1, count_x), ROWS, :],
                   cells_ref[pl.ds(1, count_x), ROWS + count_y - 1, :])
    face_ya_ref[...] = jnp.where(odd_y, last, first)
    face_yb_ref[...] = jnp.where(odd_y, first, last)


def classify_kernel(step_len, cells_ref, table_ref, field_ref, lut_ref):
    count_x, cells_z = cells_ref.shape[0] - 2, cells_ref.shape[2]
    count_y = cells_ref.shape[1] - 2 * ROWS
    pitch = field_ref.shape[1] // count_x
    lane = lax.broadcasted_iota(jnp.int32, (ROWS, cells_z), 1)
    levels = table_ref[...].astype(jnp.float32)
    for c in range(4):
        level = jnp.broadcast_to(levels[c:c + 1], (ROWS, cells_z))
        rise = jnp.where(lane == cells_z - 1, 0.0, pltpu.roll(level, cells_z - 1, 1) - level)
        lut_ref[c] = level + rise * (1.0 / PACK)

    def body(i, carry):
        slot = slot_of(i, count_x) * pitch
        for base in range(0, count_y, ROWS):
            scaled = cells_ref[i + 1, pl.ds(ROWS + base, ROWS), :] * (cells_z - 1.0)
            knot = scaled.astype(jnp.int32)
            part = (scaled - knot.astype(jnp.float32)) * PACK - 1.0
            classed = []
            for c in range(4):
                packed = lane_take(lut_ref[c], knot)
                level = (packed + ROUNDER) - ROUNDER
                classed.append(packed + (packed - level) * part)
            optical = classed[3] * (2.0 * step_len * LOG2E / 255.0)
            opacity = (1.0 - jnp.exp2(-optical)) * (1.0 / 255.0)
            values = [classed[c] * opacity for c in range(3)] + [optical]
            for c in range(4):
                field_ref[c, pl.ds(slot + base, ROWS), :] = values[c]
        return carry

    lax.fori_loop(0, count_x, body, 0, unroll=UNROLL_C)


def march(fields, shift, turned, index_ref, mask_ref, states):
    place = shift + SHEAR
    index = index_ref[place]
    mask = mask_ref[place + jnp.where(turned, 2 * SHEAR, 0)]
    out = []
    for (red, green, blue, optical), state in zip(fields, states):
        depth = lane_take(optical, index) * mask
        after = state[0] + depth
        seen = jnp.exp2(jnp.where(turned, after, state[0])) * mask
        out.append((after, state[1] + seen * lane_take(red, index),
                    state[2] + seen * lane_take(green, index),
                    state[3] + seen * lane_take(blue, index)))
    return tuple(out)


def settle(turned, state):
    sign = jnp.where(turned, 1.0, -1.0)
    total = state[0] * sign
    fade = jnp.exp2(jnp.where(turned, -total, 0.0)) * sign
    return [state[1] * fade, state[2] * fade, state[3] * fade, total]


def x_kernel(group, stages, turn_ref, shear_ref, face_xa_ref, face_xb_ref, face_ya_ref,
             face_yb_ref, field_ref, index_ref, mask_ref, _, keep_ref, give_ref, emit_ref,
             ahead_ref, cells_ref):
    count_x, cells_z = cells_ref.shape[0] - 2, cells_ref.shape[2]
    count_y = cells_ref.shape[1] - 2 * ROWS
    pitch = field_ref.shape[1] // count_x
    pad = ROWS
    lane = lax.broadcasted_iota(jnp.int32, (ROWS, cells_z), 1)

    row = lax.broadcasted_iota(jnp.int32, (ROWS, cells_z), 0)
    stage = 0
    for family, (axis, masks) in enumerate(stages):
        turned = jnp.where(row < PIECE, turn_ref[family, 0], turn_ref[family, 1])
        for mask in masks:
            ahead_ref[stage] = jnp.where(turned == jnp.where(is_set(axis, mask), 1, 0), 1.0, 0.0)
            stage += 1

    odd_x, odd_y = is_set("gx", 1), is_set("gy", 1)
    cells_ref[0, pl.ds(pad, count_y), :] = jnp.where(odd_x, face_xb_ref[...], face_xa_ref[...])
    cells_ref[count_x + 1, pl.ds(pad, count_y), :] = jnp.where(odd_x, face_xa_ref[...],
                                                               face_xb_ref[...])
    low_y = jnp.where(odd_y, face_yb_ref[...], face_ya_ref[...])
    high_y = jnp.where(odd_y, face_ya_ref[...], face_yb_ref[...])
    for i in range(count_x):
        cells_ref[i + 1, pl.ds(pad - 1, 1), :] = low_y[i:i + 1]
        cells_ref[i + 1, pl.ds(pad + count_y, 1), :] = high_y[i:i + 1]

    turned = [turn_ref[0, v] != 0 for v in range(2)]
    zeros = jnp.zeros((ROWS, cells_z), jnp.float32)
    up, down = (lane + 1) & (cells_z - 1), (lane - 1) & (cells_z - 1)

    def shade(i, base):
        here = cells_ref[i + 1, pl.ds(base + pad, ROWS), :]
        diff_x = (cells_ref[i + 2, pl.ds(base + pad, ROWS), :]
                  - cells_ref[i, pl.ds(base + pad, ROWS), :])
        diff_y = (cells_ref[i + 1, pl.ds(base + pad + 1, ROWS), :]
                  - cells_ref[i + 1, pl.ds(base + pad - 1, ROWS), :])
        above = jnp.where(lane == cells_z - 1, 0.0, lane_take(here, up))
        below = jnp.where(lane == 0, 0.0, lane_take(here, down))
        diff_z = above - below
        side = diff_y + diff_z
        facing = jnp.abs(diff_x + (side + side))
        norm = diff_x * diff_x + diff_y * diff_y + diff_z * diff_z + 0.04
        return 0.3 + (0.7 / 3.0) * facing * lax.rsqrt(norm)

    def emission(i, carry):
        slot = slot_of(i, count_x) * pitch
        for base in range(0, count_y, ROWS):
            shaded = shade(i, base)
            rows = pl.ds(slot + base, ROWS)
            for c in range(3):
                emit_ref[c, rows, :] = field_ref[c, rows, :] * shaded
        return carry

    lax.fori_loop(0, count_x, emission, 0, unroll=UNROLL_E)

    def block_of(block, carry):
        base = pl.multiple_of(block * (ROWS * group), ROWS)

        def body(i, states):
            fields = []
            slot = slot_of(i, count_x) * pitch
            for g in range(group):
                rows = pl.ds(slot + base + g * ROWS, ROWS)
                fields.append((emit_ref[0, rows, :], emit_ref[1, rows, :], emit_ref[2, rows, :],
                               field_ref[3, rows, :]))
            return tuple(march(fields, shear_ref[v, i], turned[v], index_ref, mask_ref,
                               states[v]) for v in range(2))

        states = lax.fori_loop(0, count_x, body, (((zeros,) * 4,) * group,) * 2, unroll=UNROLL_X)
        for v in range(2):
            for g in range(group):
                for c, value in enumerate(settle(turned[v], states[v][g])):
                    even, odd = value[:PIECE], value[PIECE:]
                    spot, rows = block * group + g, pl.ds(PIECE * v, PIECE)
                    keep_ref[spot, c, rows, :] = jnp.where(odd_x, odd, even)
                    give_ref[spot, c, rows, :] = jnp.where(odd_x, even, odd)
        return carry

    lax.fori_loop(0, count_y // (ROWS * group), block_of, 0)


def y_kernel(group, kept, pitch, turn_ref, shear_ref, emit_ref, field_ref, index_ref, mask_ref,
             out_ref):
    cells_z = emit_ref.shape[-1]
    count_y = shear_ref.shape[1]
    size = out_ref.shape[0] * PIECE
    first = jnp.where(is_set("gy", 1) == bool(kept), size, 0)
    turned = [turn_ref[1, v] != 0 for v in range(2)]
    zeros = jnp.zeros((ROWS, cells_z), jnp.float32)

    def block_of(block, carry):
        def body(j, states):
            fields = []
            for g in range(group):
                start = (first + (block * group + g) * ROWS) * pitch
                rows = pl.ds(start + j, ROWS, stride=pitch)
                fields.append((emit_ref[0, rows, :], emit_ref[1, rows, :], emit_ref[2, rows, :],
                               field_ref[3, rows, :]))
            return tuple(march(fields, shear_ref[v, j], turned[v], index_ref, mask_ref,
                               states[v]) for v in range(2))

        states = lax.fori_loop(0, count_y, body, (((zeros,) * 4,) * group,) * 2, unroll=UNROLL_Y)
        for v in range(2):
            for g in range(group):
                for c, value in enumerate(settle(turned[v], states[v][g])):
                    for half in range(2):
                        out_ref[2 * (block * group + g) + half, c, pl.ds(PIECE * v, PIECE), :] = (
                            value[PIECE * half:PIECE * (half + 1)])
        return carry

    lax.fori_loop(0, size // (ROWS * group), block_of, 0)


def options(micros, limit=16 << 20):
    return dict(
        compiler_params=pltpu.CompilerParams(vmem_limit_bytes=limit),
        cost_estimate=pl.CostEstimate(flops=0, transcendentals=0,
                                      bytes_accessed=int(micros * 3.5e6)))


def floats(*shape):
    return jax.ShapeDtypeStruct(shape, jnp.float32)


def load(density):
    count_x, count_y, cells_z = density.shape
    return pl.pallas_call(
        load_kernel,
        out_shape=(floats(count_x + 2, count_y + 2 * ROWS, cells_z),
                   floats(count_y, cells_z), floats(count_y, cells_z),
                   floats(count_x, cells_z), floats(count_x, cells_z),
                   jax.ShapeDtypeStruct((2 * SHEAR, ROWS, cells_z), jnp.int32),
                   floats(4 * SHEAR, ROWS, cells_z)),
        in_specs=[HBM],
        out_specs=(VMEM,) * 7,
        scratch_shapes=[pltpu.SemaphoreType.DMA],
        name="load",
        **options(LOAD_COST),
    )(density)


def classify(cells, transfer_table, step_len):
    count_x, count_y, cells_z = cells.shape[0] - 2, cells.shape[1] - 2 * ROWS, cells.shape[2]
    return pl.pallas_call(
        functools.partial(classify_kernel, step_len),
        out_shape=floats(4, count_x * (count_y + 1), cells_z),
        in_specs=[VMEM, VMEM],
        out_specs=VMEM,
        scratch_shapes=[pltpu.VMEM((4, ROWS, cells_z), jnp.float32)],
        name="classify",
        **options(3),
    )(cells, transfer_table)


def x_march(cells, halo, field, shifts, shear_x, direction):
    count_y, cells_z = cells.shape[1] - 2 * ROWS, cells.shape[2]
    part = floats(count_y // (2 * PIECE), 4, 2 * PIECE, cells_z)
    ahead = floats(sum(len(masks) for _, masks in STAGES), ROWS, cells_z)
    return pl.pallas_call(
        functools.partial(x_kernel, GROUP_X, STAGES),
        out_shape=(part, part, floats(3, *field.shape[1:]), ahead, floats(*cells.shape)),
        in_specs=[SMEM] * 2 + [VMEM] * 8,
        out_specs=(VMEM,) * 5,
        input_output_aliases={9: 4},
        name="x_march",
        **options(8),
    )(direction, shear_x, *halo, field, *shifts, cells)[:4]


def y_march(emitted, field, shifts, shear_y, direction, count_x, kept):
    cells_z = field.shape[-1]
    return pl.pallas_call(
        functools.partial(y_kernel, GROUP_Y, kept, field.shape[1] // count_x),
        out_shape=floats(count_x // (2 * PIECE), 4, 2 * PIECE, cells_z),
        in_specs=[SMEM] * 2 + [VMEM] * 4,
        out_specs=VMEM,
        **options(2.5),
    )(direction, shear_y, emitted, field, *shifts)


def neighbours(axis, offset):
    count = lax.axis_size(axis)
    pairs = [(i, i + 1) for i in range(offset, count - 1, 2)]
    return pairs + [(target, source) for source, target in pairs]


def swapped(axis, mask):
    return [(i, i ^ mask) for i in range(lax.axis_size(axis))]


def stage_kernel(axis, mask, order, split, keep_ref, got_ref, ahead_ref, *out_refs):
    mine_ahead = ahead_ref[order] > 0.5

    def joined(p):
        mine, theirs = [[ref[p, c] for c in range(4)] for ref in (keep_ref, got_ref)]
        seen = jnp.exp2(-jnp.where(mine_ahead, mine[3], theirs[3]))
        near, far = jnp.where(mine_ahead, 1.0, seen), jnp.where(mine_ahead, seen, 1.0)
        return [mine[c] * near + theirs[c] * far for c in range(3)] + [mine[3] + theirs[3]]

    parts = [joined(p) for p in range(keep_ref.shape[0])]
    if split == "image":
        red, green, blue, total = parts[0]
        for c, value in enumerate((red, green, blue, 1.0 - jnp.exp2(-total))):
            for v in range(2):
                out_refs[0][v, c] = value[PIECE * v:PIECE * (v + 1)]
        return
    pick = lambda flag, a, b: [jnp.where(flag, one, two) for one, two in zip(a, b)]
    if split == "pair":
        high = is_set(axis, mask)
        pairs = list(zip(parts[::2], parts[1::2]))
        keep = [pick(high, b, a) for a, b in pairs]
        give = [pick(high, a, b) for a, b in pairs]
    elif split == "ring_first":
        upper = is_set(axis, 2 * mask)
        edge = is_set(axis, mask) == upper
        ends, middle = (parts[0], parts[3]), (parts[1], parts[2])
        small, large = [pick(edge, ends[k], middle[k]) for k in range(2)]
        keep = [pick(upper, large, small), pick(upper, small, large)]
        small, large = [pick(edge, middle[k], ends[k]) for k in range(2)]
        give = [pick(upper, large, small), pick(upper, small, large)]
    else:
        keep, give = parts[:1], parts[1:]
    for ref, pieces in zip(out_refs, (keep, give)):
        for p, piece in enumerate(pieces):
            for c in range(4):
                ref[p, c] = piece[c]


class Exchange:
    def __init__(self, axis, first, ahead):
        self.axis, self.first, self.ahead = axis, first, ahead
        self.stage = 0

    def send(self, keep, give, mask):
        self.keep, self.stage = keep, self.stage + 1
        self.got = lax.ppermute(give, self.axis, swapped(self.axis, mask))

    def meet(self, split, mask=0):
        count, *rest = self.keep.shape
        if split == "image":
            shape = floats(2, 4, PIECE, rest[-1])
        else:
            shape = (floats(count // 2, *rest),) * 2
        return pl.pallas_call(
            functools.partial(stage_kernel, self.axis, mask, self.first + self.stage - 1, split),
            out_shape=shape,
            in_specs=[VMEM] * 3,
            out_specs=VMEM if split == "image" else (VMEM, VMEM),
            **options(0.3),
        )(self.keep, self.got, self.ahead)


def local(density, transfer_table, shear_x, shear_y, direction):
    count_x = density.shape[0]
    step_len = 1.0 / (count_x * lax.axis_size("gx"))
    cells, *faces, index, mask = load(density)
    shifts = (index, mask)
    halo = [lax.ppermute(face, axis, neighbours(axis, offset)) for face, axis, offset in
            zip(faces, ("gx", "gx", "gy", "gy"), (1, 0, 1, 0))]
    field = classify(cells, transfer_table, step_len)
    keep_x, give_x, emitted, ahead = x_march(cells, halo, field, shifts, shear_x, direction)

    x, y = Exchange("gx", 0, ahead), Exchange("gy", len(STAGES[0][1]), ahead)
    x.send(keep_x, give_x, 1)
    given = y_march(emitted, field, shifts, shear_y, direction, count_x, 0)
    kept = y_march(emitted, field, shifts, shear_y, direction, count_x, 1)
    x.send(*x.meet("pair", 2), 2)
    y.send(kept, given, 1)
    x.send(*x.meet("ring_first", 4), 4)
    x.send(*x.meet("ring_second"), 12)
    y.send(*y.meet("ring_first", 2), 2)
    image_x = x.meet("image")
    y.send(*y.meet("ring_second"), 6)
    return image_x, y.meet("image")


def solution(mesh):
    placed = (P("gx", "gy", None), P(), P(None, "gx"), P(None, "gy"), P())
    return jax.shard_map(
        local,
        mesh=mesh,
        in_specs=placed,
        out_specs=(P(None, None, ("gy", "gx"), None), P(None, None, ("gx", "gy"), None)),
        check_vma=False,
    )
```

```python
import functools

import jax
import jax.numpy as jnp
from jax import lax
from jax.experimental import pallas as pl
from jax.experimental.pallas import tpu as pltpu
from jax.sharding import PartitionSpec as P


ROWS = 8
PIECE = 4
LOG2E = 1.4426950408889634
PACK = 1024.0
ROUNDER = 12582912.0
GROUP_X, GROUP_Y = 4, 2
UNROLL_C, UNROLL_E, UNROLL_X, UNROLL_Y = 32, 32, 32, 64

VMEM = pl.BlockSpec(memory_space=pltpu.VMEM)
HBM = pl.BlockSpec(memory_space=pltpu.HBM)
STAGES = (("gx", (1, 2, 4, 8)), ("gy", (1, 2, 4)))


def is_set(axis, mask):
    return (lax.axis_index(axis) & mask) != 0


def slot_of(i, count):
    piece = i // PIECE
    return (piece % 2) * (count // 2) + (piece // 2) * PIECE + i % PIECE


def lane_take(values, index):
    numbers = lax.GatherDimensionNumbers(
        offset_dims=(), collapsed_slice_dims=(1,), start_index_map=(1,),
        operand_batching_dims=(0,), start_indices_batching_dims=(0,))
    return lax.gather(values, index[..., None], numbers, slice_sizes=(1, 1),
                      mode=lax.GatherScatterMode.PROMISE_IN_BOUNDS)


def load_kernel(stages, density_ref, table_ref, shear_x_ref, shear_y_ref, turn_ref, cells_ref,
                face_xa_ref, face_xb_ref, face_ya_ref, face_yb_ref, lut_ref, index_ref, mask_ref,
                turned_ref, ahead_ref, levels_ref, shifts_x_ref, shifts_y_ref, turns_ref, sems):
    count_x, count_y, cells_z = density_ref.shape
    inner = cells_ref.at[pl.ds(1, count_x), pl.ds(ROWS, count_y), :]
    copies = [pltpu.make_async_copy(source, target, sems.at[k]) for k, (source, target) in
              enumerate(((density_ref, inner), (turn_ref, turns_ref), (shear_x_ref, shifts_x_ref),
                         (shear_y_ref, shifts_y_ref), (table_ref, levels_ref)))]
    for copy in copies:
        copy.start()

    lane = lax.broadcasted_iota(jnp.int32, (ROWS, cells_z), 1)
    row = lax.broadcasted_iota(jnp.int32, (ROWS, cells_z), 0)
    copies[1].wait()
    stage = 0
    for family, (axis, masks) in enumerate(stages):
        turned = jnp.where(row < PIECE, turns_ref[family, 0], turns_ref[family, 1])
        for mask in masks:
            ahead_ref[stage] = jnp.where(turned == jnp.where(is_set(axis, mask), 1, 0), 1.0, 0.0)
            stage += 1

    for family, shifts_ref in enumerate((shifts_x_ref, shifts_y_ref)):
        copies[2 + family].wait()
        count = shifts_ref.shape[1]
        for v in range(2):
            turned = turns_ref[family, v]
            turned_ref[2 * family + v] = jnp.full((ROWS, cells_z), turned, jnp.int32)
            sign = jnp.full((ROWS, cells_z), jnp.where(turned != 0, 1.0, -1.0), jnp.float32)
            first = 2 * family * count_x + v * count

            def shifted(i, carry):
                source = lane - shifts_ref[v, i]
                inside = source & (cells_z - 1)
                index_ref[first + i] = inside
                mask_ref[first + i] = jnp.where(inside == source, sign, 0.0)
                return carry

            lax.fori_loop(0, count, shifted, 0, unroll=8)

    copies[4].wait()
    levels = levels_ref[...].astype(jnp.float32)
    for c in range(4):
        level = jnp.broadcast_to(levels[c:c + 1], (ROWS, cells_z))
        rise = jnp.where(lane == cells_z - 1, 0.0, pltpu.roll(level, cells_z - 1, 1) - level)
        lut_ref[c] = level + rise * (1.0 / PACK)
    copies[0].wait()

    odd_x, odd_y = is_set("gx", 1), is_set("gy", 1)
    first, last = cells_ref[1, pl.ds(ROWS, count_y), :], cells_ref[count_x, pl.ds(ROWS, count_y), :]
    face_xa_ref[...] = jnp.where(odd_x, last, first)
    face_xb_ref[...] = jnp.where(odd_x, first, last)
    first, last = (cells_ref[pl.ds(1, count_x), ROWS, :],
                   cells_ref[pl.ds(1, count_x), ROWS + count_y - 1, :])
    face_ya_ref[...] = jnp.where(odd_y, last, first)
    face_yb_ref[...] = jnp.where(odd_y, first, last)


def classify_kernel(step_len, cells_ref, lut_ref, field_ref):
    count_x, cells_z = cells_ref.shape[0] - 2, cells_ref.shape[2]
    count_y = cells_ref.shape[1] - 2 * ROWS
    pitch = field_ref.shape[1] // count_x

    def body(i, carry):
        slot = slot_of(i, count_x) * pitch
        for base in range(0, count_y, ROWS):
            scaled = cells_ref[i + 1, pl.ds(ROWS + base, ROWS), :] * (cells_z - 1.0)
            knot = scaled.astype(jnp.int32)
            part = (scaled - knot.astype(jnp.float32)) * PACK - 1.0
            classed = []
            for c in range(4):
                packed = lane_take(lut_ref[c], knot)
                level = (packed + ROUNDER) - ROUNDER
                classed.append(packed + (packed - level) * part)
            optical = classed[3] * (2.0 * step_len * LOG2E / 255.0)
            opacity = (1.0 - jnp.exp2(-optical)) * (1.0 / 255.0)
            values = [classed[c] * opacity for c in range(3)] + [optical]
            for c in range(4):
                field_ref[c, pl.ds(slot + base, ROWS), :] = values[c]
        return carry

    lax.fori_loop(0, count_x, body, 0, unroll=UNROLL_C)


def march(fields, place, turned, index_ref, mask_ref, states):
    index, mask = index_ref[place], mask_ref[place]
    out = []
    for (red, green, blue, optical), state in zip(fields, states):
        depth = lane_take(optical, index) * mask
        after = state[0] + depth
        seen = jnp.exp2(jnp.where(turned, after, state[0])) * mask
        out.append((after, state[1] + seen * lane_take(red, index),
                    state[2] + seen * lane_take(green, index),
                    state[3] + seen * lane_take(blue, index)))
    return tuple(out)


def settle(turned, state):
    sign = jnp.where(turned, 1.0, -1.0)
    total = state[0] * sign
    fade = jnp.exp2(jnp.where(turned, -total, 0.0)) * sign
    return [state[1] * fade, state[2] * fade, state[3] * fade, total]


def x_kernel(group, face_xa_ref, face_xb_ref, face_ya_ref, face_yb_ref, field_ref, index_ref,
             mask_ref, turned_ref, _, keep_ref, give_ref, emit_ref, cells_ref):
    count_x, cells_z = cells_ref.shape[0] - 2, cells_ref.shape[2]
    count_y = cells_ref.shape[1] - 2 * ROWS
    pitch = field_ref.shape[1] // count_x
    pad = ROWS
    lane = lax.broadcasted_iota(jnp.int32, (ROWS, cells_z), 1)

    odd_x, odd_y = is_set("gx", 1), is_set("gy", 1)
    cells_ref[0, pl.ds(pad, count_y), :] = jnp.where(odd_x, face_xb_ref[...], face_xa_ref[...])
    cells_ref[count_x + 1, pl.ds(pad, count_y), :] = jnp.where(odd_x, face_xa_ref[...],
                                                               face_xb_ref[...])
    low_y = jnp.where(odd_y, face_yb_ref[...], face_ya_ref[...])
    high_y = jnp.where(odd_y, face_ya_ref[...], face_yb_ref[...])
    for i in range(count_x):
        cells_ref[i + 1, pl.ds(pad - 1, 1), :] = low_y[i:i + 1]
        cells_ref[i + 1, pl.ds(pad + count_y, 1), :] = high_y[i:i + 1]

    turned = [turned_ref[v] != 0 for v in range(2)]
    zeros = jnp.zeros((ROWS, cells_z), jnp.float32)
    up, down = (lane + 1) & (cells_z - 1), (lane - 1) & (cells_z - 1)

    def shade(i, base):
        here = cells_ref[i + 1, pl.ds(base + pad, ROWS), :]
        diff_x = (cells_ref[i + 2, pl.ds(base + pad, ROWS), :]
                  - cells_ref[i, pl.ds(base + pad, ROWS), :])
        diff_y = (cells_ref[i + 1, pl.ds(base + pad + 1, ROWS), :]
                  - cells_ref[i + 1, pl.ds(base + pad - 1, ROWS), :])
        above = jnp.where(lane == cells_z - 1, 0.0, lane_take(here, up))
        below = jnp.where(lane == 0, 0.0, lane_take(here, down))
        diff_z = above - below
        side = diff_y + diff_z
        facing = jnp.abs(diff_x + (side + side))
        norm = diff_x * diff_x + diff_y * diff_y + diff_z * diff_z + 0.04
        return 0.3 + (0.7 / 3.0) * facing * lax.rsqrt(norm)

    def emission(i, carry):
        slot = slot_of(i, count_x) * pitch
        for base in range(0, count_y, ROWS):
            shaded = shade(i, base)
            rows = pl.ds(slot + base, ROWS)
            for c in range(3):
                emit_ref[c, rows, :] = field_ref[c, rows, :] * shaded
        return carry

    lax.fori_loop(0, count_x, emission, 0, unroll=UNROLL_E)

    def block_of(block, carry):
        base = pl.multiple_of(block * (ROWS * group), ROWS)

        def body(i, states):
            fields = []
            slot = slot_of(i, count_x) * pitch
            for g in range(group):
                rows = pl.ds(slot + base + g * ROWS, ROWS)
                fields.append((emit_ref[0, rows, :], emit_ref[1, rows, :], emit_ref[2, rows, :],
                               field_ref[3, rows, :]))
            return tuple(march(fields, v * count_x + i, turned[v], index_ref, mask_ref,
                               states[v]) for v in range(2))

        states = lax.fori_loop(0, count_x, body, (((zeros,) * 4,) * group,) * 2, unroll=UNROLL_X)
        for v in range(2):
            for g in range(group):
                for c, value in enumerate(settle(turned[v], states[v][g])):
                    even, odd = value[:PIECE], value[PIECE:]
                    spot, rows = block * group + g, pl.ds(PIECE * v, PIECE)
                    keep_ref[spot, c, rows, :] = jnp.where(odd_x, odd, even)
                    give_ref[spot, c, rows, :] = jnp.where(odd_x, even, odd)
        return carry

    lax.fori_loop(0, count_y // (ROWS * group), block_of, 0)


def y_kernel(group, kept, count_x, count_y, emit_ref, field_ref, index_ref, mask_ref, turned_ref,
             out_ref):
    cells_z = emit_ref.shape[-1]
    pitch = emit_ref.shape[1] // count_x
    size = out_ref.shape[0] * PIECE
    first = jnp.where(is_set("gy", 1) == bool(kept), size, 0)
    turned = [turned_ref[2 + v] != 0 for v in range(2)]
    zeros = jnp.zeros((ROWS, cells_z), jnp.float32)

    def block_of(block, carry):
        def body(j, states):
            fields = []
            for g in range(group):
                start = (first + (block * group + g) * ROWS) * pitch
                rows = pl.ds(start + j, ROWS, stride=pitch)
                fields.append((emit_ref[0, rows, :], emit_ref[1, rows, :], emit_ref[2, rows, :],
                               field_ref[3, rows, :]))
            return tuple(march(fields, 2 * count_x + v * count_y + j, turned[v], index_ref, mask_ref,
                               states[v]) for v in range(2))

        states = lax.fori_loop(0, count_y, body, (((zeros,) * 4,) * group,) * 2, unroll=UNROLL_Y)
        for v in range(2):
            for g in range(group):
                for c, value in enumerate(settle(turned[v], states[v][g])):
                    for half in range(2):
                        out_ref[2 * (block * group + g) + half, c, pl.ds(PIECE * v, PIECE), :] = (
                            value[PIECE * half:PIECE * (half + 1)])
        return carry

    lax.fori_loop(0, size // (ROWS * group), block_of, 0)


def options(micros, limit=16 << 20):
    return dict(
        compiler_params=pltpu.CompilerParams(vmem_limit_bytes=limit),
        cost_estimate=pl.CostEstimate(flops=0, transcendentals=0,
                                      bytes_accessed=int(micros * 3.5e6)))


def floats(*shape):
    return jax.ShapeDtypeStruct(shape, jnp.float32)


def load(density, transfer_table, shear_x, shear_y, direction):
    count_x, count_y, cells_z = density.shape
    places = 2 * (count_x + count_y)
    sources = [pltpu.with_memory_space_constraint(a, pltpu.HBM)
               for a in (density, transfer_table, shear_x, shear_y, direction)]
    return pl.pallas_call(
        functools.partial(load_kernel, STAGES),
        out_shape=(floats(count_x + 2, count_y + 2 * ROWS, cells_z),
                   floats(count_y, cells_z), floats(count_y, cells_z),
                   floats(count_x, cells_z), floats(count_x, cells_z),
                   floats(4, ROWS, cells_z),
                   jax.ShapeDtypeStruct((places, ROWS, cells_z), jnp.int32),
                   floats(places, ROWS, cells_z),
                   jax.ShapeDtypeStruct((4, ROWS, cells_z), jnp.int32),
                   floats(sum(len(masks) for _, masks in STAGES), ROWS, cells_z)),
        in_specs=[HBM] * 5,
        out_specs=(VMEM,) * 10,
        scratch_shapes=[pltpu.VMEM(transfer_table.shape, jnp.int32),
                        pltpu.SMEM(shear_x.shape, jnp.int32), pltpu.SMEM(shear_y.shape, jnp.int32),
                        pltpu.SMEM(direction.shape, jnp.int32), pltpu.SemaphoreType.DMA((5,))],
        name="load",
        **options(2),
    )(*sources)


def classify(cells, lut, step_len):
    count_x, count_y, cells_z = cells.shape[0] - 2, cells.shape[1] - 2 * ROWS, cells.shape[2]
    return pl.pallas_call(
        functools.partial(classify_kernel, step_len),
        out_shape=floats(4, count_x * (count_y + 1), cells_z),
        in_specs=[VMEM, VMEM],
        out_specs=VMEM,
        name="classify",
        **options(3),
    )(cells, lut)


def x_march(cells, halo, field, shifts):
    count_y, cells_z = cells.shape[1] - 2 * ROWS, cells.shape[2]
    part = floats(count_y // (2 * PIECE), 4, 2 * PIECE, cells_z)
    return pl.pallas_call(
        functools.partial(x_kernel, GROUP_X),
        out_shape=(part, part, floats(3, *field.shape[1:]), floats(*cells.shape)),
        in_specs=[VMEM] * 9,
        out_specs=(VMEM,) * 4,
        input_output_aliases={8: 3},
        name="x_march",
        **options(8),
    )(*halo, field, *shifts, cells)[:3]


def y_march(emitted, field, shifts, sizes, kept):
    cells_z = field.shape[-1]
    return pl.pallas_call(
        functools.partial(y_kernel, GROUP_Y, kept, *sizes),
        out_shape=floats(sizes[0] // (2 * PIECE), 4, 2 * PIECE, cells_z),
        in_specs=[VMEM] * 5,
        out_specs=VMEM,
        **options(2.5),
    )(emitted, field, *shifts)


def neighbours(axis, offset):
    count = lax.axis_size(axis)
    pairs = [(i, i + 1) for i in range(offset, count - 1, 2)]
    return pairs + [(target, source) for source, target in pairs]


def swapped(axis, mask):
    return [(i, i ^ mask) for i in range(lax.axis_size(axis))]


def stage_kernel(axis, mask, order, split, keep_ref, got_ref, ahead_ref, *out_refs):
    mine_ahead = ahead_ref[order] > 0.5

    def joined(p):
        mine, theirs = [[ref[p, c] for c in range(4)] for ref in (keep_ref, got_ref)]
        seen = jnp.exp2(-jnp.where(mine_ahead, mine[3], theirs[3]))
        near, far = jnp.where(mine_ahead, 1.0, seen), jnp.where(mine_ahead, seen, 1.0)
        return [mine[c] * near + theirs[c] * far for c in range(3)] + [mine[3] + theirs[3]]

    parts = [joined(p) for p in range(keep_ref.shape[0])]
    if split == "image":
        red, green, blue, total = parts[0]
        for c, value in enumerate((red, green, blue, 1.0 - jnp.exp2(-total))):
            for v in range(2):
                out_refs[0][v, c] = value[PIECE * v:PIECE * (v + 1)]
        return
    pick = lambda flag, a, b: [jnp.where(flag, one, two) for one, two in zip(a, b)]
    if split == "pair":
        high = is_set(axis, mask)
        pairs = list(zip(parts[::2], parts[1::2]))
        keep = [pick(high, b, a) for a, b in pairs]
        give = [pick(high, a, b) for a, b in pairs]
    elif split == "ring_first":
        upper = is_set(axis, 2 * mask)
        edge = is_set(axis, mask) == upper
        ends, middle = (parts[0], parts[3]), (parts[1], parts[2])
        small, large = [pick(edge, ends[k], middle[k]) for k in range(2)]
        keep = [pick(upper, large, small), pick(upper, small, large)]
        small, large = [pick(edge, middle[k], ends[k]) for k in range(2)]
        give = [pick(upper, large, small), pick(upper, small, large)]
    else:
        keep, give = parts[:1], parts[1:]
    for ref, pieces in zip(out_refs, (keep, give)):
        for p, piece in enumerate(pieces):
            for c in range(4):
                ref[p, c] = piece[c]


class Exchange:
    def __init__(self, axis, first, ahead):
        self.axis, self.first, self.ahead = axis, first, ahead
        self.stage = 0

    def send(self, keep, give, mask):
        self.keep, self.stage = keep, self.stage + 1
        self.got = lax.ppermute(give, self.axis, swapped(self.axis, mask))

    def meet(self, split, mask=0):
        count, *rest = self.keep.shape
        if split == "image":
            shape = floats(2, 4, PIECE, rest[-1])
        else:
            shape = (floats(count // 2, *rest),) * 2
        return pl.pallas_call(
            functools.partial(stage_kernel, self.axis, mask, self.first + self.stage - 1, split),
            out_shape=shape,
            in_specs=[VMEM] * 3,
            out_specs=VMEM if split == "image" else (VMEM, VMEM),
            **options(0.3),
        )(self.keep, self.got, self.ahead)


def local(density, transfer_table, shear_x, shear_y, direction):
    count_x = density.shape[0]
    step_len = 1.0 / (count_x * lax.axis_size("gx"))
    cells, xa, xb, ya, yb, lut, *shifts, ahead = load(density, transfer_table, shear_x, shear_y,
                                                      direction)
    halo = [lax.ppermute(face, axis, neighbours(axis, offset)) for face, axis, offset in
            zip((xa, xb, ya, yb), ("gx", "gx", "gy", "gy"), (1, 0, 1, 0))]
    field = classify(cells, lut, step_len)
    keep_x, give_x, emitted = x_march(cells, halo, field, shifts)

    x, y = Exchange("gx", 0, ahead), Exchange("gy", len(STAGES[0][1]), ahead)
    x.send(keep_x, give_x, 1)
    given = y_march(emitted, field, shifts, density.shape[:2], 0)
    kept = y_march(emitted, field, shifts, density.shape[:2], 1)
    x.send(*x.meet("pair", 2), 2)
    y.send(kept, given, 1)
    x.send(*x.meet("ring_first", 4), 4)
    x.send(*x.meet("ring_second"), 12)
    y.send(*y.meet("ring_first", 2), 2)
    image_x = x.meet("image")
    y.send(*y.meet("ring_second"), 6)
    return image_x, y.meet("image")


def solution(mesh):
    placed = (P("gx", "gy", None), P(), P(None, "gx"), P(None, "gy"), P())
    return jax.shard_map(
        local,
        mesh=mesh,
        in_specs=placed,
        out_specs=(P(None, None, ("gy", "gx"), None), P(None, None, ("gx", "gy"), None)),
        check_vma=False,
    )
```

```python
import functools

import jax
import jax.numpy as jnp
from jax import lax
from jax.experimental import pallas as pl
from jax.experimental.pallas import tpu as pltpu
from jax.sharding import PartitionSpec as P


ROWS = 8
PIECE = 4
LOG2E = 1.4426950408889634
PACK = 1024.0
ROUNDER = 12582912.0
GROUP_X, GROUP_Y = 4, 2
UNROLL_C, UNROLL_E, UNROLL_X, UNROLL_Y = 16, 32, 32, 64

VMEM = pl.BlockSpec(memory_space=pltpu.VMEM)
HBM = pl.BlockSpec(memory_space=pltpu.HBM)
STAGES = (("gx", (1, 2, 4, 8)), ("gy", (1, 2, 4)))


def is_set(axis, mask):
    return (lax.axis_index(axis) & mask) != 0


def slot_of(i, count):
    piece = i // PIECE
    return (piece % 2) * (count // 2) + (piece // 2) * PIECE + i % PIECE


def lane_take(values, index):
    numbers = lax.GatherDimensionNumbers(
        offset_dims=(), collapsed_slice_dims=(1,), start_index_map=(1,),
        operand_batching_dims=(0,), start_indices_batching_dims=(0,))
    return lax.gather(values, index[..., None], numbers, slice_sizes=(1, 1),
                      mode=lax.GatherScatterMode.PROMISE_IN_BOUNDS)


def load_kernel(stages, density_ref, table_ref, shear_x_ref, shear_y_ref, turn_ref, cells_ref,
                face_xa_ref, share_ref, own_ref, lut_ref, index_ref, mask_ref, turned_ref,
                ahead_ref, levels_ref, shifts_x_ref, shifts_y_ref, turns_ref, sems):
    count_x, count_y, cells_z = density_ref.shape
    inner = cells_ref.at[pl.ds(1, count_x), pl.ds(ROWS, count_y), :]
    copies = [pltpu.make_async_copy(source, target, sems.at[k]) for k, (source, target) in
              enumerate(((density_ref, inner), (turn_ref, turns_ref), (shear_x_ref, shifts_x_ref),
                         (shear_y_ref, shifts_y_ref), (table_ref, levels_ref)))]
    for copy in copies:
        copy.start()

    lane = lax.broadcasted_iota(jnp.int32, (ROWS, cells_z), 1)
    row = lax.broadcasted_iota(jnp.int32, (ROWS, cells_z), 0)
    copies[1].wait()
    stage = 0
    for family, (axis, masks) in enumerate(stages):
        turned = jnp.where(row < PIECE, turns_ref[family, 0], turns_ref[family, 1])
        for mask in masks:
            ahead_ref[stage] = jnp.where(turned == jnp.where(is_set(axis, mask), 1, 0), 1.0, 0.0)
            stage += 1

    for family, shifts_ref in enumerate((shifts_x_ref, shifts_y_ref)):
        copies[2 + family].wait()
        count = shifts_ref.shape[1]
        for v in range(2):
            turned = turns_ref[family, v]
            turned_ref[2 * family + v] = jnp.full((ROWS, cells_z), turned, jnp.int32)
            sign = jnp.full((ROWS, cells_z), jnp.where(turned != 0, 1.0, -1.0), jnp.float32)
            first = 2 * family * count_x + v * count

            def shifted(i, carry):
                source = lane - shifts_ref[v, i]
                inside = source & (cells_z - 1)
                index_ref[first + i] = inside
                mask_ref[first + i] = jnp.where(inside == source, sign, 0.0)
                return carry

            lax.fori_loop(0, count, shifted, 0, unroll=8)

    copies[4].wait()
    levels = levels_ref[...].astype(jnp.float32)
    for c in range(4):
        level = jnp.broadcast_to(levels[c:c + 1], (ROWS, cells_z))
        rise = jnp.where(lane == cells_z - 1, 0.0, pltpu.roll(level, cells_z - 1, 1) - level)
        lut_ref[c] = level + rise * (1.0 / PACK)
    copies[0].wait()

    odd_x, odd_y = is_set("gx", 1), is_set("gy", 1)
    first, last = cells_ref[1, pl.ds(ROWS, count_y), :], cells_ref[count_x, pl.ds(ROWS, count_y), :]
    face_xa_ref[...] = jnp.where(odd_x, last, first)
    share_ref[pl.ds(0, count_y), :] = jnp.where(odd_x, first, last)
    first, last = (cells_ref[pl.ds(1, count_x), ROWS, :],
                   cells_ref[pl.ds(1, count_x), ROWS + count_y - 1, :])
    outward = odd_x == odd_y
    share_ref[pl.ds(count_y, count_x), :] = jnp.where(outward, first, last)
    own_ref[...] = jnp.where(outward, last, first)


def relay_kernel(own_ref, shared_ref, out_ref):
    rows = own_ref.shape[0]
    out_ref[pl.ds(0, rows), :] = own_ref[...]
    out_ref[pl.ds(rows, rows), :] = shared_ref[pl.ds(shared_ref.shape[0] - rows, rows), :]


def classify_kernel(step_len, parity, cells_ref, lut_ref, *refs):
    field_ref = refs[-1]
    count_x, cells_z = cells_ref.shape[0] - 2, cells_ref.shape[2]
    count_y = cells_ref.shape[1] - 2 * ROWS
    pitch = field_ref.shape[1] // count_x

    def body(t, carry):
        i = (t // PIECE * 2 + parity) * PIECE + t % PIECE
        slot = (t + parity * (count_x // 2)) * pitch
        for base in range(0, count_y, ROWS):
            scaled = cells_ref[i + 1, pl.ds(ROWS + base, ROWS), :] * (cells_z - 1.0)
            knot = scaled.astype(jnp.int32)
            part = (scaled - knot.astype(jnp.float32)) * PACK - 1.0
            classed = []
            for c in range(4):
                packed = lane_take(lut_ref[c], knot)
                level = (packed + ROUNDER) - ROUNDER
                classed.append(packed + (packed - level) * part)
            optical = classed[3] * (2.0 * step_len * LOG2E / 255.0)
            opacity = (1.0 - jnp.exp2(-optical)) * (1.0 / 255.0)
            values = [classed[c] * opacity for c in range(3)] + [optical]
            for c in range(4):
                field_ref[c, pl.ds(slot + base, ROWS), :] = values[c]
        return carry

    lax.fori_loop(0, count_x // 2, body, 0, unroll=UNROLL_C)


def march(fields, place, turned, index_ref, mask_ref, states):
    index, mask = index_ref[place], mask_ref[place]
    out = []
    for (red, green, blue, optical), state in zip(fields, states):
        depth = lane_take(optical, index) * mask
        after = state[0] + depth
        seen = jnp.exp2(jnp.where(turned, after, state[0])) * mask
        out.append((after, state[1] + seen * lane_take(red, index),
                    state[2] + seen * lane_take(green, index),
                    state[3] + seen * lane_take(blue, index)))
    return tuple(out)


def settle(turned, state):
    sign = jnp.where(turned, 1.0, -1.0)
    total = state[0] * sign
    fade = jnp.exp2(jnp.where(turned, -total, 0.0)) * sign
    return [state[1] * fade, state[2] * fade, state[3] * fade, total]


def x_kernel(group, face_xa_ref, shared_ref, crossed_ref, returned_ref, field_ref, index_ref,
             mask_ref, turned_ref, _, keep_ref, give_ref, emit_ref, cells_ref):
    count_x, cells_z = cells_ref.shape[0] - 2, cells_ref.shape[2]
    count_y = cells_ref.shape[1] - 2 * ROWS
    pitch = field_ref.shape[1] // count_x
    pad = ROWS
    lane = lax.broadcasted_iota(jnp.int32, (ROWS, cells_z), 1)

    odd_x, odd_y = is_set("gx", 1), is_set("gy", 1)
    near, far = face_xa_ref[...], shared_ref[pl.ds(0, count_y), :]
    cells_ref[0, pl.ds(pad, count_y), :] = jnp.where(odd_x, far, near)
    cells_ref[count_x + 1, pl.ds(pad, count_y), :] = jnp.where(odd_x, near, far)
    own, other = crossed_ref[pl.ds(0, count_x), :], returned_ref[pl.ds(count_x, count_x), :]
    outward = odd_x == odd_y
    low_y, high_y = jnp.where(outward, other, own), jnp.where(outward, own, other)
    for i in range(count_x):
        cells_ref[i + 1, pl.ds(pad - 1, 1), :] = low_y[i:i + 1]
        cells_ref[i + 1, pl.ds(pad + count_y, 1), :] = high_y[i:i + 1]

    turned = [turned_ref[v] != 0 for v in range(2)]
    zeros = jnp.zeros((ROWS, cells_z), jnp.float32)
    up, down = (lane + 1) & (cells_z - 1), (lane - 1) & (cells_z - 1)

    def shade(i, base):
        here = cells_ref[i + 1, pl.ds(base + pad, ROWS), :]
        diff_x = (cells_ref[i + 2, pl.ds(base + pad, ROWS), :]
                  - cells_ref[i, pl.ds(base + pad, ROWS), :])
        diff_y = (cells_ref[i + 1, pl.ds(base + pad + 1, ROWS), :]
                  - cells_ref[i + 1, pl.ds(base + pad - 1, ROWS), :])
        above = jnp.where(lane == cells_z - 1, 0.0, lane_take(here, up))
        below = jnp.where(lane == 0, 0.0, lane_take(here, down))
        diff_z = above - below
        side = diff_y + diff_z
        facing = jnp.abs(diff_x + (side + side))
        norm = diff_x * diff_x + diff_y * diff_y + diff_z * diff_z + 0.04
        return 0.3 + (0.7 / 3.0) * facing * lax.rsqrt(norm)

    def emission(i, carry):
        slot = slot_of(i, count_x) * pitch
        for base in range(0, count_y, ROWS):
            shaded = shade(i, base)
            rows = pl.ds(slot + base, ROWS)
            for c in range(3):
                emit_ref[c, rows, :] = field_ref[c, rows, :] * shaded
        return carry

    lax.fori_loop(0, count_x, emission, 0, unroll=UNROLL_E)

    def block_of(block, carry):
        base = pl.multiple_of(block * (ROWS * group), ROWS)

        def body(i, states):
            fields = []
            slot = slot_of(i, count_x) * pitch
            for g in range(group):
                rows = pl.ds(slot + base + g * ROWS, ROWS)
                fields.append((emit_ref[0, rows, :], emit_ref[1, rows, :], emit_ref[2, rows, :],
                               field_ref[3, rows, :]))
            return tuple(march(fields, v * count_x + i, turned[v], index_ref, mask_ref,
                               states[v]) for v in range(2))

        states = lax.fori_loop(0, count_x, body, (((zeros,) * 4,) * group,) * 2, unroll=UNROLL_X)
        for v in range(2):
            for g in range(group):
                for c, value in enumerate(settle(turned[v], states[v][g])):
                    even, odd = value[:PIECE], value[PIECE:]
                    spot, rows = block * group + g, pl.ds(PIECE * v, PIECE)
                    keep_ref[spot, c, rows, :] = jnp.where(odd_x, odd, even)
                    give_ref[spot, c, rows, :] = jnp.where(odd_x, even, odd)
        return carry

    lax.fori_loop(0, count_y // (ROWS * group), block_of, 0)


def y_kernel(group, kept, count_x, count_y, emit_ref, field_ref, index_ref, mask_ref, turned_ref,
             out_ref):
    cells_z = emit_ref.shape[-1]
    pitch = emit_ref.shape[1] // count_x
    size = out_ref.shape[0] * PIECE
    first = jnp.where(is_set("gy", 1) == bool(kept), size, 0)
    turned = [turned_ref[2 + v] != 0 for v in range(2)]
    zeros = jnp.zeros((ROWS, cells_z), jnp.float32)

    def block_of(block, carry):
        def body(j, states):
            fields = []
            for g in range(group):
                start = (first + (block * group + g) * ROWS) * pitch
                rows = pl.ds(start + j, ROWS, stride=pitch)
                fields.append((emit_ref[0, rows, :], emit_ref[1, rows, :], emit_ref[2, rows, :],
                               field_ref[3, rows, :]))
            return tuple(march(fields, 2 * count_x + v * count_y + j, turned[v], index_ref, mask_ref,
                               states[v]) for v in range(2))

        states = lax.fori_loop(0, count_y, body, (((zeros,) * 4,) * group,) * 2, unroll=UNROLL_Y)
        for v in range(2):
            for g in range(group):
                for c, value in enumerate(settle(turned[v], states[v][g])):
                    for half in range(2):
                        out_ref[2 * (block * group + g) + half, c, pl.ds(PIECE * v, PIECE), :] = (
                            value[PIECE * half:PIECE * (half + 1)])
        return carry

    lax.fori_loop(0, size // (ROWS * group), block_of, 0)


def options(micros, limit=16 << 20):
    return dict(
        compiler_params=pltpu.CompilerParams(vmem_limit_bytes=limit),
        cost_estimate=pl.CostEstimate(flops=0, transcendentals=0,
                                      bytes_accessed=int(micros * 3.5e6)))


def floats(*shape):
    return jax.ShapeDtypeStruct(shape, jnp.float32)


def load(density, transfer_table, shear_x, shear_y, direction):
    count_x, count_y, cells_z = density.shape
    places = 2 * (count_x + count_y)
    sources = [pltpu.with_memory_space_constraint(a, pltpu.HBM)
               for a in (density, transfer_table, shear_x, shear_y, direction)]
    return pl.pallas_call(
        functools.partial(load_kernel, STAGES),
        out_shape=(floats(count_x + 2, count_y + 2 * ROWS, cells_z),
                   floats(count_y, cells_z), floats(count_y + count_x, cells_z),
                   floats(count_x, cells_z),
                   floats(4, ROWS, cells_z),
                   jax.ShapeDtypeStruct((places, ROWS, cells_z), jnp.int32),
                   floats(places, ROWS, cells_z),
                   jax.ShapeDtypeStruct((4, ROWS, cells_z), jnp.int32),
                   floats(sum(len(masks) for _, masks in STAGES), ROWS, cells_z)),
        in_specs=[HBM] * 5,
        out_specs=(VMEM,) * 9,
        scratch_shapes=[pltpu.VMEM(transfer_table.shape, jnp.int32),
                        pltpu.SMEM(shear_x.shape, jnp.int32), pltpu.SMEM(shear_y.shape, jnp.int32),
                        pltpu.SMEM(direction.shape, jnp.int32), pltpu.SemaphoreType.DMA((5,))],
        name="load",
        **options(2),
    )(*sources)


def relay(own, shared):
    return pl.pallas_call(
        relay_kernel,
        out_shape=floats(2 * own.shape[0], own.shape[1]),
        in_specs=[VMEM, VMEM],
        out_specs=VMEM,
        name="relay",
        **options(0.3),
    )(own, shared)


def classify(cells, lut, step_len, part, *before):
    count_x, count_y, cells_z = cells.shape[0] - 2, cells.shape[1] - 2 * ROWS, cells.shape[2]
    return pl.pallas_call(
        functools.partial(classify_kernel, step_len, part),
        out_shape=floats(4, count_x * (count_y + 1), cells_z),
        in_specs=[VMEM] * (2 + len(before)),
        out_specs=VMEM,
        input_output_aliases={2: 0} if before else {},
        **options(1.5),
    )(cells, lut, *before)


def x_march(cells, halo, field, shifts):
    count_y, cells_z = cells.shape[1] - 2 * ROWS, cells.shape[2]
    part = floats(count_y // (2 * PIECE), 4, 2 * PIECE, cells_z)
    return pl.pallas_call(
        functools.partial(x_kernel, GROUP_X),
        out_shape=(part, part, floats(3, *field.shape[1:]), floats(*cells.shape)),
        in_specs=[VMEM] * 9,
        out_specs=(VMEM,) * 4,
        input_output_aliases={8: 3},
        name="x_march",
        **options(8),
    )(*halo, field, *shifts, cells)[:3]


def y_march(emitted, field, shifts, sizes, kept):
    cells_z = field.shape[-1]
    return pl.pallas_call(
        functools.partial(y_kernel, GROUP_Y, kept, *sizes),
        out_shape=floats(sizes[0] // (2 * PIECE), 4, 2 * PIECE, cells_z),
        in_specs=[VMEM] * 5,
        out_specs=VMEM,
        **options(2.5),
    )(emitted, field, *shifts)


def neighbours(axis, offset):
    count = lax.axis_size(axis)
    pairs = [(i, i + 1) for i in range(offset, count - 1, 2)]
    return pairs + [(target, source) for source, target in pairs]


def crossings():
    count = lax.axis_size("gy")
    return [(i * count + source, i * count + target) for i in range(lax.axis_size("gx"))
            for source, target in neighbours("gy", i % 2)]


def swapped(axis, mask):
    return [(i, i ^ mask) for i in range(lax.axis_size(axis))]


def stage_kernel(axis, mask, order, split, keep_ref, got_ref, ahead_ref, *out_refs):
    mine_ahead = ahead_ref[order] > 0.5

    def joined(p):
        mine, theirs = [[ref[p, c] for c in range(4)] for ref in (keep_ref, got_ref)]
        seen = jnp.exp2(-jnp.where(mine_ahead, mine[3], theirs[3]))
        near, far = jnp.where(mine_ahead, 1.0, seen), jnp.where(mine_ahead, seen, 1.0)
        return [mine[c] * near + theirs[c] * far for c in range(3)] + [mine[3] + theirs[3]]

    parts = [joined(p) for p in range(keep_ref.shape[0])]
    if split == "image":
        red, green, blue, total = parts[0]
        for c, value in enumerate((red, green, blue, 1.0 - jnp.exp2(-total))):
            for v in range(2):
                out_refs[0][v, c] = value[PIECE * v:PIECE * (v + 1)]
        return
    pick = lambda flag, a, b: [jnp.where(flag, one, two) for one, two in zip(a, b)]
    if split == "pair":
        high = is_set(axis, mask)
        pairs = list(zip(parts[::2], parts[1::2]))
        keep = [pick(high, b, a) for a, b in pairs]
        give = [pick(high, a, b) for a, b in pairs]
    elif split == "ring_first":
        upper = is_set(axis, 2 * mask)
        edge = is_set(axis, mask) == upper
        ends, middle = (parts[0], parts[3]), (parts[1], parts[2])
        small, large = [pick(edge, ends[k], middle[k]) for k in range(2)]
        keep = [pick(upper, large, small), pick(upper, small, large)]
        small, large = [pick(edge, middle[k], ends[k]) for k in range(2)]
        give = [pick(upper, large, small), pick(upper, small, large)]
    else:
        keep, give = parts[:1], parts[1:]
    for ref, pieces in zip(out_refs, (keep, give)):
        for p, piece in enumerate(pieces):
            for c in range(4):
                ref[p, c] = piece[c]


class Exchange:
    def __init__(self, axis, first, ahead):
        self.axis, self.first, self.ahead = axis, first, ahead
        self.stage = 0

    def send(self, keep, give, mask):
        self.keep, self.stage = keep, self.stage + 1
        self.got = lax.ppermute(give, self.axis, swapped(self.axis, mask))

    def meet(self, split, mask=0):
        count, *rest = self.keep.shape
        if split == "image":
            shape = floats(2, 4, PIECE, rest[-1])
        else:
            shape = (floats(count // 2, *rest),) * 2
        return pl.pallas_call(
            functools.partial(stage_kernel, self.axis, mask, self.first + self.stage - 1, split),
            out_shape=shape,
            in_specs=[VMEM] * 3,
            out_specs=VMEM if split == "image" else (VMEM, VMEM),
            **options(0.3),
        )(self.keep, self.got, self.ahead)


def local(density, transfer_table, shear_x, shear_y, direction):
    count_x = density.shape[0]
    step_len = 1.0 / (count_x * lax.axis_size("gx"))
    cells, face, share, own, lut, *shifts, ahead = load(density, transfer_table, shear_x, shear_y,
                                                        direction)
    shared = lax.ppermute(share, "gx", swapped("gx", 1))
    faced = lax.ppermute(face, "gx", neighbours("gx", 1))
    crossed = lax.ppermute(relay(own, shared), ("gx", "gy"), crossings())
    returned = lax.ppermute(crossed, "gx", swapped("gx", 1))
    field = classify(cells, lut, step_len, 0)
    field = classify(cells, lut, step_len, 1, field)
    halo = (faced, shared, crossed, returned)
    keep_x, give_x, emitted = x_march(cells, halo, field, shifts)

    x, y = Exchange("gx", 0, ahead), Exchange("gy", len(STAGES[0][1]), ahead)
    x.send(keep_x, give_x, 1)
    given = y_march(emitted, field, shifts, density.shape[:2], 0)
    kept = y_march(emitted, field, shifts, density.shape[:2], 1)
    x.send(*x.meet("pair", 2), 2)
    y.send(kept, given, 1)
    x.send(*x.meet("ring_first", 4), 4)
    x.send(*x.meet("ring_second"), 12)
    y.send(*y.meet("ring_first", 2), 2)
    image_x = x.meet("image")
    y.send(*y.meet("ring_second"), 6)
    return image_x, y.meet("image")


def solution(mesh):
    placed = (P("gx", "gy", None), P(), P(None, "gx"), P(None, "gy"), P())
    return jax.shard_map(
        local,
        mesh=mesh,
        in_specs=placed,
        out_specs=(P(None, None, ("gy", "gx"), None), P(None, None, ("gx", "gy"), None)),
        check_vma=False,
    )
```

```python
import functools

import jax
import jax.numpy as jnp
from jax import lax
from jax.experimental import pallas as pl
from jax.experimental.pallas import tpu as pltpu
from jax.sharding import PartitionSpec as P


ROWS = 8
PIECE = 4
LOG2E = 1.4426950408889634
PACK = 1024.0
ROUNDER = 12582912.0
GROUP_X, GROUP_Y = 4, 2
UNROLL_C, UNROLL_E, UNROLL_X, UNROLL_Y = 16, 32, 32, 64

VMEM = pl.BlockSpec(memory_space=pltpu.VMEM)
HBM = pl.BlockSpec(memory_space=pltpu.HBM)
STAGES = (("gx", (1, 2, 4, 8)), ("gy", (1, 2, 4)))


def is_set(axis, mask):
    return (lax.axis_index(axis) & mask) != 0


def slot_of(i, count):
    piece = i // PIECE
    return (piece % 2) * (count // 2) + (piece // 2) * PIECE + i % PIECE


def lane_take(values, index):
    numbers = lax.GatherDimensionNumbers(
        offset_dims=(), collapsed_slice_dims=(1,), start_index_map=(1,),
        operand_batching_dims=(0,), start_indices_batching_dims=(0,))
    return lax.gather(values, index[..., None], numbers, slice_sizes=(1, 1),
                      mode=lax.GatherScatterMode.PROMISE_IN_BOUNDS)


def load_kernel(stages, density_ref, table_ref, shear_x_ref, shear_y_ref, turn_ref, cells_ref,
                face_xa_ref, face_xb_ref, hop_ref, own_ref, lut_ref, index_ref, mask_ref, turned_ref,
                ahead_ref, levels_ref, shifts_x_ref, shifts_y_ref, turns_ref, sems):
    count_x, count_y, cells_z = density_ref.shape
    inner = cells_ref.at[pl.ds(1, count_x), pl.ds(ROWS, count_y), :]
    copies = [pltpu.make_async_copy(source, target, sems.at[k]) for k, (source, target) in
              enumerate(((density_ref, inner), (turn_ref, turns_ref), (shear_x_ref, shifts_x_ref),
                         (shear_y_ref, shifts_y_ref), (table_ref, levels_ref)))]
    for copy in copies:
        copy.start()

    lane = lax.broadcasted_iota(jnp.int32, (ROWS, cells_z), 1)
    row = lax.broadcasted_iota(jnp.int32, (ROWS, cells_z), 0)
    copies[1].wait()
    stage = 0
    for family, (axis, masks) in enumerate(stages):
        turned = jnp.where(row < PIECE, turns_ref[family, 0], turns_ref[family, 1])
        for mask in masks:
            ahead_ref[stage] = jnp.where(turned == jnp.where(is_set(axis, mask), 1, 0), 1.0, 0.0)
            stage += 1

    for family, shifts_ref in enumerate((shifts_x_ref, shifts_y_ref)):
        copies[2 + family].wait()
        count = shifts_ref.shape[1]
        for v in range(2):
            turned = turns_ref[family, v]
            turned_ref[2 * family + v] = jnp.full((ROWS, cells_z), turned, jnp.int32)
            sign = jnp.full((ROWS, cells_z), jnp.where(turned != 0, 1.0, -1.0), jnp.float32)
            first = 2 * family * count_x + v * count

            def shifted(i, carry):
                source = lane - shifts_ref[v, i]
                inside = source & (cells_z - 1)
                index_ref[first + i] = inside
                mask_ref[first + i] = jnp.where(inside == source, sign, 0.0)
                return carry

            lax.fori_loop(0, count, shifted, 0, unroll=8)

    copies[4].wait()
    levels = levels_ref[...].astype(jnp.float32)
    for c in range(4):
        level = jnp.broadcast_to(levels[c:c + 1], (ROWS, cells_z))
        rise = jnp.where(lane == cells_z - 1, 0.0, pltpu.roll(level, cells_z - 1, 1) - level)
        lut_ref[c] = level + rise * (1.0 / PACK)
    copies[0].wait()

    odd_x, odd_y = is_set("gx", 1), is_set("gy", 1)
    first, last = cells_ref[1, pl.ds(ROWS, count_y), :], cells_ref[count_x, pl.ds(ROWS, count_y), :]
    face_xa_ref[...] = jnp.where(odd_x, last, first)
    face_xb_ref[...] = jnp.where(odd_x, first, last)
    first, last = (cells_ref[pl.ds(1, count_x), ROWS, :],
                   cells_ref[pl.ds(1, count_x), ROWS + count_y - 1, :])
    hop_ref[...] = jnp.where(odd_y, last, first)
    own_ref[...] = jnp.where(odd_y, first, last)


def relay_kernel(own_ref, hopped_ref, out_ref):
    rows = own_ref.shape[0]
    out_ref[pl.ds(0, rows), :] = own_ref[...]
    out_ref[pl.ds(rows, rows), :] = hopped_ref[...]


def classify_kernel(step_len, parity, cells_ref, lut_ref, *refs):
    field_ref = refs[-1]
    count_x, cells_z = cells_ref.shape[0] - 2, cells_ref.shape[2]
    count_y = cells_ref.shape[1] - 2 * ROWS
    pitch = field_ref.shape[1] // count_x

    def body(t, carry):
        i = (t // PIECE * 2 + parity) * PIECE + t % PIECE
        slot = (t + parity * (count_x // 2)) * pitch
        for base in range(0, count_y, ROWS):
            scaled = cells_ref[i + 1, pl.ds(ROWS + base, ROWS), :] * (cells_z - 1.0)
            knot = scaled.astype(jnp.int32)
            part = (scaled - knot.astype(jnp.float32)) * PACK - 1.0
            classed = []
            for c in range(4):
                packed = lane_take(lut_ref[c], knot)
                level = (packed + ROUNDER) - ROUNDER
                classed.append(packed + (packed - level) * part)
            optical = classed[3] * (2.0 * step_len * LOG2E / 255.0)
            opacity = (1.0 - jnp.exp2(-optical)) * (1.0 / 255.0)
            values = [classed[c] * opacity for c in range(3)] + [optical]
            for c in range(4):
                field_ref[c, pl.ds(slot + base, ROWS), :] = values[c]
        return carry

    lax.fori_loop(0, count_x // 2, body, 0, unroll=UNROLL_C)


def march(fields, place, turned, index_ref, mask_ref, states):
    index, mask = index_ref[place], mask_ref[place]
    out = []
    for (red, green, blue, optical), state in zip(fields, states):
        depth = lane_take(optical, index) * mask
        after = state[0] + depth
        seen = jnp.exp2(jnp.where(turned, after, state[0])) * mask
        out.append((after, state[1] + seen * lane_take(red, index),
                    state[2] + seen * lane_take(green, index),
                    state[3] + seen * lane_take(blue, index)))
    return tuple(out)


def settle(turned, state):
    sign = jnp.where(turned, 1.0, -1.0)
    total = state[0] * sign
    fade = jnp.exp2(jnp.where(turned, -total, 0.0)) * sign
    return [state[1] * fade, state[2] * fade, state[3] * fade, total]


def x_kernel(group, face_xa_ref, face_xb_ref, crossed_ref, field_ref, index_ref,
             mask_ref, turned_ref, _, keep_ref, give_ref, emit_ref, cells_ref):
    count_x, cells_z = cells_ref.shape[0] - 2, cells_ref.shape[2]
    count_y = cells_ref.shape[1] - 2 * ROWS
    pitch = field_ref.shape[1] // count_x
    pad = ROWS
    lane = lax.broadcasted_iota(jnp.int32, (ROWS, cells_z), 1)

    odd_x, odd_y = is_set("gx", 1), is_set("gy", 1)
    near, far = face_xa_ref[...], face_xb_ref[...]
    cells_ref[0, pl.ds(pad, count_y), :] = jnp.where(odd_x, far, near)
    cells_ref[count_x + 1, pl.ds(pad, count_y), :] = jnp.where(odd_x, near, far)
    near, far = crossed_ref[pl.ds(0, count_x), :], crossed_ref[pl.ds(count_x, count_x), :]
    low_y, high_y = jnp.where(odd_y, near, far), jnp.where(odd_y, far, near)
    for i in range(count_x):
        cells_ref[i + 1, pl.ds(pad - 1, 1), :] = low_y[i:i + 1]
        cells_ref[i + 1, pl.ds(pad + count_y, 1), :] = high_y[i:i + 1]

    turned = [turned_ref[v] != 0 for v in range(2)]
    zeros = jnp.zeros((ROWS, cells_z), jnp.float32)
    up, down = (lane + 1) & (cells_z - 1), (lane - 1) & (cells_z - 1)

    def shade(i, base):
        here = cells_ref[i + 1, pl.ds(base + pad, ROWS), :]
        diff_x = (cells_ref[i + 2, pl.ds(base + pad, ROWS), :]
                  - cells_ref[i, pl.ds(base + pad, ROWS), :])
        diff_y = (cells_ref[i + 1, pl.ds(base + pad + 1, ROWS), :]
                  - cells_ref[i + 1, pl.ds(base + pad - 1, ROWS), :])
        above = jnp.where(lane == cells_z - 1, 0.0, lane_take(here, up))
        below = jnp.where(lane == 0, 0.0, lane_take(here, down))
        diff_z = above - below
        side = diff_y + diff_z
        facing = jnp.abs(diff_x + (side + side))
        norm = diff_x * diff_x + diff_y * diff_y + diff_z * diff_z + 0.04
        return 0.3 + (0.7 / 3.0) * facing * lax.rsqrt(norm)

    def emission(i, carry):
        slot = slot_of(i, count_x) * pitch
        for base in range(0, count_y, ROWS):
            shaded = shade(i, base)
            rows = pl.ds(slot + base, ROWS)
            for c in range(3):
                emit_ref[c, rows, :] = field_ref[c, rows, :] * shaded
        return carry

    lax.fori_loop(0, count_x, emission, 0, unroll=UNROLL_E)

    def block_of(block, carry):
        base = pl.multiple_of(block * (ROWS * group), ROWS)

        def body(i, states):
            fields = []
            slot = slot_of(i, count_x) * pitch
            for g in range(group):
                rows = pl.ds(slot + base + g * ROWS, ROWS)
                fields.append((emit_ref[0, rows, :], emit_ref[1, rows, :], emit_ref[2, rows, :],
                               field_ref[3, rows, :]))
            return tuple(march(fields, v * count_x + i, turned[v], index_ref, mask_ref,
                               states[v]) for v in range(2))

        states = lax.fori_loop(0, count_x, body, (((zeros,) * 4,) * group,) * 2, unroll=UNROLL_X)
        for v in range(2):
            for g in range(group):
                for c, value in enumerate(settle(turned[v], states[v][g])):
                    even, odd = value[:PIECE], value[PIECE:]
                    spot, rows = block * group + g, pl.ds(PIECE * v, PIECE)
                    keep_ref[spot, c, rows, :] = jnp.where(odd_x, odd, even)
                    give_ref[spot, c, rows, :] = jnp.where(odd_x, even, odd)
        return carry

    lax.fori_loop(0, count_y // (ROWS * group), block_of, 0)


def y_kernel(group, kept, count_x, count_y, emit_ref, field_ref, index_ref, mask_ref, turned_ref,
             out_ref):
    cells_z = emit_ref.shape[-1]
    pitch = emit_ref.shape[1] // count_x
    size = out_ref.shape[0] * PIECE
    first = jnp.where(is_set("gy", 1) == bool(kept), size, 0)
    turned = [turned_ref[2 + v] != 0 for v in range(2)]
    zeros = jnp.zeros((ROWS, cells_z), jnp.float32)

    def block_of(block, carry):
        def body(j, states):
            fields = []
            for g in range(group):
                start = (first + (block * group + g) * ROWS) * pitch
                rows = pl.ds(start + j, ROWS, stride=pitch)
                fields.append((emit_ref[0, rows, :], emit_ref[1, rows, :], emit_ref[2, rows, :],
                               field_ref[3, rows, :]))
            return tuple(march(fields, 2 * count_x + v * count_y + j, turned[v], index_ref, mask_ref,
                               states[v]) for v in range(2))

        states = lax.fori_loop(0, count_y, body, (((zeros,) * 4,) * group,) * 2, unroll=UNROLL_Y)
        for v in range(2):
            for g in range(group):
                for c, value in enumerate(settle(turned[v], states[v][g])):
                    for half in range(2):
                        out_ref[2 * (block * group + g) + half, c, pl.ds(PIECE * v, PIECE), :] = (
                            value[PIECE * half:PIECE * (half + 1)])
        return carry

    lax.fori_loop(0, size // (ROWS * group), block_of, 0)


def options(micros, limit=16 << 20):
    return dict(
        compiler_params=pltpu.CompilerParams(vmem_limit_bytes=limit),
        cost_estimate=pl.CostEstimate(flops=0, transcendentals=0,
                                      bytes_accessed=int(micros * 3.5e6)))


def floats(*shape):
    return jax.ShapeDtypeStruct(shape, jnp.float32)


def load(density, transfer_table, shear_x, shear_y, direction):
    count_x, count_y, cells_z = density.shape
    places = 2 * (count_x + count_y)
    sources = [pltpu.with_memory_space_constraint(a, pltpu.HBM)
               for a in (density, transfer_table, shear_x, shear_y, direction)]
    return pl.pallas_call(
        functools.partial(load_kernel, STAGES),
        out_shape=(floats(count_x + 2, count_y + 2 * ROWS, cells_z),
                   floats(count_y, cells_z), floats(count_y, cells_z),
                   floats(count_x, cells_z), floats(count_x, cells_z),
                   floats(4, ROWS, cells_z),
                   jax.ShapeDtypeStruct((places, ROWS, cells_z), jnp.int32),
                   floats(places, ROWS, cells_z),
                   jax.ShapeDtypeStruct((4, ROWS, cells_z), jnp.int32),
                   floats(sum(len(masks) for _, masks in STAGES), ROWS, cells_z)),
        in_specs=[HBM] * 5,
        out_specs=(VMEM,) * 10,
        scratch_shapes=[pltpu.VMEM(transfer_table.shape, jnp.int32),
                        pltpu.SMEM(shear_x.shape, jnp.int32), pltpu.SMEM(shear_y.shape, jnp.int32),
                        pltpu.SMEM(direction.shape, jnp.int32), pltpu.SemaphoreType.DMA((5,))],
        name="load",
        **options(2),
    )(*sources)


def relay(own, hopped):
    return pl.pallas_call(
        relay_kernel,
        out_shape=floats(2 * own.shape[0], own.shape[1]),
        in_specs=[VMEM, VMEM],
        out_specs=VMEM,
        name="relay",
        **options(0.3),
    )(own, hopped)


def classify(cells, lut, step_len, part, *before):
    count_x, count_y, cells_z = cells.shape[0] - 2, cells.shape[1] - 2 * ROWS, cells.shape[2]
    return pl.pallas_call(
        functools.partial(classify_kernel, step_len, part),
        out_shape=floats(4, count_x * (count_y + 1), cells_z),
        in_specs=[VMEM] * (2 + len(before)),
        out_specs=VMEM,
        input_output_aliases={2: 0} if before else {},
        **options(1.5),
    )(cells, lut, *before)


def x_march(cells, halo, field, shifts):
    count_y, cells_z = cells.shape[1] - 2 * ROWS, cells.shape[2]
    part = floats(count_y // (2 * PIECE), 4, 2 * PIECE, cells_z)
    return pl.pallas_call(
        functools.partial(x_kernel, GROUP_X),
        out_shape=(part, part, floats(3, *field.shape[1:]), floats(*cells.shape)),
        in_specs=[VMEM] * 8,
        out_specs=(VMEM,) * 4,
        input_output_aliases={7: 3},
        name="x_march",
        **options(8),
    )(*halo, field, *shifts, cells)[:3]


def y_march(emitted, field, shifts, sizes, kept):
    cells_z = field.shape[-1]
    return pl.pallas_call(
        functools.partial(y_kernel, GROUP_Y, kept, *sizes),
        out_shape=floats(sizes[0] // (2 * PIECE), 4, 2 * PIECE, cells_z),
        in_specs=[VMEM] * 5,
        out_specs=VMEM,
        **options(2.5),
    )(emitted, field, *shifts)


def neighbours(axis, offset):
    count = lax.axis_size(axis)
    pairs = [(i, i + 1) for i in range(offset, count - 1, 2)]
    return pairs + [(target, source) for source, target in pairs]


def hops(axis):
    count = lax.axis_size(axis)
    moves = [(i, i + 4 * (i % 2) - 2) for i in range(count)]
    return [(source, target) for source, target in moves if 0 <= target < count]


def swapped(axis, mask):
    return [(i, i ^ mask) for i in range(lax.axis_size(axis))]


def stage_kernel(axis, mask, order, split, keep_ref, got_ref, ahead_ref, *out_refs):
    mine_ahead = ahead_ref[order] > 0.5

    def joined(p):
        mine, theirs = [[ref[p, c] for c in range(4)] for ref in (keep_ref, got_ref)]
        seen = jnp.exp2(-jnp.where(mine_ahead, mine[3], theirs[3]))
        near, far = jnp.where(mine_ahead, 1.0, seen), jnp.where(mine_ahead, seen, 1.0)
        return [mine[c] * near + theirs[c] * far for c in range(3)] + [mine[3] + theirs[3]]

    parts = [joined(p) for p in range(keep_ref.shape[0])]
    if split == "image":
        red, green, blue, total = parts[0]
        for c, value in enumerate((red, green, blue, 1.0 - jnp.exp2(-total))):
            for v in range(2):
                out_refs[0][v, c] = value[PIECE * v:PIECE * (v + 1)]
        return
    pick = lambda flag, a, b: [jnp.where(flag, one, two) for one, two in zip(a, b)]
    if split == "pair":
        high = is_set(axis, mask)
        pairs = list(zip(parts[::2], parts[1::2]))
        keep = [pick(high, b, a) for a, b in pairs]
        give = [pick(high, a, b) for a, b in pairs]
    elif split == "ring_first":
        upper = is_set(axis, 2 * mask)
        edge = is_set(axis, mask) == upper
        ends, middle = (parts[0], parts[3]), (parts[1], parts[2])
        small, large = [pick(edge, ends[k], middle[k]) for k in range(2)]
        keep = [pick(upper, large, small), pick(upper, small, large)]
        small, large = [pick(edge, middle[k], ends[k]) for k in range(2)]
        give = [pick(upper, large, small), pick(upper, small, large)]
    else:
        keep, give = parts[:1], parts[1:]
    for ref, pieces in zip(out_refs, (keep, give)):
        for p, piece in enumerate(pieces):
            for c in range(4):
                ref[p, c] = piece[c]


class Exchange:
    def __init__(self, axis, first, ahead):
        self.axis, self.first, self.ahead = axis, first, ahead
        self.stage = 0

    def send(self, keep, give, mask):
        self.keep, self.stage = keep, self.stage + 1
        self.got = lax.ppermute(give, self.axis, swapped(self.axis, mask))

    def meet(self, split, mask=0):
        count, *rest = self.keep.shape
        if split == "image":
            shape = floats(2, 4, PIECE, rest[-1])
        else:
            shape = (floats(count // 2, *rest),) * 2
        return pl.pallas_call(
            functools.partial(stage_kernel, self.axis, mask, self.first + self.stage - 1, split),
            out_shape=shape,
            in_specs=[VMEM] * 3,
            out_specs=VMEM if split == "image" else (VMEM, VMEM),
            **options(0.3),
        )(self.keep, self.got, self.ahead)


def local(density, transfer_table, shear_x, shear_y, direction):
    count_x = density.shape[0]
    step_len = 1.0 / (count_x * lax.axis_size("gx"))
    cells, outer, inner, hop, own, lut, *shifts, ahead = load(density, transfer_table, shear_x,
                                                              shear_y, direction)
    inner = lax.ppermute(inner, "gx", swapped("gx", 1))
    hopped = lax.ppermute(hop, "gy", hops("gy"))
    outer = lax.ppermute(outer, "gx", neighbours("gx", 1))
    crossed = lax.ppermute(relay(own, hopped), "gy", swapped("gy", 1))
    field = classify(cells, lut, step_len, 0)
    field = classify(cells, lut, step_len, 1, field)
    halo = (outer, inner, crossed)
    keep_x, give_x, emitted = x_march(cells, halo, field, shifts)

    x, y = Exchange("gx", 0, ahead), Exchange("gy", len(STAGES[0][1]), ahead)
    x.send(keep_x, give_x, 1)
    given = y_march(emitted, field, shifts, density.shape[:2], 0)
    kept = y_march(emitted, field, shifts, density.shape[:2], 1)
    x.send(*x.meet("pair", 2), 2)
    y.send(kept, given, 1)
    x.send(*x.meet("ring_first", 4), 4)
    x.send(*x.meet("ring_second"), 12)
    y.send(*y.meet("ring_first", 2), 2)
    image_x = x.meet("image")
    y.send(*y.meet("ring_second"), 6)
    return image_x, y.meet("image")


def solution(mesh):
    placed = (P("gx", "gy", None), P(), P(None, "gx"), P(None, "gy"), P())
    return jax.shard_map(
        local,
        mesh=mesh,
        in_specs=placed,
        out_specs=(P(None, None, ("gy", "gx"), None), P(None, None, ("gx", "gy"), None)),
        check_vma=False,
    )
```

```python
import functools

import jax
import jax.numpy as jnp
from jax import lax
from jax.experimental import pallas as pl
from jax.experimental.pallas import tpu as pltpu
from jax.sharding import PartitionSpec as P


ROWS = 8
PIECE = 4
LOG2E = 1.4426950408889634
PACK = 1024.0
ROUNDER = 12582912.0
GROUP_X, GROUP_Y = 4, 2
UNROLL_C, UNROLL_E, UNROLL_F, UNROLL_X, UNROLL_Y = 16, 32, 30, 32, 64

VMEM = pl.BlockSpec(memory_space=pltpu.VMEM)
HBM = pl.BlockSpec(memory_space=pltpu.HBM)
STAGES = (("gx", (1, 2, 4, 8)), ("gy", (1, 2, 4)))


def is_set(axis, mask):
    return (lax.axis_index(axis) & mask) != 0


def slot_of(i, count):
    piece = i // PIECE
    return (piece % 2) * (count // 2) + (piece // 2) * PIECE + i % PIECE


def lane_take(values, index):
    numbers = lax.GatherDimensionNumbers(
        offset_dims=(), collapsed_slice_dims=(1,), start_index_map=(1,),
        operand_batching_dims=(0,), start_indices_batching_dims=(0,))
    return lax.gather(values, index[..., None], numbers, slice_sizes=(1, 1),
                      mode=lax.GatherScatterMode.PROMISE_IN_BOUNDS)


def load_kernel(stages, density_ref, table_ref, shear_x_ref, shear_y_ref, turn_ref, cells_ref,
                face_xa_ref, face_xb_ref, hop_ref, own_ref, lut_ref, index_ref, mask_ref, turned_ref,
                ahead_ref, levels_ref, shifts_x_ref, shifts_y_ref, turns_ref, sems):
    count_x, count_y, cells_z = density_ref.shape
    inner = cells_ref.at[pl.ds(1, count_x), pl.ds(ROWS, count_y), :]
    copies = [pltpu.make_async_copy(source, target, sems.at[k]) for k, (source, target) in
              enumerate(((density_ref, inner), (turn_ref, turns_ref), (shear_x_ref, shifts_x_ref),
                         (shear_y_ref, shifts_y_ref), (table_ref, levels_ref)))]
    for copy in copies:
        copy.start()

    lane = lax.broadcasted_iota(jnp.int32, (ROWS, cells_z), 1)
    row = lax.broadcasted_iota(jnp.int32, (ROWS, cells_z), 0)
    copies[1].wait()
    stage = 0
    for family, (axis, masks) in enumerate(stages):
        turned = jnp.where(row < PIECE, turns_ref[family, 0], turns_ref[family, 1])
        for mask in masks:
            ahead_ref[stage] = jnp.where(turned == jnp.where(is_set(axis, mask), 1, 0), 1.0, 0.0)
            stage += 1

    for family, shifts_ref in enumerate((shifts_x_ref, shifts_y_ref)):
        copies[2 + family].wait()
        count = shifts_ref.shape[1]
        for v in range(2):
            turned = turns_ref[family, v]
            turned_ref[2 * family + v] = jnp.full((ROWS, cells_z), turned, jnp.int32)
            sign = jnp.full((ROWS, cells_z), jnp.where(turned != 0, 1.0, -1.0), jnp.float32)
            first = 2 * family * count_x + v * count

            def shifted(i, carry):
                source = lane - shifts_ref[v, i]
                inside = source & (cells_z - 1)
                index_ref[first + i] = inside
                mask_ref[first + i] = jnp.where(inside == source, sign, 0.0)
                return carry

            lax.fori_loop(0, count, shifted, 0, unroll=8)

    copies[4].wait()
    levels = levels_ref[...].astype(jnp.float32)
    for c in range(4):
        level = jnp.broadcast_to(levels[c:c + 1], (ROWS, cells_z))
        rise = jnp.where(lane == cells_z - 1, 0.0, pltpu.roll(level, cells_z - 1, 1) - level)
        lut_ref[c] = level + rise * (1.0 / PACK)
    copies[0].wait()

    odd_x, odd_y = is_set("gx", 1), is_set("gy", 1)
    first, last = cells_ref[1, pl.ds(ROWS, count_y), :], cells_ref[count_x, pl.ds(ROWS, count_y), :]
    face_xa_ref[...] = jnp.where(odd_x, last, first)
    face_xb_ref[...] = jnp.where(odd_x, first, last)
    first, last = (cells_ref[pl.ds(1, count_x), ROWS, :],
                   cells_ref[pl.ds(1, count_x), ROWS + count_y - 1, :])
    hop_ref[...] = jnp.where(odd_y, last, first)
    own_ref[...] = jnp.where(odd_y, first, last)


def relay_kernel(own_ref, hopped_ref, out_ref):
    rows = own_ref.shape[0]
    out_ref[pl.ds(0, rows), :] = own_ref[...]
    out_ref[pl.ds(rows, rows), :] = hopped_ref[...]


def classify_kernel(step_len, parity, cells_ref, lut_ref, *refs):
    field_ref = refs[-1]
    count_x, cells_z = cells_ref.shape[0] - 2, cells_ref.shape[2]
    count_y = cells_ref.shape[1] - 2 * ROWS
    pitch = field_ref.shape[1] // count_x

    def body(t, carry):
        i = (t // PIECE * 2 + parity) * PIECE + t % PIECE
        slot = (t + parity * (count_x // 2)) * pitch
        for base in range(0, count_y, ROWS):
            scaled = cells_ref[i + 1, pl.ds(ROWS + base, ROWS), :] * (cells_z - 1.0)
            knot = scaled.astype(jnp.int32)
            part = (scaled - knot.astype(jnp.float32)) * PACK - 1.0
            classed = []
            for c in range(4):
                packed = lane_take(lut_ref[c], knot)
                level = (packed + ROUNDER) - ROUNDER
                classed.append(packed + (packed - level) * part)
            optical = classed[3] * (2.0 * step_len * LOG2E / 255.0)
            opacity = (1.0 - jnp.exp2(-optical)) * (1.0 / 255.0)
            values = [classed[c] * opacity for c in range(3)] + [optical]
            for c in range(4):
                field_ref[c, pl.ds(slot + base, ROWS), :] = values[c]
        return carry

    lax.fori_loop(0, count_x // 2, body, 0, unroll=UNROLL_C)


def march(fields, place, turned, index_ref, mask_ref, states):
    index, mask = index_ref[place], mask_ref[place]
    out = []
    for (red, green, blue, optical), state in zip(fields, states):
        depth = lane_take(optical, index) * mask
        after = state[0] + depth
        seen = jnp.exp2(jnp.where(turned, after, state[0])) * mask
        out.append((after, state[1] + seen * lane_take(red, index),
                    state[2] + seen * lane_take(green, index),
                    state[3] + seen * lane_take(blue, index)))
    return tuple(out)


def settle(turned, state):
    sign = jnp.where(turned, 1.0, -1.0)
    total = state[0] * sign
    fade = jnp.exp2(jnp.where(turned, -total, 0.0)) * sign
    return [state[1] * fade, state[2] * fade, state[3] * fade, total]


def emission(cells_ref, field_ref, emit_ref, i, base):
    count_x, cells_z = cells_ref.shape[0] - 2, cells_ref.shape[2]
    pitch, pad = field_ref.shape[1] // count_x, ROWS
    lane = lax.broadcasted_iota(jnp.int32, (ROWS, cells_z), 1)
    here = cells_ref[i + 1, pl.ds(base + pad, ROWS), :]
    diff_x = (cells_ref[i + 2, pl.ds(base + pad, ROWS), :]
              - cells_ref[i, pl.ds(base + pad, ROWS), :])
    diff_y = (cells_ref[i + 1, pl.ds(base + pad + 1, ROWS), :]
              - cells_ref[i + 1, pl.ds(base + pad - 1, ROWS), :])
    above = lane_take(here, (lane + 1) & (cells_z - 1))
    below = lane_take(here, (lane - 1) & (cells_z - 1))
    diff_z = jnp.where(lane == cells_z - 1, 0.0, above) - jnp.where(lane == 0, 0.0, below)
    side = diff_y + diff_z
    facing = jnp.abs(diff_x + (side + side))
    norm = diff_x * diff_x + diff_y * diff_y + diff_z * diff_z + 0.04
    shaded = 0.3 + (0.7 / 3.0) * facing * lax.rsqrt(norm)
    rows = pl.ds(slot_of(i, count_x) * pitch + base, ROWS)
    for c in range(3):
        emit_ref[c, rows, :] = field_ref[c, rows, :] * shaded


def shade_kernel(cells_ref, field_ref, emit_ref):
    count_x, count_y = cells_ref.shape[0] - 2, cells_ref.shape[1] - 2 * ROWS

    def body(i, carry):
        for base in range(0, count_y, ROWS):
            emission(cells_ref, field_ref, emit_ref, i, base)
        return carry

    lax.fori_loop(0, count_x, body, 0, unroll=UNROLL_E)


def x_kernel(group, face_xa_ref, face_xb_ref, crossed_ref, field_ref, index_ref,
             mask_ref, turned_ref, _cells, _emit, keep_ref, give_ref, emit_ref, cells_ref):
    count_x, cells_z = cells_ref.shape[0] - 2, cells_ref.shape[2]
    count_y = cells_ref.shape[1] - 2 * ROWS
    pitch = field_ref.shape[1] // count_x
    pad = ROWS
    lane = lax.broadcasted_iota(jnp.int32, (ROWS, cells_z), 1)

    odd_x, odd_y = is_set("gx", 1), is_set("gy", 1)
    near, far = face_xa_ref[...], face_xb_ref[...]
    cells_ref[0, pl.ds(pad, count_y), :] = jnp.where(odd_x, far, near)
    cells_ref[count_x + 1, pl.ds(pad, count_y), :] = jnp.where(odd_x, near, far)
    near, far = crossed_ref[pl.ds(0, count_x), :], crossed_ref[pl.ds(count_x, count_x), :]
    low_y, high_y = jnp.where(odd_y, near, far), jnp.where(odd_y, far, near)
    for i in range(count_x):
        cells_ref[i + 1, pl.ds(pad - 1, 1), :] = low_y[i:i + 1]
        cells_ref[i + 1, pl.ds(pad + count_y, 1), :] = high_y[i:i + 1]

    turned = [turned_ref[v] != 0 for v in range(2)]
    zeros = jnp.zeros((ROWS, cells_z), jnp.float32)
    for i in (0, count_x - 1):
        for base in range(0, count_y, ROWS):
            emission(cells_ref, field_ref, emit_ref, i, base)

    def edges(i, carry):
        for base in (0, count_y - ROWS):
            emission(cells_ref, field_ref, emit_ref, i, base)
        return carry

    lax.fori_loop(1, count_x - 1, edges, 0, unroll=UNROLL_F)

    def block_of(block, carry):
        base = pl.multiple_of(block * (ROWS * group), ROWS)

        def body(i, states):
            fields = []
            slot = slot_of(i, count_x) * pitch
            for g in range(group):
                rows = pl.ds(slot + base + g * ROWS, ROWS)
                fields.append((emit_ref[0, rows, :], emit_ref[1, rows, :], emit_ref[2, rows, :],
                               field_ref[3, rows, :]))
            return tuple(march(fields, v * count_x + i, turned[v], index_ref, mask_ref,
                               states[v]) for v in range(2))

        states = lax.fori_loop(0, count_x, body, (((zeros,) * 4,) * group,) * 2, unroll=UNROLL_X)
        for v in range(2):
            for g in range(group):
                for c, value in enumerate(settle(turned[v], states[v][g])):
                    even, odd = value[:PIECE], value[PIECE:]
                    spot, rows = block * group + g, pl.ds(PIECE * v, PIECE)
                    keep_ref[spot, c, rows, :] = jnp.where(odd_x, odd, even)
                    give_ref[spot, c, rows, :] = jnp.where(odd_x, even, odd)
        return carry

    lax.fori_loop(0, count_y // (ROWS * group), block_of, 0)


def y_kernel(group, kept, count_x, count_y, emit_ref, field_ref, index_ref, mask_ref, turned_ref,
             out_ref):
    cells_z = emit_ref.shape[-1]
    pitch = emit_ref.shape[1] // count_x
    size = out_ref.shape[0] * PIECE
    first = jnp.where(is_set("gy", 1) == bool(kept), size, 0)
    turned = [turned_ref[2 + v] != 0 for v in range(2)]
    zeros = jnp.zeros((ROWS, cells_z), jnp.float32)

    def block_of(block, carry):
        def body(j, states):
            fields = []
            for g in range(group):
                start = (first + (block * group + g) * ROWS) * pitch
                rows = pl.ds(start + j, ROWS, stride=pitch)
                fields.append((emit_ref[0, rows, :], emit_ref[1, rows, :], emit_ref[2, rows, :],
                               field_ref[3, rows, :]))
            return tuple(march(fields, 2 * count_x + v * count_y + j, turned[v], index_ref, mask_ref,
                               states[v]) for v in range(2))

        states = lax.fori_loop(0, count_y, body, (((zeros,) * 4,) * group,) * 2, unroll=UNROLL_Y)
        for v in range(2):
            for g in range(group):
                for c, value in enumerate(settle(turned[v], states[v][g])):
                    for half in range(2):
                        out_ref[2 * (block * group + g) + half, c, pl.ds(PIECE * v, PIECE), :] = (
                            value[PIECE * half:PIECE * (half + 1)])
        return carry

    lax.fori_loop(0, size // (ROWS * group), block_of, 0)


def options(micros, limit=16 << 20):
    return dict(
        compiler_params=pltpu.CompilerParams(vmem_limit_bytes=limit),
        cost_estimate=pl.CostEstimate(flops=0, transcendentals=0,
                                      bytes_accessed=int(micros * 3.5e6)))


def floats(*shape):
    return jax.ShapeDtypeStruct(shape, jnp.float32)


def load(density, transfer_table, shear_x, shear_y, direction):
    count_x, count_y, cells_z = density.shape
    places = 2 * (count_x + count_y)
    sources = [pltpu.with_memory_space_constraint(a, pltpu.HBM)
               for a in (density, transfer_table, shear_x, shear_y, direction)]
    return pl.pallas_call(
        functools.partial(load_kernel, STAGES),
        out_shape=(floats(count_x + 2, count_y + 2 * ROWS, cells_z),
                   floats(count_y, cells_z), floats(count_y, cells_z),
                   floats(count_x, cells_z), floats(count_x, cells_z),
                   floats(4, ROWS, cells_z),
                   jax.ShapeDtypeStruct((places, ROWS, cells_z), jnp.int32),
                   floats(places, ROWS, cells_z),
                   jax.ShapeDtypeStruct((4, ROWS, cells_z), jnp.int32),
                   floats(sum(len(masks) for _, masks in STAGES), ROWS, cells_z)),
        in_specs=[HBM] * 5,
        out_specs=(VMEM,) * 10,
        scratch_shapes=[pltpu.VMEM(transfer_table.shape, jnp.int32),
                        pltpu.SMEM(shear_x.shape, jnp.int32), pltpu.SMEM(shear_y.shape, jnp.int32),
                        pltpu.SMEM(direction.shape, jnp.int32), pltpu.SemaphoreType.DMA((5,))],
        name="load",
        **options(2),
    )(*sources)


def relay(own, hopped):
    return pl.pallas_call(
        relay_kernel,
        out_shape=floats(2 * own.shape[0], own.shape[1]),
        in_specs=[VMEM, VMEM],
        out_specs=VMEM,
        name="relay",
        **options(0.3),
    )(own, hopped)


def classify(cells, lut, step_len, part, *before):
    count_x, count_y, cells_z = cells.shape[0] - 2, cells.shape[1] - 2 * ROWS, cells.shape[2]
    return pl.pallas_call(
        functools.partial(classify_kernel, step_len, part),
        out_shape=floats(4, count_x * (count_y + 1), cells_z),
        in_specs=[VMEM] * (2 + len(before)),
        out_specs=VMEM,
        input_output_aliases={2: 0} if before else {},
        **options(1.5),
    )(cells, lut, *before)


def shade(cells, field):
    return pl.pallas_call(
        shade_kernel,
        out_shape=floats(3, *field.shape[1:]),
        in_specs=[VMEM, VMEM],
        out_specs=VMEM,
        name="shade",
        **options(2),
    )(cells, field)


def x_march(cells, halo, field, shifts, emitted):
    count_y, cells_z = cells.shape[1] - 2 * ROWS, cells.shape[2]
    part = floats(count_y // (2 * PIECE), 4, 2 * PIECE, cells_z)
    return pl.pallas_call(
        functools.partial(x_kernel, GROUP_X),
        out_shape=(part, part, floats(*emitted.shape), floats(*cells.shape)),
        in_specs=[VMEM] * 9,
        out_specs=(VMEM,) * 4,
        input_output_aliases={7: 3, 8: 2},
        name="x_march",
        **options(4),
    )(*halo, field, *shifts, cells, emitted)[:3]


def y_march(emitted, field, shifts, sizes, kept):
    cells_z = field.shape[-1]
    return pl.pallas_call(
        functools.partial(y_kernel, GROUP_Y, kept, *sizes),
        out_shape=floats(sizes[0] // (2 * PIECE), 4, 2 * PIECE, cells_z),
        in_specs=[VMEM] * 5,
        out_specs=VMEM,
        **options(2.5),
    )(emitted, field, *shifts)


def neighbours(axis, offset):
    count = lax.axis_size(axis)
    pairs = [(i, i + 1) for i in range(offset, count - 1, 2)]
    return pairs + [(target, source) for source, target in pairs]


def hops(axis):
    count = lax.axis_size(axis)
    moves = [(i, i + 4 * (i % 2) - 2) for i in range(count)]
    return [(source, target) for source, target in moves if 0 <= target < count]


def swapped(axis, mask):
    return [(i, i ^ mask) for i in range(lax.axis_size(axis))]


def joined(keep_ref, got_ref, ahead, p):
    mine_ahead = ahead > 0.5
    mine, theirs = [[ref[p, c] for c in range(4)] for ref in (keep_ref, got_ref)]
    seen = jnp.exp2(-jnp.where(mine_ahead, mine[3], theirs[3]))
    near, far = jnp.where(mine_ahead, 1.0, seen), jnp.where(mine_ahead, seen, 1.0)
    return [mine[c] * near + theirs[c] * far for c in range(3)] + [mine[3] + theirs[3]]


def image_kernel(orders, keep_x_ref, got_x_ref, keep_y_ref, got_y_ref, ahead_ref, *out_refs):
    refs = ((keep_x_ref, got_x_ref), (keep_y_ref, got_y_ref))
    for order, (keep_ref, got_ref), out_ref in zip(orders, refs, out_refs):
        red, green, blue, total = joined(keep_ref, got_ref, ahead_ref[order], 0)
        for c, value in enumerate((red, green, blue, 1.0 - jnp.exp2(-total))):
            for v in range(2):
                out_ref[v, c] = value[PIECE * v:PIECE * (v + 1)]


def images(x, y):
    shape = floats(2, 4, PIECE, x.keep.shape[-1])
    return pl.pallas_call(
        functools.partial(image_kernel, (x.order(), y.order())),
        out_shape=(shape, shape),
        in_specs=[VMEM] * 5,
        out_specs=(VMEM, VMEM),
        name="images",
        **options(0.3),
    )(x.keep, x.got, y.keep, y.got, x.ahead)


def stage_kernel(axis, mask, order, split, keep_ref, got_ref, ahead_ref, *out_refs):
    parts = [joined(keep_ref, got_ref, ahead_ref[order], p) for p in range(keep_ref.shape[0])]
    pick = lambda flag, a, b: [jnp.where(flag, one, two) for one, two in zip(a, b)]
    if split == "pair":
        high = is_set(axis, mask)
        pairs = list(zip(parts[::2], parts[1::2]))
        keep = [pick(high, b, a) for a, b in pairs]
        give = [pick(high, a, b) for a, b in pairs]
    elif split == "ring_first":
        upper = is_set(axis, 2 * mask)
        edge = is_set(axis, mask) == upper
        ends, middle = (parts[0], parts[3]), (parts[1], parts[2])
        small, large = [pick(edge, ends[k], middle[k]) for k in range(2)]
        keep = [pick(upper, large, small), pick(upper, small, large)]
        small, large = [pick(edge, middle[k], ends[k]) for k in range(2)]
        give = [pick(upper, large, small), pick(upper, small, large)]
    else:
        keep, give = parts[:1], parts[1:]
    for ref, pieces in zip(out_refs, (keep, give)):
        for p, piece in enumerate(pieces):
            for c in range(4):
                ref[p, c] = piece[c]


class Exchange:
    def __init__(self, axis, first, ahead):
        self.axis, self.first, self.ahead = axis, first, ahead
        self.stage = 0

    def send(self, keep, give, mask):
        self.keep, self.stage = keep, self.stage + 1
        self.got = lax.ppermute(give, self.axis, swapped(self.axis, mask))

    def order(self):
        return self.first + self.stage - 1

    def meet(self, split, mask=0):
        count, *rest = self.keep.shape
        return pl.pallas_call(
            functools.partial(stage_kernel, self.axis, mask, self.order(), split),
            out_shape=(floats(count // 2, *rest),) * 2,
            in_specs=[VMEM] * 3,
            out_specs=(VMEM, VMEM),
            **options(0.3),
        )(self.keep, self.got, self.ahead)


def local(density, transfer_table, shear_x, shear_y, direction):
    count_x = density.shape[0]
    step_len = 1.0 / (count_x * lax.axis_size("gx"))
    cells, outer, inner, hop, own, lut, *shifts, ahead = load(density, transfer_table, shear_x,
                                                              shear_y, direction)
    inner = lax.ppermute(inner, "gx", swapped("gx", 1))
    hopped = lax.ppermute(hop, "gy", hops("gy"))
    outer = lax.ppermute(outer, "gx", neighbours("gx", 1))
    crossed = lax.ppermute(relay(own, hopped), "gy", swapped("gy", 1))
    field = classify(cells, lut, step_len, 0)
    field = classify(cells, lut, step_len, 1, field)
    emitted = shade(cells, field)
    halo = (outer, inner, crossed)
    keep_x, give_x, emitted = x_march(cells, halo, field, shifts, emitted)

    x, y = Exchange("gx", 0, ahead), Exchange("gy", len(STAGES[0][1]), ahead)
    x.send(keep_x, give_x, 1)
    given = y_march(emitted, field, shifts, density.shape[:2], 0)
    kept = y_march(emitted, field, shifts, density.shape[:2], 1)
    x.send(*x.meet("pair", 2), 2)
    y.send(kept, given, 1)
    x.send(*x.meet("ring_first", 4), 4)
    x.send(*x.meet("ring_second"), 12)
    y.send(*y.meet("ring_first", 2), 2)
    y.send(*y.meet("ring_second"), 6)
    return images(x, y)


def solution(mesh):
    placed = (P("gx", "gy", None), P(), P(None, "gx"), P(None, "gy"), P())
    return jax.shard_map(
        local,
        mesh=mesh,
        in_specs=placed,
        out_specs=(P(None, None, ("gy", "gx"), None), P(None, None, ("gx", "gy"), None)),
        check_vma=False,
    )
```

```python
import functools

import jax
import jax.numpy as jnp
from jax import lax
from jax.experimental import pallas as pl
from jax.experimental.pallas import tpu as pltpu
from jax.sharding import PartitionSpec as P


ROWS = 8
PIECE = 4
LOG2E = 1.4426950408889634
PACK = 1024.0
ROUNDER = 12582912.0
GROUP_X, GROUP_Y = 4, 2
UNROLL_C, UNROLL_E, UNROLL_F, UNROLL_X, UNROLL_Y = 16, 32, 30, 32, 64

VMEM = pl.BlockSpec(memory_space=pltpu.VMEM)
HBM = pl.BlockSpec(memory_space=pltpu.HBM)
STAGES = (("gx", (1, 2, 4, 8)), ("gy", (1, 2, 4)))


def is_set(axis, mask):
    return (lax.axis_index(axis) & mask) != 0


def slot_of(i, count):
    piece = i // PIECE
    return (piece % 2) * (count // 2) + (piece // 2) * PIECE + i % PIECE


def lane_take(values, index):
    numbers = lax.GatherDimensionNumbers(
        offset_dims=(), collapsed_slice_dims=(1,), start_index_map=(1,),
        operand_batching_dims=(0,), start_indices_batching_dims=(0,))
    return lax.gather(values, index[..., None], numbers, slice_sizes=(1, 1),
                      mode=lax.GatherScatterMode.PROMISE_IN_BOUNDS)


def load_kernel(stages, density_ref, table_ref, shear_x_ref, shear_y_ref, turn_ref, cells_ref,
                face_xa_ref, face_xb_ref, hop_ref, own_ref, lut_ref, index_ref, mask_ref, turned_ref,
                ahead_ref, levels_ref, shifts_x_ref, shifts_y_ref, turns_ref, sems):
    count_x, count_y, cells_z = density_ref.shape
    inner = cells_ref.at[pl.ds(1, count_x), pl.ds(ROWS, count_y), :]
    copies = [pltpu.make_async_copy(source, target, sems.at[k]) for k, (source, target) in
              enumerate(((density_ref, inner), (turn_ref, turns_ref), (shear_x_ref, shifts_x_ref),
                         (shear_y_ref, shifts_y_ref), (table_ref, levels_ref)))]
    for copy in copies:
        copy.start()

    lane = lax.broadcasted_iota(jnp.int32, (ROWS, cells_z), 1)
    row = lax.broadcasted_iota(jnp.int32, (ROWS, cells_z), 0)
    copies[1].wait()
    stage = 0
    for family, (axis, masks) in enumerate(stages):
        turned = jnp.where(row < PIECE, turns_ref[family, 0], turns_ref[family, 1])
        for mask in masks:
            ahead_ref[stage] = jnp.where(turned == jnp.where(is_set(axis, mask), 1, 0), 1.0, 0.0)
            stage += 1

    for family, shifts_ref in enumerate((shifts_x_ref, shifts_y_ref)):
        copies[2 + family].wait()
        count = shifts_ref.shape[1]
        for v in range(2):
            turned = turns_ref[family, v]
            turned_ref[2 * family + v] = jnp.full((ROWS, cells_z), turned, jnp.int32)
            sign = jnp.full((ROWS, cells_z), jnp.where(turned != 0, 1.0, -1.0), jnp.float32)
            first = 2 * family * count_x + v * count

            def shifted(i, carry):
                source = lane - shifts_ref[v, i]
                inside = source & (cells_z - 1)
                index_ref[first + i] = inside
                mask_ref[first + i] = jnp.where(inside == source, sign, 0.0)
                return carry

            lax.fori_loop(0, count, shifted, 0, unroll=8)

    copies[4].wait()
    levels = levels_ref[...].astype(jnp.float32)
    for c in range(4):
        level = jnp.broadcast_to(levels[c:c + 1], (ROWS, cells_z))
        rise = jnp.where(lane == cells_z - 1, 0.0, pltpu.roll(level, cells_z - 1, 1) - level)
        lut_ref[c] = level + rise * (1.0 / PACK)
    copies[0].wait()

    odd_x, odd_y = is_set("gx", 1), is_set("gy", 1)
    first, last = cells_ref[1, pl.ds(ROWS, count_y), :], cells_ref[count_x, pl.ds(ROWS, count_y), :]
    face_xa_ref[...] = jnp.where(odd_x, last, first)
    face_xb_ref[...] = jnp.where(odd_x, first, last)
    first, last = (cells_ref[pl.ds(1, count_x), ROWS, :],
                   cells_ref[pl.ds(1, count_x), ROWS + count_y - 1, :])
    hop_ref[...] = jnp.where(odd_y, last, first)
    own_ref[...] = jnp.where(odd_y, first, last)


def relay_kernel(own_ref, hopped_ref, out_ref):
    rows = own_ref.shape[0]
    out_ref[pl.ds(0, rows), :] = own_ref[...]
    out_ref[pl.ds(rows, rows), :] = hopped_ref[...]


def turn_kernel(own_ref, hopped_ref, out_ref):
    middle = is_set("gx", 1) != is_set("gx", 2)
    out_ref[...] = jnp.where(middle, own_ref[...], hopped_ref[...])


def classify_kernel(step_len, parity, cells_ref, lut_ref, *refs):
    field_ref = refs[-1]
    count_x, cells_z = cells_ref.shape[0] - 2, cells_ref.shape[2]
    count_y = cells_ref.shape[1] - 2 * ROWS
    pitch = field_ref.shape[1] // count_x

    def body(t, carry):
        i = (t // PIECE * 2 + parity) * PIECE + t % PIECE
        slot = (t + parity * (count_x // 2)) * pitch
        for base in range(0, count_y, ROWS):
            scaled = cells_ref[i + 1, pl.ds(ROWS + base, ROWS), :] * (cells_z - 1.0)
            knot = scaled.astype(jnp.int32)
            part = (scaled - knot.astype(jnp.float32)) * PACK - 1.0
            classed = []
            for c in range(4):
                packed = lane_take(lut_ref[c], knot)
                level = (packed + ROUNDER) - ROUNDER
                classed.append(packed + (packed - level) * part)
            optical = classed[3] * (2.0 * step_len * LOG2E / 255.0)
            opacity = (1.0 - jnp.exp2(-optical)) * (1.0 / 255.0)
            values = [classed[c] * opacity for c in range(3)] + [optical]
            for c in range(4):
                field_ref[c, pl.ds(slot + base, ROWS), :] = values[c]
        return carry

    lax.fori_loop(0, count_x // 2, body, 0, unroll=UNROLL_C)


def march(fields, place, turned, index_ref, mask_ref, states):
    index, mask = index_ref[place], mask_ref[place]
    out = []
    for (red, green, blue, optical), state in zip(fields, states):
        depth = lane_take(optical, index) * mask
        after = state[0] + depth
        seen = jnp.exp2(jnp.where(turned, after, state[0])) * mask
        out.append((after, state[1] + seen * lane_take(red, index),
                    state[2] + seen * lane_take(green, index),
                    state[3] + seen * lane_take(blue, index)))
    return tuple(out)


def settle(turned, state):
    sign = jnp.where(turned, 1.0, -1.0)
    total = state[0] * sign
    fade = jnp.exp2(jnp.where(turned, -total, 0.0)) * sign
    return [state[1] * fade, state[2] * fade, state[3] * fade, total]


def emission(cells_ref, field_ref, emit_ref, i, base):
    count_x, cells_z = cells_ref.shape[0] - 2, cells_ref.shape[2]
    pitch, pad = field_ref.shape[1] // count_x, ROWS
    lane = lax.broadcasted_iota(jnp.int32, (ROWS, cells_z), 1)
    here = cells_ref[i + 1, pl.ds(base + pad, ROWS), :]
    diff_x = (cells_ref[i + 2, pl.ds(base + pad, ROWS), :]
              - cells_ref[i, pl.ds(base + pad, ROWS), :])
    diff_y = (cells_ref[i + 1, pl.ds(base + pad + 1, ROWS), :]
              - cells_ref[i + 1, pl.ds(base + pad - 1, ROWS), :])
    above = lane_take(here, (lane + 1) & (cells_z - 1))
    below = lane_take(here, (lane - 1) & (cells_z - 1))
    diff_z = jnp.where(lane == cells_z - 1, 0.0, above) - jnp.where(lane == 0, 0.0, below)
    side = diff_y + diff_z
    facing = jnp.abs(diff_x + (side + side))
    norm = diff_x * diff_x + diff_y * diff_y + diff_z * diff_z + 0.04
    shaded = 0.3 + (0.7 / 3.0) * facing * lax.rsqrt(norm)
    rows = pl.ds(slot_of(i, count_x) * pitch + base, ROWS)
    for c in range(3):
        emit_ref[c, rows, :] = field_ref[c, rows, :] * shaded


def shade_kernel(cells_ref, field_ref, emit_ref):
    count_x, count_y = cells_ref.shape[0] - 2, cells_ref.shape[1] - 2 * ROWS

    def body(i, carry):
        for base in range(0, count_y, ROWS):
            emission(cells_ref, field_ref, emit_ref, i, base)
        return carry

    lax.fori_loop(0, count_x, body, 0, unroll=UNROLL_E)


def x_kernel(group, face_xa_ref, face_xb_ref, crossed_ref, field_ref, index_ref,
             mask_ref, turned_ref, _cells, _emit, keep_ref, give_ref, emit_ref, cells_ref):
    count_x, cells_z = cells_ref.shape[0] - 2, cells_ref.shape[2]
    count_y = cells_ref.shape[1] - 2 * ROWS
    pitch = field_ref.shape[1] // count_x
    pad = ROWS
    lane = lax.broadcasted_iota(jnp.int32, (ROWS, cells_z), 1)

    odd_x, odd_y = is_set("gx", 1), is_set("gy", 1)
    near, far = face_xa_ref[...], face_xb_ref[...]
    cells_ref[0, pl.ds(pad, count_y), :] = jnp.where(odd_x, far, near)
    cells_ref[count_x + 1, pl.ds(pad, count_y), :] = jnp.where(odd_x, near, far)
    near, far = crossed_ref[pl.ds(0, count_x), :], crossed_ref[pl.ds(count_x, count_x), :]
    low_y, high_y = jnp.where(odd_y, near, far), jnp.where(odd_y, far, near)
    for i in range(count_x):
        cells_ref[i + 1, pl.ds(pad - 1, 1), :] = low_y[i:i + 1]
        cells_ref[i + 1, pl.ds(pad + count_y, 1), :] = high_y[i:i + 1]

    turned = [turned_ref[v] != 0 for v in range(2)]
    zeros = jnp.zeros((ROWS, cells_z), jnp.float32)
    for i in (0, count_x - 1):
        for base in range(0, count_y, ROWS):
            emission(cells_ref, field_ref, emit_ref, i, base)

    def edges(i, carry):
        for base in (0, count_y - ROWS):
            emission(cells_ref, field_ref, emit_ref, i, base)
        return carry

    lax.fori_loop(1, count_x - 1, edges, 0, unroll=UNROLL_F)

    def block_of(block, carry):
        base = pl.multiple_of(block * (ROWS * group), ROWS)

        def body(i, states):
            fields = []
            slot = slot_of(i, count_x) * pitch
            for g in range(group):
                rows = pl.ds(slot + base + g * ROWS, ROWS)
                fields.append((emit_ref[0, rows, :], emit_ref[1, rows, :], emit_ref[2, rows, :],
                               field_ref[3, rows, :]))
            return tuple(march(fields, v * count_x + i, turned[v], index_ref, mask_ref,
                               states[v]) for v in range(2))

        states = lax.fori_loop(0, count_x, body, (((zeros,) * 4,) * group,) * 2, unroll=UNROLL_X)
        for v in range(2):
            for g in range(group):
                for c, value in enumerate(settle(turned[v], states[v][g])):
                    even, odd = value[:PIECE], value[PIECE:]
                    spot, rows = block * group + g, pl.ds(PIECE * v, PIECE)
                    keep_ref[spot, c, rows, :] = jnp.where(odd_x, odd, even)
                    give_ref[spot, c, rows, :] = jnp.where(odd_x, even, odd)
        return carry

    lax.fori_loop(0, count_y // (ROWS * group), block_of, 0)


def y_kernel(group, kept, count_x, count_y, emit_ref, field_ref, index_ref, mask_ref, turned_ref,
             out_ref):
    cells_z = emit_ref.shape[-1]
    pitch = emit_ref.shape[1] // count_x
    size = out_ref.shape[0] * PIECE
    first = jnp.where(is_set("gy", 1) == bool(kept), size, 0)
    turned = [turned_ref[2 + v] != 0 for v in range(2)]
    zeros = jnp.zeros((ROWS, cells_z), jnp.float32)

    def block_of(block, carry):
        def body(j, states):
            fields = []
            for g in range(group):
                start = (first + (block * group + g) * ROWS) * pitch
                rows = pl.ds(start + j, ROWS, stride=pitch)
                fields.append((emit_ref[0, rows, :], emit_ref[1, rows, :], emit_ref[2, rows, :],
                               field_ref[3, rows, :]))
            return tuple(march(fields, 2 * count_x + v * count_y + j, turned[v], index_ref, mask_ref,
                               states[v]) for v in range(2))

        states = lax.fori_loop(0, count_y, body, (((zeros,) * 4,) * group,) * 2, unroll=UNROLL_Y)
        for v in range(2):
            for g in range(group):
                for c, value in enumerate(settle(turned[v], states[v][g])):
                    for half in range(2):
                        out_ref[2 * (block * group + g) + half, c, pl.ds(PIECE * v, PIECE), :] = (
                            value[PIECE * half:PIECE * (half + 1)])
        return carry

    lax.fori_loop(0, size // (ROWS * group), block_of, 0)


def options(micros, limit=16 << 20):
    return dict(
        compiler_params=pltpu.CompilerParams(vmem_limit_bytes=limit),
        cost_estimate=pl.CostEstimate(flops=0, transcendentals=0,
                                      bytes_accessed=int(micros * 3.5e6)))


def floats(*shape):
    return jax.ShapeDtypeStruct(shape, jnp.float32)


def load(density, transfer_table, shear_x, shear_y, direction):
    count_x, count_y, cells_z = density.shape
    places = 2 * (count_x + count_y)
    sources = [pltpu.with_memory_space_constraint(a, pltpu.HBM)
               for a in (density, transfer_table, shear_x, shear_y, direction)]
    return pl.pallas_call(
        functools.partial(load_kernel, STAGES),
        out_shape=(floats(count_x + 2, count_y + 2 * ROWS, cells_z),
                   floats(count_y, cells_z), floats(count_y, cells_z),
                   floats(count_x, cells_z), floats(count_x, cells_z),
                   floats(4, ROWS, cells_z),
                   jax.ShapeDtypeStruct((places, ROWS, cells_z), jnp.int32),
                   floats(places, ROWS, cells_z),
                   jax.ShapeDtypeStruct((4, ROWS, cells_z), jnp.int32),
                   floats(sum(len(masks) for _, masks in STAGES), ROWS, cells_z)),
        in_specs=[HBM] * 5,
        out_specs=(VMEM,) * 10,
        scratch_shapes=[pltpu.VMEM(transfer_table.shape, jnp.int32),
                        pltpu.SMEM(shear_x.shape, jnp.int32), pltpu.SMEM(shear_y.shape, jnp.int32),
                        pltpu.SMEM(direction.shape, jnp.int32), pltpu.SemaphoreType.DMA((5,))],
        name="load",
        **options(2),
    )(*sources)


def relay(own, hopped):
    return pl.pallas_call(
        relay_kernel,
        out_shape=floats(2 * own.shape[0], own.shape[1]),
        in_specs=[VMEM, VMEM],
        out_specs=VMEM,
        name="relay",
        **options(0.3),
    )(own, hopped)


def turn(own, hopped):
    return pl.pallas_call(
        turn_kernel,
        out_shape=floats(*own.shape),
        in_specs=[VMEM, VMEM],
        out_specs=VMEM,
        name="turn",
        **options(0.3),
    )(own, hopped)


def classify(cells, lut, step_len, part, *before):
    count_x, count_y, cells_z = cells.shape[0] - 2, cells.shape[1] - 2 * ROWS, cells.shape[2]
    return pl.pallas_call(
        functools.partial(classify_kernel, step_len, part),
        out_shape=floats(4, count_x * (count_y + 1), cells_z),
        in_specs=[VMEM] * (2 + len(before)),
        out_specs=VMEM,
        input_output_aliases={2: 0} if before else {},
        **options(1.5),
    )(cells, lut, *before)


def shade(cells, field):
    return pl.pallas_call(
        shade_kernel,
        out_shape=floats(3, *field.shape[1:]),
        in_specs=[VMEM, VMEM],
        out_specs=VMEM,
        name="shade",
        **options(2),
    )(cells, field)


def x_march(cells, halo, field, shifts, emitted):
    count_y, cells_z = cells.shape[1] - 2 * ROWS, cells.shape[2]
    part = floats(count_y // (2 * PIECE), 4, 2 * PIECE, cells_z)
    return pl.pallas_call(
        functools.partial(x_kernel, GROUP_X),
        out_shape=(part, part, floats(*emitted.shape), floats(*cells.shape)),
        in_specs=[VMEM] * 9,
        out_specs=(VMEM,) * 4,
        input_output_aliases={7: 3, 8: 2},
        name="x_march",
        **options(4),
    )(*halo, field, *shifts, cells, emitted)[:3]


def y_march(emitted, field, shifts, sizes, kept):
    cells_z = field.shape[-1]
    return pl.pallas_call(
        functools.partial(y_kernel, GROUP_Y, kept, *sizes),
        out_shape=floats(sizes[0] // (2 * PIECE), 4, 2 * PIECE, cells_z),
        in_specs=[VMEM] * 5,
        out_specs=VMEM,
        **options(2.5),
    )(emitted, field, *shifts)


def ends(axis):
    count = lax.axis_size(axis)
    return ([(i, i + 4) for i in range(3, count - 4, 4)] + [(i, i - 4) for i in range(4, count, 4)])


def hops(axis):
    count = lax.axis_size(axis)
    moves = [(i, i + 4 * (i % 2) - 2) for i in range(count)]
    return [(source, target) for source, target in moves if 0 <= target < count]


def swapped(axis, mask):
    return [(i, i ^ mask) for i in range(lax.axis_size(axis))]


def joined(keep_ref, got_ref, ahead, p):
    mine_ahead = ahead > 0.5
    mine, theirs = [[ref[p, c] for c in range(4)] for ref in (keep_ref, got_ref)]
    seen = jnp.exp2(-jnp.where(mine_ahead, mine[3], theirs[3]))
    near, far = jnp.where(mine_ahead, 1.0, seen), jnp.where(mine_ahead, seen, 1.0)
    return [mine[c] * near + theirs[c] * far for c in range(3)] + [mine[3] + theirs[3]]


def image_kernel(orders, keep_x_ref, got_x_ref, keep_y_ref, got_y_ref, ahead_ref, *out_refs):
    refs = ((keep_x_ref, got_x_ref), (keep_y_ref, got_y_ref))
    for order, (keep_ref, got_ref), out_ref in zip(orders, refs, out_refs):
        red, green, blue, total = joined(keep_ref, got_ref, ahead_ref[order], 0)
        for c, value in enumerate((red, green, blue, 1.0 - jnp.exp2(-total))):
            for v in range(2):
                out_ref[v, c] = value[PIECE * v:PIECE * (v + 1)]


def images(x, y):
    shape = floats(2, 4, PIECE, x.keep.shape[-1])
    return pl.pallas_call(
        functools.partial(image_kernel, (x.order(), y.order())),
        out_shape=(shape, shape),
        in_specs=[VMEM] * 5,
        out_specs=(VMEM, VMEM),
        name="images",
        **options(0.3),
    )(x.keep, x.got, y.keep, y.got, x.ahead)


def stage_kernel(axis, mask, order, split, keep_ref, got_ref, ahead_ref, *out_refs):
    parts = [joined(keep_ref, got_ref, ahead_ref[order], p) for p in range(keep_ref.shape[0])]
    pick = lambda flag, a, b: [jnp.where(flag, one, two) for one, two in zip(a, b)]
    if split == "pair":
        high = is_set(axis, mask)
        pairs = list(zip(parts[::2], parts[1::2]))
        keep = [pick(high, b, a) for a, b in pairs]
        give = [pick(high, a, b) for a, b in pairs]
    elif split == "ring_first":
        upper = is_set(axis, 2 * mask)
        edge = is_set(axis, mask) == upper
        ends, middle = (parts[0], parts[3]), (parts[1], parts[2])
        small, large = [pick(edge, ends[k], middle[k]) for k in range(2)]
        keep = [pick(upper, large, small), pick(upper, small, large)]
        small, large = [pick(edge, middle[k], ends[k]) for k in range(2)]
        give = [pick(upper, large, small), pick(upper, small, large)]
    else:
        keep, give = parts[:1], parts[1:]
    for ref, pieces in zip(out_refs, (keep, give)):
        for p, piece in enumerate(pieces):
            for c in range(4):
                ref[p, c] = piece[c]


class Exchange:
    def __init__(self, axis, first, ahead):
        self.axis, self.first, self.ahead = axis, first, ahead
        self.stage = 0

    def send(self, keep, give, mask):
        self.keep, self.stage = keep, self.stage + 1
        self.got = lax.ppermute(give, self.axis, swapped(self.axis, mask))

    def order(self):
        return self.first + self.stage - 1

    def meet(self, split, mask=0):
        count, *rest = self.keep.shape
        return pl.pallas_call(
            functools.partial(stage_kernel, self.axis, mask, self.order(), split),
            out_shape=(floats(count // 2, *rest),) * 2,
            in_specs=[VMEM] * 3,
            out_specs=(VMEM, VMEM),
            **options(0.3),
        )(self.keep, self.got, self.ahead)


def local(density, transfer_table, shear_x, shear_y, direction):
    count_x = density.shape[0]
    step_len = 1.0 / (count_x * lax.axis_size("gx"))
    cells, outer, inner, hop, own, lut, *shifts, ahead = load(density, transfer_table, shear_x,
                                                              shear_y, direction)
    inner = lax.ppermute(inner, "gx", swapped("gx", 1))
    hopped = lax.ppermute(hop, "gy", hops("gy"))
    along = lax.ppermute(outer, "gx", ends("gx"))
    crossed = lax.ppermute(relay(own, hopped), "gy", swapped("gy", 1))
    outer = lax.ppermute(turn(outer, along), "gx", swapped("gx", 3))
    field = classify(cells, lut, step_len, 0)
    field = classify(cells, lut, step_len, 1, field)
    emitted = shade(cells, field)
    halo = (outer, inner, crossed)
    keep_x, give_x, emitted = x_march(cells, halo, field, shifts, emitted)

    x, y = Exchange("gx", 0, ahead), Exchange("gy", len(STAGES[0][1]), ahead)
    x.send(keep_x, give_x, 1)
    given = y_march(emitted, field, shifts, density.shape[:2], 0)
    kept = y_march(emitted, field, shifts, density.shape[:2], 1)
    x.send(*x.meet("pair", 2), 2)
    y.send(kept, given, 1)
    x.send(*x.meet("ring_first", 4), 4)
    x.send(*x.meet("ring_second"), 12)
    y.send(*y.meet("ring_first", 2), 2)
    y.send(*y.meet("ring_second"), 6)
    return images(x, y)


def solution(mesh):
    placed = (P("gx", "gy", None), P(), P(None, "gx"), P(None, "gy"), P())
    return jax.shard_map(
        local,
        mesh=mesh,
        in_specs=placed,
        out_specs=(P(None, None, ("gy", "gx"), None), P(None, None, ("gx", "gy"), None)),
        check_vma=False,
    )
```

```python
import functools

import jax
import jax.numpy as jnp
from jax import lax
from jax.experimental import pallas as pl
from jax.experimental.pallas import tpu as pltpu
from jax.sharding import PartitionSpec as P


ROWS = 8
PIECE = 4
LOG2E = 1.4426950408889634
PACK = 1024.0
ROUNDER = 12582912.0
GROUP_X, GROUP_Y = 4, 2
UNROLL_C, UNROLL_E, UNROLL_X, UNROLL_Y = 16, 32, 32, 64

VMEM = pl.BlockSpec(memory_space=pltpu.VMEM)
HBM = pl.BlockSpec(memory_space=pltpu.HBM)
STAGES = (("gx", (1, 2, 4, 8)), ("gy", (1, 2, 4)))


def is_set(axis, mask):
    return (lax.axis_index(axis) & mask) != 0


def slot_of(i, count):
    piece = i // PIECE
    return (piece % 2) * (count // 2) + (piece // 2) * PIECE + i % PIECE


def lane_take(values, index):
    numbers = lax.GatherDimensionNumbers(
        offset_dims=(), collapsed_slice_dims=(1,), start_index_map=(1,),
        operand_batching_dims=(0,), start_indices_batching_dims=(0,))
    return lax.gather(values, index[..., None], numbers, slice_sizes=(1, 1),
                      mode=lax.GatherScatterMode.PROMISE_IN_BOUNDS)


def load_kernel(stages, density_ref, table_ref, shear_x_ref, shear_y_ref, turn_ref, cells_ref,
                face_xa_ref, face_xb_ref, hop_ref, own_ref, lut_ref, index_ref, mask_ref, turned_ref,
                ahead_ref, levels_ref, shifts_x_ref, shifts_y_ref, turns_ref, sems):
    count_x, count_y, cells_z = density_ref.shape
    inner = cells_ref.at[pl.ds(1, count_x), pl.ds(ROWS, count_y), :]
    copies = [pltpu.make_async_copy(source, target, sems.at[k]) for k, (source, target) in
              enumerate(((density_ref, inner), (turn_ref, turns_ref), (shear_x_ref, shifts_x_ref),
                         (shear_y_ref, shifts_y_ref), (table_ref, levels_ref)))]
    for copy in copies:
        copy.start()

    lane = lax.broadcasted_iota(jnp.int32, (ROWS, cells_z), 1)
    row = lax.broadcasted_iota(jnp.int32, (ROWS, cells_z), 0)
    copies[1].wait()
    stage = 0
    for family, (axis, masks) in enumerate(stages):
        turned = jnp.where(row < PIECE, turns_ref[family, 0], turns_ref[family, 1])
        for mask in masks:
            ahead_ref[stage] = jnp.where(turned == jnp.where(is_set(axis, mask), 1, 0), 1.0, 0.0)
            stage += 1

    for family, shifts_ref in enumerate((shifts_x_ref, shifts_y_ref)):
        copies[2 + family].wait()
        count = shifts_ref.shape[1]
        for v in range(2):
            turned = turns_ref[family, v]
            turned_ref[2 * family + v] = jnp.full((ROWS, cells_z), turned, jnp.int32)
            sign = jnp.full((ROWS, cells_z), jnp.where(turned != 0, 1.0, -1.0), jnp.float32)
            first = 2 * family * count_x + v * count

            def shifted(i, carry):
                source = lane - shifts_ref[v, i]
                inside = source & (cells_z - 1)
                index_ref[first + i] = inside
                mask_ref[first + i] = jnp.where(inside == source, sign, 0.0)
                return carry

            lax.fori_loop(0, count, shifted, 0, unroll=8)

    copies[4].wait()
    levels = levels_ref[...].astype(jnp.float32)
    for c in range(4):
        level = jnp.broadcast_to(levels[c:c + 1], (ROWS, cells_z))
        rise = jnp.where(lane == cells_z - 1, 0.0, pltpu.roll(level, cells_z - 1, 1) - level)
        lut_ref[c] = level + rise * (1.0 / PACK)
    copies[0].wait()

    odd_x, odd_y = is_set("gx", 1), is_set("gy", 1)
    first, last = cells_ref[1, pl.ds(ROWS, count_y), :], cells_ref[count_x, pl.ds(ROWS, count_y), :]
    face_xa_ref[...] = jnp.where(odd_x, last, first)
    face_xb_ref[...] = jnp.where(odd_x, first, last)
    first, last = (cells_ref[pl.ds(1, count_x), ROWS, :],
                   cells_ref[pl.ds(1, count_x), ROWS + count_y - 1, :])
    hop_ref[...] = jnp.where(odd_y, last, first)
    own_ref[...] = jnp.where(odd_y, first, last)


def relay_kernel(own_ref, hopped_ref, out_ref):
    rows = own_ref.shape[0]
    out_ref[pl.ds(0, rows), :] = own_ref[...]
    out_ref[pl.ds(rows, rows), :] = hopped_ref[...]


def classify_kernel(step_len, parity, cells_ref, lut_ref, *refs):
    field_ref = refs[-1]
    count_x, cells_z = cells_ref.shape[0] - 2, cells_ref.shape[2]
    count_y = cells_ref.shape[1] - 2 * ROWS
    pitch = field_ref.shape[1] // count_x

    def body(t, carry):
        i = (t // PIECE * 2 + parity) * PIECE + t % PIECE
        slot = (t + parity * (count_x // 2)) * pitch
        for base in range(0, count_y, ROWS):
            scaled = cells_ref[i + 1, pl.ds(ROWS + base, ROWS), :] * (cells_z - 1.0)
            knot = scaled.astype(jnp.int32)
            part = (scaled - knot.astype(jnp.float32)) * PACK - 1.0
            classed = []
            for c in range(4):
                packed = lane_take(lut_ref[c], knot)
                level = (packed + ROUNDER) - ROUNDER
                classed.append(packed + (packed - level) * part)
            optical = classed[3] * (2.0 * step_len * LOG2E / 255.0)
            opacity = (1.0 - jnp.exp2(-optical)) * (1.0 / 255.0)
            values = [classed[c] * opacity for c in range(3)] + [optical]
            for c in range(4):
                field_ref[c, pl.ds(slot + base, ROWS), :] = values[c]
        return carry

    lax.fori_loop(0, count_x // 2, body, 0, unroll=UNROLL_C)


def march(fields, place, turned, index_ref, mask_ref, states):
    index, mask = index_ref[place], mask_ref[place]
    out = []
    for (red, green, blue, optical), state in zip(fields, states):
        depth = lane_take(optical, index) * mask
        after = state[0] + depth
        seen = jnp.exp2(jnp.where(turned, after, state[0])) * mask
        out.append((after, state[1] + seen * lane_take(red, index),
                    state[2] + seen * lane_take(green, index),
                    state[3] + seen * lane_take(blue, index)))
    return tuple(out)


def settle(turned, state):
    sign = jnp.where(turned, 1.0, -1.0)
    total = state[0] * sign
    fade = jnp.exp2(jnp.where(turned, -total, 0.0)) * sign
    return [state[1] * fade, state[2] * fade, state[3] * fade, total]


def emission(cells_ref, field_ref, emit_ref, i, base):
    count_x, cells_z = cells_ref.shape[0] - 2, cells_ref.shape[2]
    pitch, pad = field_ref.shape[1] // count_x, ROWS
    lane = lax.broadcasted_iota(jnp.int32, (ROWS, cells_z), 1)
    here = cells_ref[i + 1, pl.ds(base + pad, ROWS), :]
    diff_x = (cells_ref[i + 2, pl.ds(base + pad, ROWS), :]
              - cells_ref[i, pl.ds(base + pad, ROWS), :])
    diff_y = (cells_ref[i + 1, pl.ds(base + pad + 1, ROWS), :]
              - cells_ref[i + 1, pl.ds(base + pad - 1, ROWS), :])
    above = lane_take(here, (lane + 1) & (cells_z - 1))
    below = lane_take(here, (lane - 1) & (cells_z - 1))
    diff_z = jnp.where(lane == cells_z - 1, 0.0, above) - jnp.where(lane == 0, 0.0, below)
    side = diff_y + diff_z
    facing = jnp.abs(diff_x + (side + side))
    norm = diff_x * diff_x + diff_y * diff_y + diff_z * diff_z + 0.04
    shaded = 0.3 + (0.7 / 3.0) * facing * lax.rsqrt(norm)
    rows = pl.ds(slot_of(i, count_x) * pitch + base, ROWS)
    for c in range(3):
        emit_ref[c, rows, :] = field_ref[c, rows, :] * shaded


def x_kernel(group, face_xa_ref, face_xb_ref, crossed_ref, field_ref, index_ref,
             mask_ref, turned_ref, _cells, keep_ref, give_ref, emit_ref, cells_ref):
    count_x, cells_z = cells_ref.shape[0] - 2, cells_ref.shape[2]
    count_y = cells_ref.shape[1] - 2 * ROWS
    pitch = field_ref.shape[1] // count_x
    pad = ROWS
    lane = lax.broadcasted_iota(jnp.int32, (ROWS, cells_z), 1)

    odd_x, odd_y = is_set("gx", 1), is_set("gy", 1)
    near, far = face_xa_ref[...], face_xb_ref[...]
    cells_ref[0, pl.ds(pad, count_y), :] = jnp.where(odd_x, far, near)
    cells_ref[count_x + 1, pl.ds(pad, count_y), :] = jnp.where(odd_x, near, far)
    near, far = crossed_ref[pl.ds(0, count_x), :], crossed_ref[pl.ds(count_x, count_x), :]
    low_y, high_y = jnp.where(odd_y, near, far), jnp.where(odd_y, far, near)
    for i in range(count_x):
        cells_ref[i + 1, pl.ds(pad - 1, 1), :] = low_y[i:i + 1]
        cells_ref[i + 1, pl.ds(pad + count_y, 1), :] = high_y[i:i + 1]

    turned = [turned_ref[v] != 0 for v in range(2)]
    zeros = jnp.zeros((ROWS, cells_z), jnp.float32)

    def shade(i, carry):
        for base in range(0, count_y, ROWS):
            emission(cells_ref, field_ref, emit_ref, i, base)
        return carry

    lax.fori_loop(0, count_x, shade, 0, unroll=UNROLL_E)

    def block_of(block, carry):
        base = pl.multiple_of(block * (ROWS * group), ROWS)

        def body(i, states):
            fields = []
            slot = slot_of(i, count_x) * pitch
            for g in range(group):
                rows = pl.ds(slot + base + g * ROWS, ROWS)
                fields.append((emit_ref[0, rows, :], emit_ref[1, rows, :], emit_ref[2, rows, :],
                               field_ref[3, rows, :]))
            return tuple(march(fields, v * count_x + i, turned[v], index_ref, mask_ref,
                               states[v]) for v in range(2))

        states = lax.fori_loop(0, count_x, body, (((zeros,) * 4,) * group,) * 2, unroll=UNROLL_X)
        for v in range(2):
            for g in range(group):
                for c, value in enumerate(settle(turned[v], states[v][g])):
                    even, odd = value[:PIECE], value[PIECE:]
                    spot, rows = block * group + g, pl.ds(PIECE * v, PIECE)
                    keep_ref[spot, c, rows, :] = jnp.where(odd_x, odd, even)
                    give_ref[spot, c, rows, :] = jnp.where(odd_x, even, odd)
        return carry

    lax.fori_loop(0, count_y // (ROWS * group), block_of, 0)


def y_kernel(group, kept, count_x, count_y, emit_ref, field_ref, index_ref, mask_ref, turned_ref,
             out_ref):
    cells_z = emit_ref.shape[-1]
    pitch = emit_ref.shape[1] // count_x
    size = out_ref.shape[0] * PIECE
    first = jnp.where(is_set("gy", 1) == bool(kept), size, 0)
    turned = [turned_ref[2 + v] != 0 for v in range(2)]
    zeros = jnp.zeros((ROWS, cells_z), jnp.float32)

    def block_of(block, carry):
        def body(j, states):
            fields = []
            for g in range(group):
                start = (first + (block * group + g) * ROWS) * pitch
                rows = pl.ds(start + j, ROWS, stride=pitch)
                fields.append((emit_ref[0, rows, :], emit_ref[1, rows, :], emit_ref[2, rows, :],
                               field_ref[3, rows, :]))
            return tuple(march(fields, 2 * count_x + v * count_y + j, turned[v], index_ref, mask_ref,
                               states[v]) for v in range(2))

        states = lax.fori_loop(0, count_y, body, (((zeros,) * 4,) * group,) * 2, unroll=UNROLL_Y)
        for v in range(2):
            for g in range(group):
                for c, value in enumerate(settle(turned[v], states[v][g])):
                    for half in range(2):
                        out_ref[2 * (block * group + g) + half, c, pl.ds(PIECE * v, PIECE), :] = (
                            value[PIECE * half:PIECE * (half + 1)])
        return carry

    lax.fori_loop(0, size // (ROWS * group), block_of, 0)


def options(micros, limit=16 << 20):
    return dict(
        compiler_params=pltpu.CompilerParams(vmem_limit_bytes=limit),
        cost_estimate=pl.CostEstimate(flops=0, transcendentals=0,
                                      bytes_accessed=int(micros * 3.5e6)))


def floats(*shape):
    return jax.ShapeDtypeStruct(shape, jnp.float32)


def load(density, transfer_table, shear_x, shear_y, direction):
    count_x, count_y, cells_z = density.shape
    places = 2 * (count_x + count_y)
    sources = [pltpu.with_memory_space_constraint(a, pltpu.HBM)
               for a in (density, transfer_table, shear_x, shear_y, direction)]
    return pl.pallas_call(
        functools.partial(load_kernel, STAGES),
        out_shape=(floats(count_x + 2, count_y + 2 * ROWS, cells_z),
                   floats(count_y, cells_z), floats(count_y, cells_z),
                   floats(count_x, cells_z), floats(count_x, cells_z),
                   floats(4, ROWS, cells_z),
                   jax.ShapeDtypeStruct((places, ROWS, cells_z), jnp.int32),
                   floats(places, ROWS, cells_z),
                   jax.ShapeDtypeStruct((4, ROWS, cells_z), jnp.int32),
                   floats(sum(len(masks) for _, masks in STAGES), ROWS, cells_z)),
        in_specs=[HBM] * 5,
        out_specs=(VMEM,) * 10,
        scratch_shapes=[pltpu.VMEM(transfer_table.shape, jnp.int32),
                        pltpu.SMEM(shear_x.shape, jnp.int32), pltpu.SMEM(shear_y.shape, jnp.int32),
                        pltpu.SMEM(direction.shape, jnp.int32), pltpu.SemaphoreType.DMA((5,))],
        name="load",
        **options(2),
    )(*sources)


def relay(own, hopped):
    return pl.pallas_call(
        relay_kernel,
        out_shape=floats(2 * own.shape[0], own.shape[1]),
        in_specs=[VMEM, VMEM],
        out_specs=VMEM,
        name="relay",
        **options(0.3),
    )(own, hopped)


def classify(cells, lut, step_len, part, *before):
    count_x, count_y, cells_z = cells.shape[0] - 2, cells.shape[1] - 2 * ROWS, cells.shape[2]
    return pl.pallas_call(
        functools.partial(classify_kernel, step_len, part),
        out_shape=floats(4, count_x * (count_y + 1), cells_z),
        in_specs=[VMEM] * (2 + len(before)),
        out_specs=VMEM,
        input_output_aliases={2: 0} if before else {},
        **options(1.5),
    )(cells, lut, *before)


def x_march(cells, halo, field, shifts):
    count_y, cells_z = cells.shape[1] - 2 * ROWS, cells.shape[2]
    part = floats(count_y // (2 * PIECE), 4, 2 * PIECE, cells_z)
    return pl.pallas_call(
        functools.partial(x_kernel, GROUP_X),
        out_shape=(part, part, floats(3, *field.shape[1:]), floats(*cells.shape)),
        in_specs=[VMEM] * 8,
        out_specs=(VMEM,) * 4,
        input_output_aliases={7: 3},
        name="x_march",
        **options(4),
    )(*halo, field, *shifts, cells)[:3]


def y_march(emitted, field, shifts, sizes, kept):
    cells_z = field.shape[-1]
    return pl.pallas_call(
        functools.partial(y_kernel, GROUP_Y, kept, *sizes),
        out_shape=floats(sizes[0] // (2 * PIECE), 4, 2 * PIECE, cells_z),
        in_specs=[VMEM] * 5,
        out_specs=VMEM,
        **options(2.5),
    )(emitted, field, *shifts)


def neighbours(axis, offset):
    count = lax.axis_size(axis)
    pairs = [(i, i + 1) for i in range(offset, count - 1, 2)]
    return pairs + [(target, source) for source, target in pairs]


def hops(axis):
    count = lax.axis_size(axis)
    moves = [(i, i + 4 * (i % 2) - 2) for i in range(count)]
    return [(source, target) for source, target in moves if 0 <= target < count]


def swapped(axis, mask):
    return [(i, i ^ mask) for i in range(lax.axis_size(axis))]


def joined(keep_ref, got_ref, ahead, p):
    mine_ahead = ahead > 0.5
    mine, theirs = [[ref[p, c] for c in range(4)] for ref in (keep_ref, got_ref)]
    seen = jnp.exp2(-jnp.where(mine_ahead, mine[3], theirs[3]))
    near, far = jnp.where(mine_ahead, 1.0, seen), jnp.where(mine_ahead, seen, 1.0)
    return [mine[c] * near + theirs[c] * far for c in range(3)] + [mine[3] + theirs[3]]


def image_kernel(orders, keep_x_ref, got_x_ref, keep_y_ref, got_y_ref, ahead_ref, *out_refs):
    refs = ((keep_x_ref, got_x_ref), (keep_y_ref, got_y_ref))
    for order, (keep_ref, got_ref), out_ref in zip(orders, refs, out_refs):
        red, green, blue, total = joined(keep_ref, got_ref, ahead_ref[order], 0)
        for c, value in enumerate((red, green, blue, 1.0 - jnp.exp2(-total))):
            for v in range(2):
                out_ref[v, c] = value[PIECE * v:PIECE * (v + 1)]


def images(x, y):
    shape = floats(2, 4, PIECE, x.keep.shape[-1])
    return pl.pallas_call(
        functools.partial(image_kernel, (x.order(), y.order())),
        out_shape=(shape, shape),
        in_specs=[VMEM] * 5,
        out_specs=(VMEM, VMEM),
        name="images",
        **options(0.3),
    )(x.keep, x.got, y.keep, y.got, x.ahead)


def stage_kernel(axis, mask, order, split, keep_ref, got_ref, ahead_ref, *out_refs):
    parts = [joined(keep_ref, got_ref, ahead_ref[order], p) for p in range(keep_ref.shape[0])]
    pick = lambda flag, a, b: [jnp.where(flag, one, two) for one, two in zip(a, b)]
    if split == "pair":
        high = is_set(axis, mask)
        pairs = list(zip(parts[::2], parts[1::2]))
        keep = [pick(high, b, a) for a, b in pairs]
        give = [pick(high, a, b) for a, b in pairs]
    elif split == "ring_first":
        upper = is_set(axis, 2 * mask)
        edge = is_set(axis, mask) == upper
        ends, middle = (parts[0], parts[3]), (parts[1], parts[2])
        small, large = [pick(edge, ends[k], middle[k]) for k in range(2)]
        keep = [pick(upper, large, small), pick(upper, small, large)]
        small, large = [pick(edge, middle[k], ends[k]) for k in range(2)]
        give = [pick(upper, large, small), pick(upper, small, large)]
    else:
        keep, give = parts[:1], parts[1:]
    for ref, pieces in zip(out_refs, (keep, give)):
        for p, piece in enumerate(pieces):
            for c in range(4):
                ref[p, c] = piece[c]


class Exchange:
    def __init__(self, axis, first, ahead):
        self.axis, self.first, self.ahead = axis, first, ahead
        self.stage = 0

    def send(self, keep, give, mask):
        self.keep, self.stage = keep, self.stage + 1
        self.got = lax.ppermute(give, self.axis, swapped(self.axis, mask))

    def order(self):
        return self.first + self.stage - 1

    def meet(self, split, mask=0):
        count, *rest = self.keep.shape
        return pl.pallas_call(
            functools.partial(stage_kernel, self.axis, mask, self.order(), split),
            out_shape=(floats(count // 2, *rest),) * 2,
            in_specs=[VMEM] * 3,
            out_specs=(VMEM, VMEM),
            **options(0.3),
        )(self.keep, self.got, self.ahead)


def local(density, transfer_table, shear_x, shear_y, direction):
    count_x = density.shape[0]
    step_len = 1.0 / (count_x * lax.axis_size("gx"))
    cells, outer, inner, hop, own, lut, *shifts, ahead = load(density, transfer_table, shear_x,
                                                              shear_y, direction)
    inner = lax.ppermute(inner, "gx", swapped("gx", 1))
    hopped = lax.ppermute(hop, "gy", hops("gy"))
    outer = lax.ppermute(outer, "gx", neighbours("gx", 1))
    crossed = lax.ppermute(relay(own, hopped), "gy", swapped("gy", 1))
    field = classify(cells, lut, step_len, 0)
    field = classify(cells, lut, step_len, 1, field)
    halo = (outer, inner, crossed)
    keep_x, give_x, emitted = x_march(cells, halo, field, shifts)

    x, y = Exchange("gx", 0, ahead), Exchange("gy", len(STAGES[0][1]), ahead)
    x.send(keep_x, give_x, 1)
    given = y_march(emitted, field, shifts, density.shape[:2], 0)
    kept = y_march(emitted, field, shifts, density.shape[:2], 1)
    x.send(*x.meet("pair", 2), 2)
    y.send(kept, given, 1)
    x.send(*x.meet("ring_first", 4), 4)
    x.send(*x.meet("ring_second"), 12)
    y.send(*y.meet("ring_first", 2), 2)
    y.send(*y.meet("ring_second"), 6)
    return images(x, y)


def solution(mesh):
    placed = (P("gx", "gy", None), P(), P(None, "gx"), P(None, "gy"), P())
    return jax.shard_map(
        local,
        mesh=mesh,
        in_specs=placed,
        out_specs=(P(None, None, ("gy", "gx"), None), P(None, None, ("gx", "gy"), None)),
        check_vma=False,
    )
```
